256 devices in a mesh: gx: 16 (over y, x), gy: 4 (over z_lo, core), gz: 4 (over z_hi).
Axes of the slice: x: 4, y: 4, z: 8 (z_hi: 4, z_lo: 2; z = z_hi * 2 + z_lo), core: 2. Of those that a mesh axis runs over, the one named last changes fastest.
Arguments:
- positions: float32 [3, 131072], P(None, ('gx', 'gy', 'gz')), may hold values from 0 to 1
- features: bfloat16 [64, 131072], P(None, ('gx', 'gy', 'gz')), may hold values from -6 to 6
- species: int32 [131072], P(('gx', 'gy', 'gz')), may hold values from 0 to 3
- species_scale: bfloat16 [4], replicated, may hold values from 0.5 to 2
- w_first: bfloat16 [64, 64], replicated, may hold values from -0.75 to 0.75
- w_second: bfloat16 [64, 64], replicated, may hold values from -0.75 to 0.75
- w_radial: float32 [64, 8], replicated, may hold values from -4 to 4
- w_mid: bfloat16 [64, 64], replicated, may hold values from -0.75 to 0.75
- w_last: bfloat16 [64, 64], replicated, may hold values from -0.75 to 0.75
- w_out: float32 [64], replicated, may hold values from -0.75 to 0.75
- ghost_send: int32 [65536], P(('gx', 'gy', 'gz')), may hold values from 0 to 511
- local_first: int32 [5242880], P(('gx', 'gy', 'gz')), may hold values from 0 to 511
- local_second: int32 [5242880], P(('gx', 'gy', 'gz')), may hold values from 0 to 511
- local_mask: int32 [5242880], P(('gx', 'gy', 'gz')), may hold values 0 or 1
- ghost_owner: int32 [3145728], P(('gx', 'gy', 'gz')), may hold values from 0 to 511
- ghost_index: int32 [3145728], P(('gx', 'gy', 'gz')), may hold values from 0 to 1791
- ghost_mask: int32 [3145728], P(('gx', 'gy', 'gz')), may hold values 0 or 1
Outputs:
- forces: float32 [3, 131072], P(None, ('gx', 'gy', 'gz'))
- atom_energy: float32 [131072], P(('gx', 'gy', 'gz'))
The draws below stay inside these ranges and needn't reach their ends.
Inputs may be any that keep to these rules, and one draw needn't show every extreme that they name: `ghost_send`: rows of the domain's own atoms. `local_first`: owned atoms of the domain. `local_second`: owned atoms of the domain. `ghost_owner`: owned atoms of the domain. `ghost_index`: ghost rows of the domain.
All inputs are finite; a program needn't handle non-finite values. No bound on the sum of `local_mask` or of `ghost_mask` on one device may be relied on, other than what follows from the above.
Results may differ from the reference program's by a relative error of at most 0.0085.
Values may be sent and summed in bfloat16 or wider, within the bound.
A program may use at most 64 MiB of HBM per device.

```python
import math
import jax
import jax.numpy as jnp
from jax import lax

C = 64
NB = 8
K = 4
A_DEV = 512
G = 256
PL = 20480
PG = 12288
ATOMS = 131072
SENDS = 65536
LOCAL_SLOTS = 5242880
GHOST_SLOTS = 3145728
N_GX = 16
N_GY = 4
N_GZ = 4


def place_ends(values, stream_key, low, largest):
    longest = values.shape.index(max(values.shape))
    spots = []
    for shift in (0, 1):
        where = [jax.random.randint(jax.random.fold_in(stream_key, axis), (), 0, length) for axis, length in enumerate(values.shape)]
        where[longest] = (where[longest] + shift) % values.shape[longest]
        spots.append(tuple(where))
    return values.at[spots[0]].set(low).at[spots[1]].set(largest)


def shard_levels(key, dims, cuts, low, high):
    gain, own = 1.0, jax.random.fold_in(key, 6)
    for position, blocks in cuts:
        heights = jnp.exp(jax.random.uniform(jax.random.fold_in(own, position), (blocks,), jnp.float32, low / len(cuts), high / len(cuts)))
        gain = gain * jnp.repeat(heights, dims[position] // blocks).reshape([-1 if axis == position else 1 for axis in range(len(dims))])
    return gain


def scatter_about(rng, extent, scale, reach, shards=(), kind=jnp.bfloat16):
    gain = shard_levels(rng, extent, shards, -0.22, 0.18) if shards else 1.0
    values = jax.random.normal(rng, extent, jnp.float32) * scale * gain
    return jnp.minimum(jnp.maximum(values, -reach), reach).astype(kind)


def setup_inputs(seed: int = 0) -> dict:
    key_of = jax.random.split(jax.random.key(seed), 18)
    positions = jnp.clip(1.0 * jax.random.uniform(key_of[0], (3, ATOMS), jnp.float32) ** shard_levels(key_of[0], (3, ATOMS), ((1, 256),), -0.2, 0.2), 0.0, 1.0)
    features = scatter_about(key_of[1], (C, ATOMS), 1.0, 6.0, ((1, 256),))
    species = place_ends(jax.random.randint(key_of[2], (ATOMS,), 0, K), jax.random.fold_in(key_of[2], 1), 0, K - 1).astype(jnp.int32)
    species_scale = jnp.clip(jnp.exp(jax.random.uniform(key_of[3], (K,), jnp.float32, math.log(0.5), math.log(2.0))), 0.5, 2.0).astype(jnp.bfloat16)
    w_first = scatter_about(key_of[4], (C, C), C ** -0.5, 0.75)
    w_second = scatter_about(key_of[5], (C, C), C ** -0.5, 0.75)
    w_radial = scatter_about(key_of[6], (C, NB), 2 ** -0.5, 4.0, (), jnp.float32)
    w_mid = scatter_about(key_of[7], (C, C), C ** -0.5, 0.75)
    w_last = scatter_about(key_of[8], (C, C), C ** -0.5, 0.75)
    w_out = scatter_about(key_of[9], (C,), C ** -0.5, 0.75, (), jnp.float32)
    ghost_send = place_ends(jax.random.randint(key_of[10], (SENDS,), 0, A_DEV), jax.random.fold_in(key_of[10], 1), 0, A_DEV - 1).astype(jnp.int32)
    local_first = place_ends(jax.random.randint(key_of[11], (LOCAL_SLOTS,), 0, A_DEV), jax.random.fold_in(key_of[11], 1), 0, A_DEV - 1).astype(jnp.int32)
    local_second = place_ends(jax.random.randint(key_of[12], (LOCAL_SLOTS,), 0, A_DEV), jax.random.fold_in(key_of[12], 1), 0, A_DEV - 1).astype(jnp.int32)
    local_mask = place_ends((jax.random.randint(key_of[13], (LOCAL_SLOTS,), 0, 4) < 3).astype(jnp.int32), jax.random.fold_in(key_of[13], 1), 0, 1)
    ghost_owner = place_ends(jax.random.randint(key_of[14], (GHOST_SLOTS,), 0, A_DEV), jax.random.fold_in(key_of[14], 1), 0, A_DEV - 1).astype(jnp.int32)
    ghost_index = place_ends(jax.random.randint(key_of[15], (GHOST_SLOTS,), 0, 7 * G), jax.random.fold_in(key_of[15], 1), 0, (7 * G) - 1).astype(jnp.int32)
    ghost_mask = place_ends((jax.random.randint(key_of[16], (GHOST_SLOTS,), 0, 4) < 3).astype(jnp.int32), jax.random.fold_in(key_of[16], 1), 0, 1)
    return dict(positions=positions, features=features, species=species, species_scale=species_scale, w_first=w_first, w_second=w_second, w_radial=w_radial, w_mid=w_mid, w_last=w_last, w_out=w_out, ghost_send=ghost_send, local_first=local_first, local_second=local_second, local_mask=local_mask, ghost_owner=ghost_owner, ghost_index=ghost_index, ghost_mask=ghost_mask)


basis_width = 24.0
domain_edge = 1.0
ghost_offsets = ((1, 0, 0), (0, 1, 0), (0, 0, 1), (1, 1, 0), (1, 0, 1), (0, 1, 1), (1, 1, 1))

def pair_energy(squared, left_proj, right_proj, weights, w_radial, w_mid, w_last, w_out):
    basis_count = w_radial.shape[1]
    centers = jnp.arange(basis_count, dtype=jnp.float32) / (basis_count - 1)
    radial_basis = jnp.exp(-basis_width * (squared[None, :] - centers[:, None]) ** 2)
    radial = jnp.dot(w_radial, radial_basis, precision=lax.Precision.HIGHEST, preferred_element_type=jnp.float32)
    hidden_one = jax.nn.silu(left_proj.astype(jnp.float32) + right_proj.astype(jnp.float32) + radial).astype(jnp.bfloat16)
    hidden_two = jax.nn.silu(jnp.dot(w_mid, hidden_one, preferred_element_type=jnp.float32)).astype(jnp.bfloat16)
    hidden_three = jax.nn.silu(jnp.dot(w_last, hidden_two, preferred_element_type=jnp.float32))
    readout = jnp.dot(w_out, hidden_three, precision=lax.Precision.HIGHEST, preferred_element_type=jnp.float32)
    envelope = jnp.maximum(1.0 - squared, 0.0) ** 2
    return weights * envelope * readout

def pair_terms(owners, partners, slot_mask, own_coords, own_gain, left_all, right_table, right_coords, right_gain, w_radial, w_mid, w_last, w_out):
    total = owners.shape[0]
    block_size = math.gcd(total, 8192)
    step_count = total // block_size

    def one_block(pieces):
        owner_rows, partner_rows, live = pieces
        displace = jnp.take(right_coords, partner_rows, axis=1) - jnp.take(own_coords, owner_rows, axis=1)
        squared = lax.optimization_barrier(jnp.sum(displace * displace, axis=0))
        weights = live.astype(jnp.float32) * jnp.take(own_gain, owner_rows) * jnp.take(right_gain, partner_rows)
        left_proj = jnp.take(left_all, owner_rows, axis=1)
        right_proj = jnp.take(right_table, partner_rows, axis=1)

        def energy_of(squared_in):
            return pair_energy(squared_in, left_proj, right_proj, weights, w_radial, w_mid, w_last, w_out)
        energy, pullback = jax.vjp(energy_of, squared)
        slope = pullback(jnp.ones_like(energy))[0]
        return (energy, 2.0 * displace * slope[None, :])
    energies, pushes = lax.map(one_block, (owners.reshape(step_count, block_size), partners.reshape(step_count, block_size), slot_mask.reshape(step_count, block_size)))
    return (energies.reshape(total), jnp.moveaxis(pushes, 1, 0).reshape(3, total))

def reference(positions, features, species, species_scale, w_first, w_second, w_radial, w_mid, w_last, w_out, ghost_send, local_first, local_second, local_mask, ghost_owner, ghost_index, ghost_mask):
    device_count = N_GX * N_GY * N_GZ
    channels = features.shape[0]
    atom_gain = species_scale.astype(jnp.float32)[species]
    coord_high = positions.astype(jnp.bfloat16)
    coord_low = (positions - coord_high.astype(jnp.float32)).astype(jnp.bfloat16)
    payload = jnp.concatenate([features, coord_high, coord_low, atom_gain.astype(jnp.bfloat16)[None, :]], 0)
    payload_dev = payload.reshape(channels + 7, device_count, A_DEV)
    send_dev = ghost_send.reshape(device_count, G)
    picked = jax.vmap(lambda table, rows_in: jnp.take(table, rows_in, axis=1), in_axes=(1, 0), out_axes=1)(payload_dev, send_dev)
    picked_grid = picked.reshape(channels + 7, N_GX, N_GY, N_GZ, G)
    blocks = [jnp.roll(picked_grid, (-offset[0], -offset[1], -offset[2]), axis=(1, 2, 3)) for offset in ghost_offsets]
    ghosts = jnp.stack(blocks, 4).reshape(channels + 7, device_count, 7 * G)
    shifts = domain_edge * jnp.array(ghost_offsets, dtype=jnp.float32).T

    def device_terms(pieces):
        own_pos, own_feat, own_gain, ghost_rows, first_l, second_l, mask_l, owner_g, index_g, mask_g = pieces
        ghost_feat = ghost_rows[:channels]
        ghost_high = ghost_rows[channels:channels + 3].astype(jnp.float32)
        ghost_low = ghost_rows[channels + 3:channels + 6].astype(jnp.float32)
        ghost_coords = ((ghost_high + ghost_low).reshape(3, 7, G) + shifts[:, :, None]).reshape(3, 7 * G)
        ghost_gain = ghost_rows[channels + 6].astype(jnp.float32)
        left_all = jnp.dot(w_first, own_feat, preferred_element_type=jnp.float32).astype(jnp.bfloat16)
        right_own = jnp.dot(w_second, own_feat, preferred_element_type=jnp.float32).astype(jnp.bfloat16)
        right_ghost = jnp.dot(w_second, ghost_feat, preferred_element_type=jnp.float32).astype(jnp.bfloat16)
        local_energy, local_push = pair_terms(first_l, second_l, mask_l, own_pos, own_gain, left_all, right_own, own_pos, own_gain, w_radial, w_mid, w_last, w_out)
        ghost_energy, ghost_push = pair_terms(owner_g, index_g, mask_g, own_pos, own_gain, left_all, right_ghost, ghost_coords, ghost_gain, w_radial, w_mid, w_last, w_out)
        energy_out = jnp.zeros((A_DEV,), jnp.float32).at[first_l].add(local_energy).at[owner_g].add(ghost_energy)
        force_out = jnp.zeros((3, A_DEV), jnp.float32).at[:, first_l].add(local_push).at[:, second_l].add(-local_push).at[:, owner_g].add(ghost_push)
        ghost_force = jnp.zeros((3, 7 * G), jnp.float32).at[:, index_g].add(-ghost_push)
        return (force_out, energy_out, ghost_force)
    pieces = (jnp.moveaxis(positions.reshape(3, device_count, A_DEV), 1, 0), jnp.moveaxis(features.reshape(channels, device_count, A_DEV), 1, 0), atom_gain.reshape(device_count, A_DEV), jnp.moveaxis(ghosts, 1, 0), local_first.reshape(device_count, PL), local_second.reshape(device_count, PL), local_mask.reshape(device_count, PL), ghost_owner.reshape(device_count, PG), ghost_index.reshape(device_count, PG), ghost_mask.reshape(device_count, PG))
    force_dev, energy_dev, ghost_dev = lax.map(device_terms, pieces)
    ghost_grid = ghost_dev.reshape(N_GX, N_GY, N_GZ, 3, 7, G)
    incoming = jnp.zeros((N_GX, N_GY, N_GZ, 3, G), jnp.float32)
    for slot in range(7):
        offset = ghost_offsets[slot]
        incoming = incoming + jnp.roll(ghost_grid[:, :, :, :, slot, :], (offset[0], offset[1], offset[2]), axis=(0, 1, 2))
    incoming = incoming.reshape(device_count, 3, G)
    force_dev = jax.vmap(lambda table, rows_in, values: table.at[:, rows_in].add(values))(force_dev, send_dev, incoming)
    forces = jnp.moveaxis(force_dev, 0, 1).reshape(3, device_count * A_DEV)
    atom_energy = energy_dev.reshape(device_count * A_DEV)
    return (forces, atom_energy)
```

```python
import jax
import jax.numpy as jnp
from jax import lax
from jax.experimental import pallas as pl
from jax.experimental.pallas import tpu as pltpu
from jax.sharding import PartitionSpec as P

OFFSETS = ((1, 0, 0), (0, 1, 0), (0, 0, 1), (1, 1, 0), (1, 0, 1), (0, 1, 1), (1, 1, 1))
MESH_IDS = pl.DeviceIdType.MESH
VMEM = pl.BlockSpec(memory_space=pltpu.VMEM)
NT = (((1,), (1,)), ((), ()))
WIDTH = 24.0
F32, BF16, I32 = jnp.float32, jnp.bfloat16, jnp.int32
LIVE = 128
ROWS = 80


def neighbour(offset, sign):
    where = []
    for axis, step in zip(("gx", "gy", "gz"), offset):
        count = lax.axis_size(axis)
        where.append(lax.rem(lax.axis_index(axis) + sign * step + count, count))
    return tuple(where)


def meet(sign):
    barrier = pltpu.get_barrier_semaphore()
    for offset in OFFSETS:
        pl.semaphore_signal(barrier, inc=1, device_id=neighbour(offset, sign), device_id_type=MESH_IDS)
    return barrier


def one_hot(row, count):
    levels = lax.broadcasted_iota(jnp.int16, (count, row.shape[1]), 0)
    return jnp.where(levels == row.astype(jnp.int16), jnp.ones((), BF16), jnp.zeros((), BF16))


def split_two(value):
    high = value.astype(BF16).astype(F32)
    return high, value - high


def offer_kernel(pos_ref, feat_ref, species_ref, scale_ref, first_ref, second_ref, send_ref,
                 own_ref, tables_ref, ghost_ref, offered, send_sem, recv_sem):
    barrier = meet(1)
    pos = pos_ref[...]
    species = species_ref[...]
    scale = scale_ref[...].astype(F32)
    gain = jnp.zeros(species.shape, F32)
    for kind in range(scale.shape[1]):
        gain = jnp.where(species == kind, scale[:, kind:kind + 1], gain)
    count = pos.shape[1]
    own_ref[0:3, :] = pos
    own_ref[3:4, :] = gain
    own_ref[4:8, :] = jnp.zeros((4, count), F32)
    feat = feat_ref[...]
    right = (jnp.dot(second_ref[...], feat, preferred_element_type=F32).astype(BF16).astype(F32) * 0.5).astype(BF16)
    high = pos.astype(BF16).astype(F32)
    tail = jnp.concatenate([high, pos - high, gain, jnp.zeros((9, count), F32)], 0).astype(BF16)
    payload = jnp.concatenate([right, tail], 0)
    hot = one_hot(send_ref[...], count)
    offered[...] = jnp.dot(payload, hot, preferred_element_type=F32).astype(BF16)
    pl.semaphore_wait(barrier, len(OFFSETS))
    copies = []
    for k, offset in enumerate(OFFSETS):
        copy = pltpu.make_async_remote_copy(
            src_ref=offered, dst_ref=ghost_ref.at[k], send_sem=send_sem.at[k], recv_sem=recv_sem.at[k],
            device_id=neighbour(offset, -1), device_id_type=MESH_IDS)
        copy.start()
        copies.append(copy)
    left = (jnp.dot(first_ref[...], feat, preferred_element_type=F32).astype(BF16).astype(F32) * 0.5).astype(BF16)
    tables_ref[:, 0:count] = left
    tables_ref[:, count:2 * count] = right
    for copy in copies:
        copy.wait()


def home_kernel(sums_ref, ghost_ref, send_ref, force_ref, energy_ref, arrived, send_sem, recv_sem):
    barrier = meet(-1)
    pl.semaphore_wait(barrier, len(OFFSETS))
    copies = []
    for k, offset in enumerate(OFFSETS):
        copy = pltpu.make_async_remote_copy(
            src_ref=ghost_ref.at[k], dst_ref=arrived.at[k], send_sem=send_sem.at[k], recv_sem=recv_sem.at[k],
            device_id=neighbour(offset, 1), device_id_type=MESH_IDS)
        copy.start()
        copies.append(copy)
    sums = sums_ref[...]
    count = sums.shape[1]
    energy_ref[...] = sums[3:4, :]
    hot = one_hot(send_ref[...], count)
    for copy in copies:
        copy.wait()
    total = arrived[0]
    for k in range(1, len(OFFSETS)):
        total = total + arrived[k]
    high, rest = split_two(total)
    mid, low = split_two(rest)
    parts = jnp.concatenate([high, mid, low, jnp.zeros_like(low)], 0).astype(BF16)
    back = lax.dot_general(parts, hot, NT, preferred_element_type=F32)
    back = back[0:8] + back[8:16] + back[16:24]
    force_ref[...] = sums[0:3, :] - back[0:3, :]


def take_lanes(table, index):
    return jnp.take_along_axis(table, index, axis=1, mode="promise_in_bounds")


def pairs_kernel(own_ref, tables_ref, ghost_ref, first_ref, second_ref, lmask_ref, gowner_ref, gindex_ref, gmask_ref,
                 radial_ref, mid_ref, last_ref, out_ref, sums_ref, gforce_ref,
                 own_tab, ghost_tab, gtable, words, live, ranks, packed, hot_own, hot_par, quant, back,
                 acc_own, acc_loc, acc_gho):
    count = own_ref.shape[1]
    chunks = count // 128
    blocks = len(OFFSETS)
    sends = ghost_ref.shape[2]
    gchunks = blocks * sends // 128
    lrows, grows = first_ref.shape[0], gowner_ref.shape[0]
    lane = lax.broadcasted_iota(I32, (8, 128), 1)

    for c in range(4):
        for ch in range(chunks):
            own_tab[c * chunks + ch] = jnp.broadcast_to(own_ref[c:c + 1, 128 * ch:128 * ch + 128], (8, 128))
    for k, offset in enumerate(OFFSETS):
        gtable[:, sends * k:sends * (k + 1)] = ghost_ref[k, 0:64, :]
        tail = ghost_ref[k, 64:80, :].astype(F32)
        for c in range(4):
            row = tail[c:c + 1] + tail[c + 3:c + 4] + float(offset[c]) if c < 3 else tail[6:7]
            for half in range(sends // 128):
                ghost_tab[c * gchunks + k * (sends // 128) + half] = jnp.broadcast_to(row[:, 128 * half:128 * half + 128], (8, 128))

    def pick(tab, n, c, low, high):
        value = take_lanes(tab[c * n], low)
        for ch in range(1, n):
            value = jnp.where(high == ch, take_lanes(tab[c * n + ch], low), value)
        return value

    def geometry(own, partner, tab, n):
        low_i, high_i, low_j, high_j = own & 127, own >> 7, partner & 127, partner >> 7
        gap = [pick(tab, n, c, low_j, high_j) - pick(own_tab, chunks, c, low_i, high_i) for c in range(3)]
        return gap, gap[0] * gap[0] + gap[1] * gap[1] + gap[2] * gap[2]

    for base, rows, own_list, par_list, mask_list, tab, n in (
        (0, lrows, first_ref, second_ref, lmask_ref, own_tab, chunks),
        (lrows, grows, gowner_ref, gindex_ref, gmask_ref, ghost_tab, gchunks),
    ):
        def find(v, carry, base=base, own_list=own_list, par_list=par_list, mask_list=mask_list, tab=tab, n=n):
            at = pl.ds(pl.multiple_of(8 * v, 8), 8)
            own, partner = own_list[at, :], par_list[at, :]
            gap, squared = geometry(own, partner, tab, n)
            alive = jnp.logical_and(mask_list[at, :] > 0, squared < 1.0)
            to = pl.ds(pl.multiple_of(base + 8 * v, 8), 8)
            live[to, :] = jnp.where(alive, 1.0, 0.0)
            words[to, :] = jnp.where(alive, (own << 8) + (partner << 17) + LIVE, 0)
            return carry
        lax.fori_loop(0, rows // 8, find, 0, unroll=4)

    above = jnp.where(lax.broadcasted_iota(I32, (128, 128), 0) < lax.broadcasted_iota(I32, (128, 128), 1), 1.0, 0.0)
    adder = jnp.concatenate([above, jnp.ones((128, 128), F32)], 1).astype(BF16)
    ranks[...] = jnp.dot(live[...].astype(BF16), adder, preferred_element_type=F32)

    trips = []
    for base, rows in ((0, lrows), (lrows, grows)):
        tiles = rows // 8
        stand = jnp.zeros((8, 128), I32)
        slots = [jnp.zeros((8, 128), I32) for _ in range(tiles)]
        for v in range(tiles):
            at = slice(base + 8 * v, base + 8 * v + 8)
            word = words[at, :]
            rank = ranks[at, 0:128].astype(I32)
            number = ranks[at, 128:256].astype(I32)
            word = jnp.where(word > 0, word + (lane - rank), 0)
            for bit in range(7):
                moved = pltpu.roll(word, 128 - (1 << bit), 1)
                stay = jnp.where((word & (1 << bit)) > 0, 0, word)
                word = jnp.where((moved & (1 << bit)) > 0, moved, stay)
            turn = (lane - stand) & 127
            word = take_lanes(word, turn)
            row = jnp.where(turn < number, (stand + turn) >> 7, -1)
            for t in range(v + 1):
                slots[t] = jnp.where(row == t, word, slots[t])
            stand = stand + number
        for t in range(tiles):
            packed[base + 8 * t:base + 8 * t + 8, :] = slots[t]
        trips.append((jnp.max(stand) + 127) >> 7)

    acc_own[...] = jnp.zeros_like(acc_own)
    acc_loc[...] = jnp.zeros_like(acc_loc)
    acc_gho[...] = jnp.zeros_like(acc_gho)

    w_mid = (mid_ref[...].astype(F32) * 0.5).astype(BF16)
    w_last = (last_ref[...].astype(F32) * 0.5).astype(BF16)
    radial_high, radial_low = split_two(radial_ref[...] * 0.5)
    nb = radial_ref.shape[1]
    spot = lax.broadcasted_iota(I32, (nb, 4 * nb), 1)
    term = lax.broadcasted_iota(I32, (nb, 4 * nb), 0)
    place_high = jnp.where((spot == term) | (spot == term + nb), 1.0, 0.0).astype(BF16)
    place_low = jnp.where(spot == term + 2 * nb, 1.0, 0.0).astype(BF16)
    w_radial = (jnp.dot(radial_high.astype(BF16), place_high, preferred_element_type=F32)
                + jnp.dot(radial_low.astype(BF16), place_low, preferred_element_type=F32)).astype(BF16)
    channels = mid_ref.shape[0]
    eye = lax.broadcasted_iota(I32, (channels, channels), 0) == lax.broadcasted_iota(I32, (channels, channels), 1)
    w_out = jnp.sum(jnp.where(eye, jnp.broadcast_to(out_ref[...], (channels, channels)), 0.0), 1, keepdims=True)
    centers = lax.broadcasted_iota(I32, (nb, 128), 0).astype(F32) / (nb - 1)

    def activate(y, tangent):
        up = 1.0 + jnp.tanh(y)
        value = y * up
        return value, (up + value * (2.0 - up)) * tangent

    for base, tab, n, acc_par, is_ghost in ((0, own_tab, chunks, acc_loc, False), (lrows, ghost_tab, gchunks, acc_gho, True)):
        def step(t, carry, base=base, tab=tab, n=n, acc_par=acc_par, is_ghost=is_ghost):
            word = packed[pl.ds(pl.multiple_of(base + 8 * t, 8), 8), :]
            own, partner = (word >> 8) & 511, word >> 17
            low_i, high_i, low_j, high_j = own & 127, own >> 7, partner & 127, partner >> 7
            gap, squared = geometry(own, partner, tab, n)
            weight = jnp.where((word & LIVE) > 0, pick(own_tab, chunks, 3, low_i, high_i) * pick(tab, n, 3, low_j, high_j), 0.0)
            reads, slopes = [], []
            for half in range(4):
                pair = (2 * half, 2 * half + 1)
                wide = lambda x: jnp.concatenate([x[r:r + 1] for r in pair], 1)
                li, hi, lj, hj = wide(low_i), wide(high_i), wide(low_j), wide(high_j)
                cols = slice(256 * half, 256 * half + 256)
                ho, hp = one_hot(li, 128), one_hot(lj, 128)
                hot_own[:, cols] = ho
                hot_par[:, cols] = hp
                zero = jnp.zeros((), BF16)
                hi_b = jnp.broadcast_to(hi.astype(jnp.int16), (128, 256))
                hj_b = jnp.broadcast_to(hj.astype(jnp.int16), (128, 256))
                hots_i = jnp.concatenate([jnp.where(hi_b == jnp.int16(ch), ho, zero) for ch in range(chunks)], 0)
                hots_j = jnp.concatenate([jnp.where(hj_b == jnp.int16(ch), hp, zero) for ch in range(n)], 0)
                tiles, slants = [], []
                for r in pair:
                    off = squared[r:r + 1] - centers
                    basis = jnp.exp(-WIDTH * off * off)
                    tiles.append(basis)
                    slants.append((-2.0 * WIDTH) * off * basis)
                both = jnp.concatenate(tiles + slants, 1)
                high, low = split_two(both)
                stack = jnp.concatenate([high, low, high, jnp.zeros_like(low)], 0).astype(BF16)
                radial = jnp.dot(w_radial, stack, preferred_element_type=F32)
                if is_ghost:
                    gathered = jnp.dot(tables_ref[:, 0:count], hots_i, preferred_element_type=F32) + jnp.dot(
                        gtable[...], hots_j, preferred_element_type=F32)
                else:
                    gathered = jnp.dot(tables_ref[...], jnp.concatenate([hots_i, hots_j], 0), preferred_element_type=F32)
                value, slope = activate(gathered + radial[:, 0:256], radial[:, 256:512])
                for w in (w_mid, w_last):
                    mixed = jnp.dot(w, jnp.concatenate([value, slope], 1).astype(BF16), preferred_element_type=F32)
                    value, slope = activate(mixed[:, 0:256], mixed[:, 256:512])
                reads.append(jnp.sum(value * w_out, 0, keepdims=True))
                slopes.append(jnp.sum(slope * w_out, 0, keepdims=True))
            tall = lambda xs: jnp.concatenate([x[:, 128 * k:128 * k + 128] for x in xs for k in range(2)], 0)
            readout, reslope = tall(reads), tall(slopes)
            near = jnp.maximum(1.0 - squared, 0.0)
            envelope = near * near
            energy = weight * envelope * readout
            slope = weight * (envelope * reslope - 2.0 * near * readout)
            outs = [2.0 * g * slope for g in gap] + [energy]
            splits = [split_two(x) for x in outs]
            for q in range(4):
                quant[8 * q:8 * q + 8, :] = splits[q][0]
                quant[32 + 8 * q:40 + 8 * q, :] = splits[q][1]
            a_own, a_par = [], []
            for r in range(8):
                tile = quant[pl.ds(r, 8, stride=8), :]
                a_own.append(jnp.concatenate([jnp.where(high_i[r:r + 1] == ch, tile, 0.0) for ch in range(chunks)], 0))
                a_par.append(jnp.concatenate([jnp.where(high_j[r:r + 1] == ch, tile, 0.0) for ch in range(n)], 0))
            acc_own[...] += lax.dot_general(jnp.concatenate(a_own, 1).astype(BF16), hot_own[...], NT, preferred_element_type=F32)
            acc_par[...] += lax.dot_general(jnp.concatenate(a_par, 1).astype(BF16), hot_par[...], NT, preferred_element_type=F32)
            return carry
        lax.fori_loop(0, trips[1 if is_ghost else 0], step, 0)

    for ch in range(chunks):
        own = acc_own[8 * ch:8 * ch + 4, :] + acc_own[8 * ch + 4:8 * ch + 8, :]
        loc = acc_loc[8 * ch:8 * ch + 4, :] + acc_loc[8 * ch + 4:8 * ch + 8, :]
        cols = slice(128 * ch, 128 * ch + 128)
        sums_ref[0:3, cols] = own[0:3] - loc[0:3]
        sums_ref[3:4, cols] = own[3:4]
        sums_ref[4:8, cols] = jnp.zeros((4, 128), F32)
    per = sends // 128
    for ch in range(gchunks):
        cols = slice(128 * (ch % per), 128 * (ch % per) + 128)
        gforce_ref[ch // per, 0:4, cols] = acc_gho[8 * ch:8 * ch + 4, :] + acc_gho[8 * ch + 4:8 * ch + 8, :]
        gforce_ref[ch // per, 4:8, cols] = jnp.zeros((4, 128), F32)


def call_pairs(own, tables, ghosts, first, second, lmask, gowner, gindex, gmask, w_radial, w_mid, w_last, w_out):
    count = own.shape[1]
    channels = w_mid.shape[0]
    gcount = len(OFFSETS) * ghosts.shape[2]
    total = first.shape[0] + gowner.shape[0]
    chunks, gchunks = count // 128, gcount // 128
    v = pltpu.VMEM
    return pl.pallas_call(
        pairs_kernel,
        name="pairs",
        out_shape=(jax.ShapeDtypeStruct((8, count), F32),
                   jax.ShapeDtypeStruct((len(OFFSETS), 8, ghosts.shape[2]), F32)),
        in_specs=[VMEM] * 13,
        out_specs=(VMEM, VMEM),
        scratch_shapes=[
            v((4 * chunks, 8, 128), F32), v((4 * gchunks, 8, 128), F32), v((channels, gcount), BF16),
            v((total, 128), I32), v((total, 128), F32), v((total, 256), F32), v((total, 128), I32),
            v((128, 1024), BF16), v((128, 1024), BF16), v((64, 128), F32), v((8, 128), F32),
            v((8 * chunks, 128), F32), v((8 * chunks, 128), F32), v((8 * gchunks, 128), F32),
        ],
        compiler_params=pltpu.CompilerParams(vmem_limit_bytes=48 << 20),
    )(own, tables, ghosts, first, second, lmask, gowner, gindex, gmask, w_radial, w_mid, w_last, w_out)


def on_device(positions, features, species, species_scale, w_first, w_second, w_radial, w_mid, w_last, w_out,
              ghost_send, local_first, local_second, local_mask, ghost_owner, ghost_index, ghost_mask):
    count = positions.shape[1]
    sends = ghost_send.shape[0]
    channels = features.shape[0]
    blocks = len(OFFSETS)
    send_row = ghost_send.reshape(1, sends)
    own, tables, ghosts = pl.pallas_call(
        offer_kernel,
        name="offer",
        out_shape=(jax.ShapeDtypeStruct((8, count), F32),
                   jax.ShapeDtypeStruct((channels, 2 * count), BF16),
                   jax.ShapeDtypeStruct((blocks, ROWS, sends), BF16)),
        in_specs=[VMEM] * 7,
        out_specs=(VMEM, VMEM, VMEM),
        scratch_shapes=[pltpu.VMEM((ROWS, sends), BF16), pltpu.SemaphoreType.DMA((blocks,)), pltpu.SemaphoreType.DMA((blocks,))],
        compiler_params=pltpu.CompilerParams(collective_id=0, has_side_effects=True),
    )(positions, features, species.reshape(1, count), species_scale.reshape(1, -1), w_first, w_second, send_row)
    lists = [x.reshape(-1, 128) for x in (local_first, local_second, local_mask, ghost_owner, ghost_index, ghost_mask)]
    sums, gforce = call_pairs(own, tables, ghosts, *lists, w_radial, w_mid, w_last, w_out.reshape(1, channels))
    forces, energy = pl.pallas_call(
        home_kernel,
        name="home",
        out_shape=(jax.ShapeDtypeStruct((3, count), F32), jax.ShapeDtypeStruct((1, count), F32)),
        in_specs=[VMEM] * 3,
        out_specs=(VMEM, VMEM),
        scratch_shapes=[pltpu.VMEM((blocks, 8, sends), F32), pltpu.SemaphoreType.DMA((blocks,)), pltpu.SemaphoreType.DMA((blocks,))],
        compiler_params=pltpu.CompilerParams(collective_id=1, has_side_effects=True),
    )(sums, gforce, send_row)
    return forces, energy.reshape(count)


def solution(mesh):
    everywhere = ("gx", "gy", "gz")
    wide, flat, copied = P(None, everywhere), P(everywhere), P()
    in_specs = (wide, wide, flat) + (copied,) * 7 + (flat,) * 7
    return jax.shard_map(on_device, mesh=mesh, in_specs=in_specs, out_specs=(wide, flat), check_vma=False)
```

```python
import jax
import jax.numpy as jnp
from jax import lax
from jax.experimental import pallas as pl
from jax.experimental.pallas import tpu as pltpu
from jax.sharding import PartitionSpec as P

OFFSETS = ((1, 0, 0), (0, 1, 0), (0, 0, 1), (1, 1, 0), (1, 0, 1), (0, 1, 1), (1, 1, 1))
DIRECT = (2, 0, 1, 3)
RELAYED = ((0, 4), (1, 5), (3, 6))
MESH_IDS = pl.DeviceIdType.MESH
ANY = pl.BlockSpec(memory_space=pl.ANY)
NT = (((1,), (1,)), ((), ()))
TN = (((0,), (0,)), ((), ()))
WIDTH = 24.0
F32, BF16, I32 = jnp.float32, jnp.bfloat16, jnp.int32
LIVE = 128
ROWS = 72
EARLY = 8
LATE = 4
HALVES = 4


def neighbour(offset, sign):
    where = []
    for axis, step in zip(("gx", "gy", "gz"), offset):
        count = lax.axis_size(axis)
        where.append(lax.rem(lax.axis_index(axis) + sign * step + count, count))
    return tuple(where)


def meet(offsets, sign):
    barrier = pltpu.get_barrier_semaphore()
    for offset in offsets:
        pl.semaphore_signal(barrier, inc=1, device_id=neighbour(offset, sign), device_id_type=MESH_IDS)
    return barrier


def move(sources, targets, sems):
    copies = [pltpu.make_async_copy(s, t, sems.at[k]) for k, (s, t) in enumerate(zip(sources, targets))]
    for copy in copies:
        copy.start()
    return copies


def finish(copies):
    for copy in copies:
        copy.wait()


def one_hot(row, count):
    levels = lax.broadcasted_iota(jnp.int16, (count, row.shape[1]), 0)
    return jnp.where(levels == row.astype(jnp.int16), jnp.ones((), BF16), jnp.zeros((), BF16))


def split_two(value):
    high = value.astype(BF16).astype(F32)
    return high, value - high


def take_lanes(table, index):
    return jnp.take_along_axis(table, index, axis=1, mode="promise_in_bounds")


def pick(tab, n, c, low, high):
    value = take_lanes(tab[c * n], low)
    for ch in range(1, n):
        value = jnp.where(high == ch, take_lanes(tab[c * n + ch], low), value)
    return value


def geometry(low_i, high_i, low_j, high_j, own_tab, tab, chunks, n):
    gap = [pick(tab, n, c, low_j, high_j) - pick(own_tab, chunks, c, low_i, high_i) for c in range(3)]
    return gap, gap[0] * gap[0] + gap[1] * gap[1] + gap[2] * gap[2]


def spread(row, tab, first):
    for ch in range(row.shape[1] // 128):
        tab[first + ch] = jnp.broadcast_to(row[:, 128 * ch:128 * ch + 128], (8, 128))


def compact(own_list, par_list, mask_list, own_tab, tab, chunks, n, words, live, ranks, packed):
    rows = own_list.shape[0]
    lane = lax.broadcasted_iota(I32, (8, 128), 1)

    def find(v, carry):
        at = pl.ds(pl.multiple_of(8 * v, 8), 8)
        own, partner = own_list[at, :], par_list[at, :]
        gap, squared = geometry(own & 127, own >> 7, partner & 127, partner >> 7, own_tab, tab, chunks, n)
        alive = jnp.logical_and(mask_list[at, :] > 0, squared < 1.0)
        live[at, :] = jnp.where(alive, 1.0, 0.0)
        words[at, :] = jnp.where(alive, (own << 8) + (partner << 17) + LIVE, 0)
        return carry
    lax.fori_loop(0, rows // 8, find, 0, unroll=4)
    above = jnp.where(lax.broadcasted_iota(I32, (128, 128), 0) < lax.broadcasted_iota(I32, (128, 128), 1), 1.0, 0.0)
    adder = jnp.concatenate([above, jnp.ones((128, 128), F32)], 1).astype(BF16)
    ranks[0:rows, :] = jnp.dot(live[0:rows, :].astype(BF16), adder, preferred_element_type=F32)

    tiles = rows // 8
    stand = jnp.zeros((8, 128), I32)
    slots = [jnp.zeros((8, 128), I32) for _ in range(tiles)]
    for v in range(tiles):
        at = slice(8 * v, 8 * v + 8)
        word = words[at, :]
        rank = ranks[at, 0:128].astype(I32)
        number = ranks[at, 128:256].astype(I32)
        word = jnp.where(word > 0, word + (lane - rank), 0)
        for bit in range(7):
            moved = pltpu.roll(word, 128 - (1 << bit), 1)
            stay = jnp.where((word & (1 << bit)) > 0, 0, word)
            word = jnp.where((moved & (1 << bit)) > 0, moved, stay)
        turn = (lane - stand) & 127
        word = take_lanes(word, turn)
        row = jnp.where(turn < number, (stand + turn) >> 7, -1)
        for t in range(v + 1):
            slots[t] = jnp.where(row == t, word, slots[t])
        stand = stand + number
    for t in range(tiles):
        packed[8 * t:8 * t + 8, :] = slots[t]
    return stand


def weights(radial, mid, last, out, w_mids, w_lasts, w_radials):
    nb, channels = radial.shape
    high, low = split_two(radial[...] * 0.5)
    spot = lax.broadcasted_iota(I32, (nb, 4 * nb), 1)
    term = lax.broadcasted_iota(I32, (nb, 4 * nb), 0)
    place_high = jnp.where((spot == term) | (spot == term + nb), 1.0, 0.0).astype(BF16)
    place_low = jnp.where(spot == term + 2 * nb, 1.0, 0.0).astype(BF16)
    w_radial = (lax.dot_general(high.astype(BF16), place_high, TN, preferred_element_type=F32)
                + lax.dot_general(low.astype(BF16), place_low, TN, preferred_element_type=F32)).astype(BF16)
    w_mid = (mid[...].astype(F32) * 0.5).astype(BF16)
    w_last = (last[...].astype(F32) * 0.5).astype(BF16)
    for store, w in ((w_mids, w_mid), (w_lasts, w_last), (w_radials, w_radial)):
        for half in range(HALVES):
            store[channels * half:channels * half + channels, :] = jnp.concatenate(
                [w if other == half else jnp.zeros_like(w) for other in range(HALVES)], 1)
    eye = lax.broadcasted_iota(I32, (channels, channels), 0) == lax.broadcasted_iota(I32, (channels, channels), 1)
    return jnp.sum(jnp.where(eye, jnp.broadcast_to(out[...], (channels, channels)), 0.0), 1, keepdims=True)


def activate(y, tangent):
    up = 1.0 + jnp.tanh(y)
    value = y * up
    return value, (up + value * (2.0 - up)) * tangent


def pair_step(packed, own_tab, tab, chunks, n, left_tab, right_tab, w_mids, w_lasts, w_radials, w_out,
              hot_own, hot_par, quant, acc_own, acc_par):
    nb = 8
    centers = lax.broadcasted_iota(I32, (nb, 128), 0).astype(F32) / (nb - 1)
    zero = jnp.zeros((), BF16)

    def step(t, carry):
        word = packed[pl.ds(pl.multiple_of(8 * t, 8), 8), :]
        own, partner = (word >> 8) & 511, word >> 17
        low_i, high_i, low_j, high_j = own & 127, own >> 7, partner & 127, partner >> 7
        wide = lambda x, half: jnp.concatenate([x[2 * half:2 * half + 1], x[2 * half + 1:2 * half + 2]], 1)

        def gather(low, high, keep, table, groups, half):
            hot = one_hot(wide(low, half), 128)
            keep[:, 256 * half:256 * half + 256] = hot
            top = wide(high, half)
            odd = jnp.broadcast_to((top & 1).astype(jnp.int16), (128, 256))
            hot = jnp.concatenate([jnp.where(odd == jnp.int16(0), hot, zero), jnp.where(odd == jnp.int16(1), hot, zero)], 0)
            found = jnp.dot(table[...], hot, preferred_element_type=F32)
            group = top >> 1
            value = found[0:64]
            for g in range(1, groups):
                value = jnp.where(group == g, found[64 * g:64 * g + 64], value)
            return value

        gathered = [gather(low_i, high_i, hot_own, left_tab, chunks // 2, half)
                    + gather(low_j, high_j, hot_par, right_tab, n // 2, half) for half in range(HALVES)]
        gap, squared = geometry(low_i, high_i, low_j, high_j, own_tab, tab, chunks, n)
        weight = jnp.where((word & LIVE) > 0, pick(own_tab, chunks, 3, low_i, high_i) * pick(tab, n, 3, low_j, high_j), 0.0)
        radials = []
        for half in range(HALVES):
            tiles, slants = [], []
            for r in (2 * half, 2 * half + 1):
                off = squared[r:r + 1] - centers
                basis = jnp.exp(-WIDTH * off * off)
                tiles.append(basis)
                slants.append((-2.0 * WIDTH) * off * basis)
            high, low = split_two(jnp.concatenate(tiles + slants, 1))
            radials += [high, low, high, jnp.zeros_like(low)]
        radials = jnp.dot(w_radials[...], jnp.concatenate(radials, 0).astype(BF16), preferred_element_type=F32)
        quarter = lambda x, half: x[64 * half:64 * half + 64]
        now = [activate(g + quarter(radials, half)[:, 0:256], quarter(radials, half)[:, 256:512]) for half, g in enumerate(gathered)]
        for w in (w_mids, w_lasts):
            stack = jnp.concatenate([jnp.concatenate(pair, 1).astype(BF16) for pair in now], 0)
            mixed = jnp.dot(w[...], stack, preferred_element_type=F32)
            now = [activate(quarter(mixed, half)[:, 0:256], quarter(mixed, half)[:, 256:512]) for half in range(HALVES)]
        reads = [jnp.sum(value * w_out, 0, keepdims=True) for value, _ in now]
        slopes = [jnp.sum(slope * w_out, 0, keepdims=True) for _, slope in now]
        tall = lambda xs: jnp.concatenate([x[:, 128 * k:128 * k + 128] for x in xs for k in range(2)], 0)
        readout, reslope = tall(reads), tall(slopes)
        near = jnp.maximum(1.0 - squared, 0.0)
        envelope = near * near
        energy = weight * envelope * readout
        slope = weight * (envelope * reslope - 2.0 * near * readout)
        outs = [2.0 * g * slope for g in gap] + [energy]
        for q, out in enumerate(outs):
            high, low = split_two(out)
            quant[8 * q:8 * q + 8, :] = high
            quant[32 + 8 * q:40 + 8 * q, :] = low
        a_own, a_par = [], []
        for r in range(8):
            tile = quant[pl.ds(r, 8, stride=8), :]
            a_own.append(jnp.concatenate([jnp.where(high_i[r:r + 1] == ch, tile, 0.0) for ch in range(chunks)], 0))
            a_par.append(jnp.concatenate([jnp.where(high_j[r:r + 1] == ch, tile, 0.0) for ch in range(n)], 0))
        acc_own[...] += lax.dot_general(jnp.concatenate(a_own, 1).astype(BF16), hot_own[...], NT, preferred_element_type=F32)
        acc_par[...] += lax.dot_general(jnp.concatenate(a_par, 1).astype(BF16), hot_par[...], NT, preferred_element_type=F32)
        return carry
    return step


def offer_kernel(pos_hbm, feat_hbm, species_hbm, scale_hbm, first_hbm, second_hbm, send_hbm,
                 one_hbm, two_hbm, mask_hbm, radial_hbm, mid_hbm, last_hbm, out_hbm,
                 own_out, left_out, right_out, ghost_out, packed_out, stand_out, acc_own_out, acc_loc_out,
                 pos, feat, species, scale, first, second, send, one, two, mask, radial, mid, last, out,
                 offered, own, left_tab, right_tab, packed, stand, acc_own, acc_loc,
                 own_tab, words, live, ranks, hot_own, hot_par, quant, w_mids, w_lasts, w_radials,
                 in_sem, out_sem, send_sem, recv_sem):
    paths = [OFFSETS[k] for k in DIRECT]
    barrier = meet(paths, 1)
    loads = move((pos_hbm, feat_hbm, species_hbm, scale_hbm, first_hbm, second_hbm, send_hbm,
                  one_hbm, two_hbm, mask_hbm, radial_hbm, mid_hbm, last_hbm, out_hbm),
                 (pos, feat, species, scale, first, second, send, one, two, mask, radial, mid, last, out), in_sem)
    finish(loads[0:7])
    count = pos.shape[1]
    chunks = count // 128
    where = pos[...]
    kinds = species[...]
    scales = scale[...].astype(F32)
    gain = jnp.zeros(kinds.shape, F32)
    for kind in range(scales.shape[1]):
        gain = jnp.where(kinds == kind, scales[:, kind:kind + 1], gain)
    right = (jnp.dot(second[...], feat[...], preferred_element_type=F32).astype(BF16).astype(F32) * 0.5).astype(BF16)
    high = where.astype(BF16).astype(F32)
    tail = jnp.concatenate([high, where - high, gain, jnp.zeros((9, count), F32)], 0).astype(BF16)
    payload = jnp.concatenate([right, tail], 0)
    offered[...] = jnp.dot(payload, one_hot(send[...], count), preferred_element_type=F32).astype(BF16)[0:ROWS]
    pl.semaphore_wait(barrier, len(paths))

    def remote(source, k, offset):
        copy = pltpu.make_async_remote_copy(
            src_ref=source, dst_ref=ghost_out.at[k], send_sem=send_sem.at[k], recv_sem=recv_sem.at[k],
            device_id=neighbour(offset, -1), device_id_type=MESH_IDS)
        copy.start()
        return copy
    copies = [remote(offered, k, OFFSETS[k]) for k in DIRECT]

    own[0:3, :] = where
    own[3:4, :] = gain
    own[4:8, :] = jnp.zeros((4, count), F32)
    left = (jnp.dot(first[...], feat[...], preferred_element_type=F32).astype(BF16).astype(F32) * 0.5).astype(BF16)
    for g in range(count // 256):
        left_tab[64 * g:64 * g + 64, :] = left[:, 256 * g:256 * g + 256]
        right_tab[64 * g:64 * g + 64, :] = right[:, 256 * g:256 * g + 256]
    for c in range(4):
        spread(own[c:c + 1, :], own_tab, c * chunks)
    finish(loads[7:])
    w_out = weights(radial, mid, last, out, w_mids, w_lasts, w_radials)
    copies[0].wait_recv()
    relays = [remote(ghost_out.at[2], k, OFFSETS[step]) for step, k in RELAYED]
    stand[...] = compact(one, two, mask, own_tab, own_tab, chunks, chunks, words, live, ranks, packed)
    acc_own[...] = jnp.zeros_like(acc_own)
    acc_loc[...] = jnp.zeros_like(acc_loc)
    step = pair_step(packed, own_tab, own_tab, chunks, chunks, left_tab, right_tab, w_mids, w_lasts, w_radials, w_out,
                     hot_own, hot_par, quant, acc_own, acc_loc)
    lax.fori_loop(0, EARLY, step, 0)
    stores = move((own, left_tab, right_tab, packed, stand, acc_own, acc_loc),
                  (own_out, left_out, right_out, packed_out, stand_out, acc_own_out, acc_loc_out), out_sem)
    copies[0].wait_send()
    finish(copies[1:])
    finish(relays)
    finish(stores)


def pairs_kernel(own_hbm, left_hbm, right_hbm, ghost_hbm, packed_hbm, stand_hbm, acc_own_hbm, acc_loc_hbm,
                 one_hbm, two_hbm, mask_hbm, radial_hbm, mid_hbm, last_hbm, out_hbm,
                 acc_own_out, acc_loc_out, force_out,
                 own, left_tab, right_tab, ghost, packed, stand, acc_own, acc_loc, one, two, mask, radial, mid, last, out,
                 own_tab, ghost_tab, gtable, gpacked, words, live, ranks, hot_own, hot_par, quant, acc_gho, force,
                 w_mids, w_lasts, w_radials, in_sem, out_sem):
    loads = move((own_hbm, ghost_hbm, one_hbm, two_hbm, mask_hbm, left_hbm, right_hbm, packed_hbm, stand_hbm,
                  acc_own_hbm, acc_loc_hbm, radial_hbm, mid_hbm, last_hbm, out_hbm),
                 (own, ghost, one, two, mask, left_tab, right_tab, packed, stand,
                  acc_own, acc_loc, radial, mid, last, out), in_sem)
    finish(loads)
    count = own.shape[1]
    chunks = count // 128
    sends = ghost.shape[2]
    per = sends // 128
    gchunks = len(OFFSETS) * per
    for c in range(4):
        spread(own[c:c + 1, :], own_tab, c * chunks)
    for k, offset in enumerate(OFFSETS):
        gtable[64 * k:64 * k + 64, :] = ghost[k, 0:64, :]
        tail = ghost[k, 64:72, :].astype(F32)
        for c in range(4):
            row = tail[c:c + 1] + tail[c + 3:c + 4] + float(offset[c]) if c < 3 else tail[6:7]
            spread(row, ghost_tab, c * gchunks + k * per)
    w_out = weights(radial, mid, last, out, w_mids, w_lasts, w_radials)
    gstand = compact(one, two, mask, own_tab, ghost_tab, chunks, gchunks, words, live, ranks, gpacked)
    acc_gho[...] = jnp.zeros_like(acc_gho)
    gstep = pair_step(gpacked, own_tab, ghost_tab, chunks, gchunks, left_tab, gtable, w_mids, w_lasts, w_radials, w_out,
                      hot_own, hot_par, quant, acc_own, acc_gho)
    lax.fori_loop(0, (jnp.max(gstand) + 127) >> 7, gstep, 0)
    for ch in range(gchunks):
        cols = slice(128 * (ch % per), 128 * (ch % per) + 128)
        force[ch // per, 0:4, cols] = acc_gho[8 * ch:8 * ch + 4, :] + acc_gho[8 * ch + 4:8 * ch + 8, :]
        force[ch // per, 4:8, cols] = jnp.zeros((4, 128), F32)
    step = pair_step(packed, own_tab, own_tab, chunks, chunks, left_tab, right_tab, w_mids, w_lasts, w_radials, w_out,
                     hot_own, hot_par, quant, acc_own, acc_loc)
    lax.fori_loop(EARLY + LATE, (jnp.max(stand[...]) + 127) >> 7, step, 0)
    finish(move((acc_own, acc_loc, force), (acc_own_out, acc_loc_out, force_out), out_sem))


def home_kernel(own_hbm, left_hbm, right_hbm, packed_hbm, acc_own_hbm, acc_loc_hbm, force_hbm, send_hbm,
                radial_hbm, mid_hbm, last_hbm, out_hbm,
                force_out, energy_out,
                own, left_tab, right_tab, packed, acc_own, acc_loc, force, send, radial, mid, last, out,
                arrived, own_tab, hot_own, hot_par, quant, w_mids, w_lasts, w_radials, result, energy,
                in_sem, out_sem, send_sem, recv_sem):
    barrier = meet(OFFSETS, -1)
    loads = move((force_hbm, own_hbm, left_hbm, right_hbm, packed_hbm, acc_own_hbm, acc_loc_hbm, send_hbm,
                  radial_hbm, mid_hbm, last_hbm, out_hbm),
                 (force, own, left_tab, right_tab, packed, acc_own, acc_loc, send, radial, mid, last, out), in_sem)
    loads[0].wait()
    pl.semaphore_wait(barrier, len(OFFSETS))
    copies = []
    for k, offset in enumerate(OFFSETS):
        copy = pltpu.make_async_remote_copy(
            src_ref=force.at[k], dst_ref=arrived.at[k], send_sem=send_sem.at[k], recv_sem=recv_sem.at[k],
            device_id=neighbour(offset, 1), device_id_type=MESH_IDS)
        copy.start()
        copies.append(copy)
    finish(loads[1:])
    count = own.shape[1]
    chunks = count // 128
    for c in range(4):
        spread(own[c:c + 1, :], own_tab, c * chunks)
    w_out = weights(radial, mid, last, out, w_mids, w_lasts, w_radials)
    step = pair_step(packed, own_tab, own_tab, chunks, chunks, left_tab, right_tab, w_mids, w_lasts, w_radials, w_out,
                     hot_own, hot_par, quant, acc_own, acc_loc)
    lax.fori_loop(EARLY, EARLY + LATE, step, 0)
    hot = one_hot(send[...], count)
    finish(copies)
    total = arrived[0]
    for k in range(1, len(OFFSETS)):
        total = total + arrived[k]
    high, rest = split_two(total)
    mid_part, low = split_two(rest)
    parts = jnp.concatenate([high, mid_part, low, jnp.zeros_like(low)], 0).astype(BF16)
    back = lax.dot_general(parts, hot, NT, preferred_element_type=F32)
    back = back[0:8] + back[8:16] + back[16:24]
    for ch in range(chunks):
        cols = slice(128 * ch, 128 * ch + 128)
        mine = acc_own[8 * ch:8 * ch + 4, :] + acc_own[8 * ch + 4:8 * ch + 8, :]
        other = acc_loc[8 * ch:8 * ch + 4, :] + acc_loc[8 * ch + 4:8 * ch + 8, :]
        result[:, cols] = mine[0:3] - other[0:3] - back[0:3, cols]
        energy[:, cols] = mine[3:4]
    finish(move((result, energy), (force_out, energy_out), out_sem))


def on_device(positions, features, species, species_scale, w_first, w_second, w_radial, w_mid, w_last, w_out,
              ghost_send, local_first, local_second, local_mask, ghost_owner, ghost_index, ghost_mask):
    v, shape = pltpu.VMEM, jax.ShapeDtypeStruct
    count = positions.shape[1]
    sends = ghost_send.shape[0]
    channels, nb = w_radial.shape
    blocks = len(OFFSETS)
    chunks, gchunks = count // 128, blocks * sends // 128
    lrows, grows = local_first.shape[0] // 128, ghost_owner.shape[0] // 128
    buffers = lambda arrays: [v(x.shape, x.dtype) for x in arrays]
    sems = lambda number: pltpu.SemaphoreType.DMA((number,))
    send_row = ghost_send.reshape(1, sends)
    net = [w_radial.T, w_mid, w_last, w_out.reshape(1, channels)]
    local = [x.reshape(lrows, 128) for x in (local_first, local_second, local_mask)]
    ghostly = [x.reshape(grows, 128) for x in (ghost_owner, ghost_index, ghost_mask)]
    blocks_w = [v((4 * channels, 4 * channels), BF16), v((4 * channels, 4 * channels), BF16), v((4 * channels, 16 * nb), BF16)]
    hots = [v((128, 1024), BF16), v((128, 1024), BF16), v((64, 128), F32)]
    table = shape((channels * count // 256, 256), BF16)
    acc = shape((8 * chunks, 128), F32)
    own_tab = v((4 * chunks, 8, 128), F32)

    args = [positions, features, species.reshape(1, count), species_scale.reshape(1, -1), w_first, w_second, send_row] + local + net
    made = [shape((8, count), F32), table, table, shape((blocks, ROWS, sends), BF16),
            shape((lrows, 128), I32), shape((8, 128), I32), acc, acc]
    own, left_tab, right_tab, ghosts, packed, stand, acc_own, acc_loc = pl.pallas_call(
        offer_kernel,
        name="offer",
        out_shape=made,
        in_specs=[ANY] * len(args),
        out_specs=[ANY] * len(made),
        scratch_shapes=buffers(args) + [v((ROWS, sends), BF16)] + buffers(made[0:3] + made[4:]) + [
            own_tab, v((lrows, 128), I32), v((lrows, 128), F32), v((lrows, 256), F32)] + hots + blocks_w + [
            sems(len(args)), sems(len(made) - 1), sems(blocks), sems(blocks)],
        compiler_params=pltpu.CompilerParams(collective_id=0, has_side_effects=True, vmem_limit_bytes=48 << 20),
    )(*args)

    args = [own, left_tab, right_tab, ghosts, packed, stand, acc_own, acc_loc] + ghostly + net
    made = [acc, acc, shape((blocks, 8, sends), F32)]
    acc_own, acc_loc, gforce = pl.pallas_call(
        pairs_kernel,
        name="pairs",
        out_shape=made,
        in_specs=[ANY] * len(args),
        out_specs=[ANY] * len(made),
        scratch_shapes=buffers(args) + [
            own_tab, v((4 * gchunks, 8, 128), F32), v((channels * gchunks // 2, 256), BF16), v((grows, 128), I32),
            v((grows, 128), I32), v((grows, 128), F32), v((grows, 256), F32)] + hots + [
            v((8 * gchunks, 128), F32), v((blocks, 8, sends), F32)] + blocks_w + [sems(len(args)), sems(len(made))],
        compiler_params=pltpu.CompilerParams(vmem_limit_bytes=48 << 20),
    )(*args)

    args = [own, left_tab, right_tab, packed, acc_own, acc_loc, gforce, send_row] + net
    made = [shape((3, count), F32), shape((1, count), F32)]
    forces, energy = pl.pallas_call(
        home_kernel,
        name="home",
        out_shape=made,
        in_specs=[ANY] * len(args),
        out_specs=[ANY] * len(made),
        scratch_shapes=buffers(args) + [v((blocks, 8, sends), F32), own_tab] + hots + blocks_w + buffers(made) + [
            sems(len(args)), sems(len(made)), sems(blocks), sems(blocks)],
        compiler_params=pltpu.CompilerParams(collective_id=1, has_side_effects=True, vmem_limit_bytes=48 << 20),
    )(*args)
    return forces, energy.reshape(count)


def solution(mesh):
    everywhere = ("gx", "gy", "gz")
    wide, flat, copied = P(None, everywhere), P(everywhere), P()
    in_specs = (wide, wide, flat) + (copied,) * 7 + (flat,) * 7
    return jax.shard_map(on_device, mesh=mesh, in_specs=in_specs, out_specs=(wide, flat), check_vma=False)
```

```python
import jax
import jax.numpy as jnp
from jax import lax
from jax.experimental import pallas as pl
from jax.experimental.pallas import tpu as pltpu
from jax.sharding import PartitionSpec as P

OFFSETS = ((1, 0, 0), (0, 1, 0), (0, 0, 1), (1, 1, 0), (1, 0, 1), (0, 1, 1), (1, 1, 1))
DIRECT = (2, 0, 1, 3)
RELAYED = ((0, 4), (1, 5), (3, 6))
MESH_IDS = pl.DeviceIdType.MESH
HBM = pl.BlockSpec(memory_space=pltpu.HBM)
NT = (((1,), (1,)), ((), ()))
TN = (((0,), (0,)), ((), ()))
WIDTH = 24.0
F32, BF16, I32 = jnp.float32, jnp.bfloat16, jnp.int32
LIVE = 128
ROWS = 72
EARLY = 8
LATE = 4
HALVES = 4
U = 2
LAG = 0


def neighbour(offset, sign):
    where = []
    for axis, step in zip(("gx", "gy", "gz"), offset):
        count = lax.axis_size(axis)
        where.append(lax.rem(lax.axis_index(axis) + sign * step + count, count))
    return tuple(where)


def meet(offsets, sign):
    barrier = pltpu.get_barrier_semaphore()
    for offset in offsets:
        pl.semaphore_signal(barrier, inc=1, device_id=neighbour(offset, sign), device_id_type=MESH_IDS)
    return barrier


def move(sources, targets, sems):
    copies = [pltpu.make_async_copy(s, t, sems.at[k]) for k, (s, t) in enumerate(zip(sources, targets))]
    for copy in copies:
        copy.start()
    return copies


def finish(copies):
    for copy in copies:
        copy.wait()


def one_hot(row, count):
    levels = lax.broadcasted_iota(jnp.int16, (count, row.shape[1]), 0)
    return jnp.where(levels == row.astype(jnp.int16), jnp.ones((), BF16), jnp.zeros((), BF16))


def split_two(value):
    high = value.astype(BF16).astype(F32)
    return high, value - high


def take_lanes(table, index):
    return jnp.take_along_axis(table, index, axis=1, mode="promise_in_bounds")


def pick(tab, n, c, low, high):
    value = take_lanes(tab[c * n], low)
    for ch in range(1, n):
        value = jnp.where(high == ch, take_lanes(tab[c * n + ch], low), value)
    return value


def geometry(low_i, high_i, low_j, high_j, own_tab, tab, chunks, n):
    gap = [pick(tab, n, c, low_j, high_j) - pick(own_tab, chunks, c, low_i, high_i) for c in range(3)]
    return gap, gap[0] * gap[0] + gap[1] * gap[1] + gap[2] * gap[2]


def spread(row, tab, first):
    for ch in range(row.shape[1] // 128):
        tab[first + ch] = jnp.broadcast_to(row[:, 128 * ch:128 * ch + 128], (8, 128))


def compact(own_list, par_list, mask_list, own_tab, tab, chunks, n, words, live, ranks, packed):
    rows = own_list.shape[0]
    lane = lax.broadcasted_iota(I32, (8, 128), 1)

    def find(v, carry):
        at = pl.ds(pl.multiple_of(8 * v, 8), 8)
        own, partner = own_list[at, :], par_list[at, :]
        gap, squared = geometry(own & 127, own >> 7, partner & 127, partner >> 7, own_tab, tab, chunks, n)
        alive = jnp.logical_and(mask_list[at, :] > 0, squared < 1.0)
        live[at, :] = jnp.where(alive, 1.0, 0.0)
        words[at, :] = jnp.where(alive, (own << 8) + (partner << 17) + LIVE, 0)
        return carry
    lax.fori_loop(0, rows // 8, find, 0, unroll=4)
    above = jnp.where(lax.broadcasted_iota(I32, (128, 128), 0) < lax.broadcasted_iota(I32, (128, 128), 1), 1.0, 0.0)
    adder = jnp.concatenate([above, jnp.ones((128, 128), F32)], 1).astype(BF16)
    ranks[0:rows, :] = jnp.dot(live[0:rows, :].astype(BF16), adder, preferred_element_type=F32)

    tiles = rows // 8
    stand = jnp.zeros((8, 128), I32)
    slots = [jnp.zeros((8, 128), I32) for _ in range(tiles)]
    for v in range(tiles):
        at = slice(8 * v, 8 * v + 8)
        word = words[at, :]
        rank = ranks[at, 0:128].astype(I32)
        number = ranks[at, 128:256].astype(I32)
        word = jnp.where(word > 0, word + (lane - rank), 0)
        for bit in range(7):
            moved = pltpu.roll(word, 128 - (1 << bit), 1)
            stay = jnp.where((word & (1 << bit)) > 0, 0, word)
            word = jnp.where((moved & (1 << bit)) > 0, moved, stay)
        turn = (lane - stand) & 127
        word = take_lanes(word, turn)
        row = jnp.where(turn < number, (stand + turn) >> 7, -1)
        for t in range(v + 1):
            slots[t] = jnp.where(row == t, word, slots[t])
        stand = stand + number
    for t in range(tiles):
        packed[8 * t:8 * t + 8, :] = slots[t]
    return stand


def weights(radial, mid, last, out, w_mids, w_lasts, w_radials):
    nb, channels = radial.shape
    high, low = split_two(radial[...] * 0.5)
    spot = lax.broadcasted_iota(I32, (nb, 4 * nb), 1)
    term = lax.broadcasted_iota(I32, (nb, 4 * nb), 0)
    place_high = jnp.where((spot == term) | (spot == term + nb), 1.0, 0.0).astype(BF16)
    place_low = jnp.where(spot == term + 2 * nb, 1.0, 0.0).astype(BF16)
    w_radial = (lax.dot_general(high.astype(BF16), place_high, TN, preferred_element_type=F32)
                + lax.dot_general(low.astype(BF16), place_low, TN, preferred_element_type=F32)).astype(BF16)
    w_mid = (mid[...].astype(F32) * 0.5).astype(BF16)
    w_last = (last[...].astype(F32) * 0.5).astype(BF16)
    for store, w in ((w_mids, w_mid), (w_lasts, w_last), (w_radials, w_radial)):
        for half in range(HALVES):
            store[channels * half:channels * half + channels, :] = jnp.concatenate(
                [w if other == half else jnp.zeros_like(w) for other in range(HALVES)], 1)
    eye = lax.broadcasted_iota(I32, (channels, channels), 0) == lax.broadcasted_iota(I32, (channels, channels), 1)
    return jnp.sum(jnp.where(eye, jnp.broadcast_to(out[...], (channels, channels)), 0.0), 1, keepdims=True)


def activate(y, tangent):
    up = 1.0 + jnp.tanh(y)
    value = y * up
    return value, (up + value * (2.0 - up)) * tangent


def pair_step(packed, own_tab, tab, chunks, n, left_tab, right_tab, w_mids, w_lasts, w_radials, w_out,
              hot_own, hot_par, quant, acc_own, acc_par):
    nb = 8
    centers = lax.broadcasted_iota(I32, (nb, 128), 0).astype(F32) / (nb - 1)
    zero = jnp.zeros((), BF16)

    def stages(t, u):
        word = packed[pl.ds(pl.multiple_of(8 * t, 8), 8), :]
        own, partner = (word >> 8) & 511, word >> 17
        low_i, high_i, low_j, high_j = own & 127, own >> 7, partner & 127, partner >> 7
        wide = lambda x, half: jnp.concatenate([x[2 * half:2 * half + 1], x[2 * half + 1:2 * half + 2]], 1)

        def gather(low, high, keep, table, groups, half):
            hot = one_hot(wide(low, half), 128)
            keep[u, :, 256 * half:256 * half + 256] = hot
            top = wide(high, half)
            odd = jnp.broadcast_to((top & 1).astype(jnp.int16), (128, 256))
            hot = jnp.concatenate([jnp.where(odd == jnp.int16(0), hot, zero), jnp.where(odd == jnp.int16(1), hot, zero)], 0)
            found = jnp.dot(table[...], hot, preferred_element_type=F32)
            group = top >> 1
            value = found[0:64]
            for g in range(1, groups):
                value = jnp.where(group == g, found[64 * g:64 * g + 64], value)
            return value

        gathered = [gather(low_i, high_i, hot_own, left_tab, chunks // 2, half)
                    + gather(low_j, high_j, hot_par, right_tab, n // 2, half) for half in range(HALVES)]
        yield
        gap, squared = geometry(low_i, high_i, low_j, high_j, own_tab, tab, chunks, n)
        weight = jnp.where((word & LIVE) > 0, pick(own_tab, chunks, 3, low_i, high_i) * pick(tab, n, 3, low_j, high_j), 0.0)
        radials = []
        for half in range(HALVES):
            tiles, slants = [], []
            for r in (2 * half, 2 * half + 1):
                off = squared[r:r + 1] - centers
                basis = jnp.exp(-WIDTH * off * off)
                tiles.append(basis)
                slants.append((-2.0 * WIDTH) * off * basis)
            high, low = split_two(jnp.concatenate(tiles + slants, 1))
            radials += [high, low, high, jnp.zeros_like(low)]
        radials = jnp.dot(w_radials[...], jnp.concatenate(radials, 0).astype(BF16), preferred_element_type=F32)
        yield
        quarter = lambda x, half: x[64 * half:64 * half + 64]
        now = [activate(g + quarter(radials, half)[:, 0:256], quarter(radials, half)[:, 256:512]) for half, g in enumerate(gathered)]
        for w in (w_mids, w_lasts):
            stack = jnp.concatenate([jnp.concatenate(pair, 1).astype(BF16) for pair in now], 0)
            mixed = jnp.dot(w[...], stack, preferred_element_type=F32)
            yield
            now = [activate(quarter(mixed, half)[:, 0:256], quarter(mixed, half)[:, 256:512]) for half in range(HALVES)]
        reads = [jnp.sum(value * w_out, 0, keepdims=True) for value, _ in now]
        slopes = [jnp.sum(slope * w_out, 0, keepdims=True) for _, slope in now]
        yield
        tall = lambda xs: jnp.concatenate([x[:, 128 * k:128 * k + 128] for x in xs for k in range(2)], 0)
        readout, reslope = tall(reads), tall(slopes)
        near = jnp.maximum(1.0 - squared, 0.0)
        envelope = near * near
        energy = weight * envelope * readout
        slope = weight * (envelope * reslope - 2.0 * near * readout)
        outs = [2.0 * g * slope for g in gap] + [energy]
        for q, out in enumerate(outs):
            high, low = split_two(out)
            quant[u, 8 * q:8 * q + 8, :] = high
            quant[u, 32 + 8 * q:40 + 8 * q, :] = low
        a_own, a_par = [], []
        for r in range(8):
            tile = quant[u, pl.ds(r, 8, stride=8), :]
            a_own.append(jnp.concatenate([jnp.where(high_i[r:r + 1] == ch, tile, 0.0) for ch in range(chunks)], 0))
            a_par.append(jnp.concatenate([jnp.where(high_j[r:r + 1] == ch, tile, 0.0) for ch in range(n)], 0))
        acc_own[...] += lax.dot_general(jnp.concatenate(a_own, 1).astype(BF16), hot_own[u], NT, preferred_element_type=F32)
        acc_par[...] += lax.dot_general(jnp.concatenate(a_par, 1).astype(BF16), hot_par[u], NT, preferred_element_type=F32)

    def step(t, carry):
        streams = [stages(U * t + u, u) for u in range(U)]
        done, clock = 0, 0
        while done < U:
            for u, stream in enumerate(streams):
                if stream is not None and clock >= LAG * u:
                    try:
                        next(stream)
                    except StopIteration:
                        streams[u] = None
                        done += 1
            clock += 1
        return carry
    return step


def trips(stand):
    return (jnp.max(stand) + 128 * U - 1) // (128 * U)


def offer_kernel(pos_hbm, feat_hbm, species_hbm, scale_hbm, first_hbm, second_hbm, send_hbm,
                 one_hbm, two_hbm, mask_hbm, radial_hbm, mid_hbm, last_hbm, out_hbm,
                 own_out, left_out, right_out, ghost_out, packed_out, stand_out, acc_own_out, acc_loc_out,
                 pos, feat, species, scale, first, second, send, one, two, mask, radial, mid, last, out,
                 offered, own, left_tab, right_tab, packed, stand, acc_own, acc_loc,
                 own_tab, words, live, ranks, hot_own, hot_par, quant, w_mids, w_lasts, w_radials,
                 in_sem, out_sem, send_sem, recv_sem):
    paths = [OFFSETS[k] for k in DIRECT]
    barrier = meet(paths, 1)
    loads = move((pos_hbm, feat_hbm, species_hbm, scale_hbm, first_hbm, second_hbm, send_hbm,
                  one_hbm, two_hbm, mask_hbm, radial_hbm, mid_hbm, last_hbm, out_hbm),
                 (pos, feat, species, scale, first, second, send, one, two, mask, radial, mid, last, out), in_sem)
    finish(loads[0:7])
    count = pos.shape[1]
    chunks = count // 128
    where = pos[...]
    kinds = species[...]
    scales = scale[...].astype(F32)
    gain = jnp.zeros(kinds.shape, F32)
    for kind in range(scales.shape[1]):
        gain = jnp.where(kinds == kind, scales[:, kind:kind + 1], gain)
    right = (jnp.dot(second[...], feat[...], preferred_element_type=F32).astype(BF16).astype(F32) * 0.5).astype(BF16)
    high = where.astype(BF16).astype(F32)
    tail = jnp.concatenate([high, where - high, gain, jnp.zeros((9, count), F32)], 0).astype(BF16)
    payload = jnp.concatenate([right, tail], 0)
    offered[...] = jnp.dot(payload, one_hot(send[...], count), preferred_element_type=F32).astype(BF16)[0:ROWS]
    pl.semaphore_wait(barrier, len(paths))

    def remote(source, k, offset):
        copy = pltpu.make_async_remote_copy(
            src_ref=source, dst_ref=ghost_out.at[k], send_sem=send_sem.at[k], recv_sem=recv_sem.at[k],
            device_id=neighbour(offset, -1), device_id_type=MESH_IDS)
        copy.start()
        return copy
    copies = [remote(offered, k, OFFSETS[k]) for k in DIRECT]

    own[0:3, :] = where
    own[3:4, :] = gain
    own[4:8, :] = jnp.zeros((4, count), F32)
    left = (jnp.dot(first[...], feat[...], preferred_element_type=F32).astype(BF16).astype(F32) * 0.5).astype(BF16)
    for g in range(count // 256):
        left_tab[64 * g:64 * g + 64, :] = left[:, 256 * g:256 * g + 256]
        right_tab[64 * g:64 * g + 64, :] = right[:, 256 * g:256 * g + 256]
    for c in range(4):
        spread(own[c:c + 1, :], own_tab, c * chunks)
    finish(loads[7:])
    w_out = weights(radial, mid, last, out, w_mids, w_lasts, w_radials)
    copies[0].wait_recv()
    relays = [remote(ghost_out.at[2], k, OFFSETS[step]) for step, k in RELAYED]
    stand[...] = compact(one, two, mask, own_tab, own_tab, chunks, chunks, words, live, ranks, packed)
    acc_own[...] = jnp.zeros_like(acc_own)
    acc_loc[...] = jnp.zeros_like(acc_loc)
    step = pair_step(packed, own_tab, own_tab, chunks, chunks, left_tab, right_tab, w_mids, w_lasts, w_radials, w_out,
                     hot_own, hot_par, quant, acc_own, acc_loc)
    lax.fori_loop(0, EARLY // U, step, 0)
    stores = move((own, left_tab, right_tab, packed, stand, acc_own, acc_loc),
                  (own_out, left_out, right_out, packed_out, stand_out, acc_own_out, acc_loc_out), out_sem)
    copies[0].wait_send()
    finish(copies[1:])
    finish(relays)
    finish(stores)


def pairs_kernel(own_hbm, left_hbm, right_hbm, ghost_hbm, packed_hbm, stand_hbm, acc_own_hbm, acc_loc_hbm,
                 one_hbm, two_hbm, mask_hbm, radial_hbm, mid_hbm, last_hbm, out_hbm,
                 acc_own_out, acc_loc_out, force_out,
                 own, left_tab, right_tab, ghost, packed, stand, acc_own, acc_loc, one, two, mask, radial, mid, last, out,
                 own_tab, ghost_tab, gtable, gpacked, words, live, ranks, hot_own, hot_par, quant, acc_gho, force,
                 w_mids, w_lasts, w_radials, in_sem, out_sem):
    loads = move((own_hbm, ghost_hbm, one_hbm, two_hbm, mask_hbm, left_hbm, right_hbm, packed_hbm, stand_hbm,
                  acc_own_hbm, acc_loc_hbm, radial_hbm, mid_hbm, last_hbm, out_hbm),
                 (own, ghost, one, two, mask, left_tab, right_tab, packed, stand,
                  acc_own, acc_loc, radial, mid, last, out), in_sem)
    finish(loads)
    count = own.shape[1]
    chunks = count // 128
    sends = ghost.shape[2]
    per = sends // 128
    gchunks = len(OFFSETS) * per
    for c in range(4):
        spread(own[c:c + 1, :], own_tab, c * chunks)
    for k, offset in enumerate(OFFSETS):
        gtable[64 * k:64 * k + 64, :] = ghost[k, 0:64, :]
        tail = ghost[k, 64:72, :].astype(F32)
        for c in range(4):
            row = tail[c:c + 1] + tail[c + 3:c + 4] + float(offset[c]) if c < 3 else tail[6:7]
            spread(row, ghost_tab, c * gchunks + k * per)
    w_out = weights(radial, mid, last, out, w_mids, w_lasts, w_radials)
    gstand = compact(one, two, mask, own_tab, ghost_tab, chunks, gchunks, words, live, ranks, gpacked)
    acc_gho[...] = jnp.zeros_like(acc_gho)
    gstep = pair_step(gpacked, own_tab, ghost_tab, chunks, gchunks, left_tab, gtable, w_mids, w_lasts, w_radials, w_out,
                      hot_own, hot_par, quant, acc_own, acc_gho)
    lax.fori_loop(0, trips(gstand), gstep, 0)
    for ch in range(gchunks):
        cols = slice(128 * (ch % per), 128 * (ch % per) + 128)
        force[ch // per, 0:4, cols] = acc_gho[8 * ch:8 * ch + 4, :] + acc_gho[8 * ch + 4:8 * ch + 8, :]
        force[ch // per, 4:8, cols] = jnp.zeros((4, 128), F32)
    step = pair_step(packed, own_tab, own_tab, chunks, chunks, left_tab, right_tab, w_mids, w_lasts, w_radials, w_out,
                     hot_own, hot_par, quant, acc_own, acc_loc)
    lax.fori_loop((EARLY + LATE) // U, trips(stand[...]), step, 0)
    finish(move((acc_own, acc_loc, force), (acc_own_out, acc_loc_out, force_out), out_sem))


def home_kernel(own_hbm, left_hbm, right_hbm, packed_hbm, acc_own_hbm, acc_loc_hbm, force_hbm, send_hbm,
                radial_hbm, mid_hbm, last_hbm, out_hbm,
                force_out, energy_out,
                own, left_tab, right_tab, packed, acc_own, acc_loc, force, send, radial, mid, last, out,
                arrived, own_tab, hot_own, hot_par, quant, w_mids, w_lasts, w_radials, result, energy,
                in_sem, out_sem, send_sem, recv_sem):
    barrier = meet(OFFSETS, -1)
    loads = move((force_hbm, own_hbm, left_hbm, right_hbm, packed_hbm, acc_own_hbm, acc_loc_hbm, send_hbm,
                  radial_hbm, mid_hbm, last_hbm, out_hbm),
                 (force, own, left_tab, right_tab, packed, acc_own, acc_loc, send, radial, mid, last, out), in_sem)
    loads[0].wait()
    pl.semaphore_wait(barrier, len(OFFSETS))
    copies = []
    for k, offset in enumerate(OFFSETS):
        copy = pltpu.make_async_remote_copy(
            src_ref=force.at[k], dst_ref=arrived.at[k], send_sem=send_sem.at[k], recv_sem=recv_sem.at[k],
            device_id=neighbour(offset, 1), device_id_type=MESH_IDS)
        copy.start()
        copies.append(copy)
    finish(loads[1:])
    count = own.shape[1]
    chunks = count // 128
    for c in range(4):
        spread(own[c:c + 1, :], own_tab, c * chunks)
    w_out = weights(radial, mid, last, out, w_mids, w_lasts, w_radials)
    step = pair_step(packed, own_tab, own_tab, chunks, chunks, left_tab, right_tab, w_mids, w_lasts, w_radials, w_out,
                     hot_own, hot_par, quant, acc_own, acc_loc)
    lax.fori_loop(EARLY // U, (EARLY + LATE) // U, step, 0)
    hot = one_hot(send[...], count)
    finish(copies)
    total = arrived[0]
    for k in range(1, len(OFFSETS)):
        total = total + arrived[k]
    high, rest = split_two(total)
    mid_part, low = split_two(rest)
    parts = jnp.concatenate([high, mid_part, low, jnp.zeros_like(low)], 0).astype(BF16)
    back = lax.dot_general(parts, hot, NT, preferred_element_type=F32)
    back = back[0:8] + back[8:16] + back[16:24]
    for ch in range(chunks):
        cols = slice(128 * ch, 128 * ch + 128)
        mine = acc_own[8 * ch:8 * ch + 4, :] + acc_own[8 * ch + 4:8 * ch + 8, :]
        other = acc_loc[8 * ch:8 * ch + 4, :] + acc_loc[8 * ch + 4:8 * ch + 8, :]
        result[:, cols] = mine[0:3] - other[0:3] - back[0:3, cols]
        energy[:, cols] = mine[3:4]
    finish(move((result, energy), (force_out, energy_out), out_sem))


def on_device(positions, features, species, species_scale, w_first, w_second, w_radial, w_mid, w_last, w_out,
              ghost_send, local_first, local_second, local_mask, ghost_owner, ghost_index, ghost_mask):
    v, shape = pltpu.VMEM, jax.ShapeDtypeStruct
    count = positions.shape[1]
    sends = ghost_send.shape[0]
    channels, nb = w_radial.shape
    blocks = len(OFFSETS)
    chunks, gchunks = count // 128, blocks * sends // 128
    lrows, grows = local_first.shape[0] // 128, ghost_owner.shape[0] // 128
    buffers = lambda arrays: [v(x.shape, x.dtype) for x in arrays]
    sems = lambda number: pltpu.SemaphoreType.DMA((number,))
    send_row = ghost_send.reshape(1, sends)
    net = [w_radial.T, w_mid, w_last, w_out.reshape(1, channels)]
    local = [x.reshape(lrows, 128) for x in (local_first, local_second, local_mask)]
    ghostly = [x.reshape(grows, 128) for x in (ghost_owner, ghost_index, ghost_mask)]
    blocks_w = [v((4 * channels, 4 * channels), BF16), v((4 * channels, 4 * channels), BF16), v((4 * channels, 16 * nb), BF16)]
    hots = [v((U, 128, 1024), BF16), v((U, 128, 1024), BF16), v((U, 64, 128), F32)]
    table = shape((channels * count // 256, 256), BF16)
    acc = shape((8 * chunks, 128), F32)
    own_tab = v((4 * chunks, 8, 128), F32)

    args = [positions, features, species.reshape(1, count), species_scale.reshape(1, -1), w_first, w_second, send_row] + local + net
    made = [shape((8, count), F32), table, table, shape((blocks, ROWS, sends), BF16),
            shape((lrows, 128), I32), shape((8, 128), I32), acc, acc]
    own, left_tab, right_tab, ghosts, packed, stand, acc_own, acc_loc = pl.pallas_call(
        offer_kernel,
        name="offer",
        out_shape=made,
        in_specs=[HBM] * len(args),
        out_specs=[HBM] * len(made),
        scratch_shapes=buffers(args) + [v((ROWS, sends), BF16)] + buffers(made[0:3] + made[4:]) + [
            own_tab, v((lrows, 128), I32), v((lrows, 128), F32), v((lrows, 256), F32)] + hots + blocks_w + [
            sems(len(args)), sems(len(made) - 1), sems(blocks), sems(blocks)],
        compiler_params=pltpu.CompilerParams(collective_id=0, has_side_effects=True, vmem_limit_bytes=60 << 20),
    )(*args)

    args = [own, left_tab, right_tab, ghosts, packed, stand, acc_own, acc_loc] + ghostly + net
    made = [acc, acc, shape((blocks, 8, sends), F32)]
    acc_own, acc_loc, gforce = pl.pallas_call(
        pairs_kernel,
        name="pairs",
        out_shape=made,
        in_specs=[HBM] * len(args),
        out_specs=[HBM] * len(made),
        scratch_shapes=buffers(args) + [
            own_tab, v((4 * gchunks, 8, 128), F32), v((channels * gchunks // 2, 256), BF16), v((grows, 128), I32),
            v((grows, 128), I32), v((grows, 128), F32), v((grows, 256), F32)] + hots + [
            v((8 * gchunks, 128), F32), v((blocks, 8, sends), F32)] + blocks_w + [sems(len(args)), sems(len(made))],
        compiler_params=pltpu.CompilerParams(vmem_limit_bytes=60 << 20),
    )(*args)

    args = [own, left_tab, right_tab, packed, acc_own, acc_loc, gforce, send_row] + net
    made = [shape((3, count), F32), shape((1, count), F32)]
    forces, energy = pl.pallas_call(
        home_kernel,
        name="home",
        out_shape=made,
        in_specs=[HBM] * len(args),
        out_specs=[HBM] * len(made),
        scratch_shapes=buffers(args) + [v((blocks, 8, sends), F32), own_tab] + hots + blocks_w + buffers(made) + [
            sems(len(args)), sems(len(made)), sems(blocks), sems(blocks)],
        compiler_params=pltpu.CompilerParams(collective_id=1, has_side_effects=True, vmem_limit_bytes=60 << 20),
    )(*args)
    return forces, energy.reshape(count)


def solution(mesh):
    everywhere = ("gx", "gy", "gz")
    wide, flat, copied = P(None, everywhere), P(everywhere), P()
    in_specs = (wide, wide, flat) + (copied,) * 7 + (flat,) * 7
    return jax.shard_map(on_device, mesh=mesh, in_specs=in_specs, out_specs=(wide, flat), check_vma=False)
```

```python
import jax
import jax.numpy as jnp
from jax import lax
from jax.experimental import pallas as pl
from jax.experimental.pallas import tpu as pltpu
from jax.sharding import PartitionSpec as P

OFFSETS = ((1, 0, 0), (0, 1, 0), (0, 0, 1), (1, 1, 0), (1, 0, 1), (0, 1, 1), (1, 1, 1))
DIRECT = (2, 0, 1, 3)
RELAYED = ((0, 4), (1, 5), (3, 6))
MESH_IDS = pl.DeviceIdType.MESH
HBM = pl.BlockSpec(memory_space=pltpu.HBM)
NT = (((1,), (1,)), ((), ()))
TN = (((0,), (0,)), ((), ()))
WIDTH = 24.0
F32, BF16, I32 = jnp.float32, jnp.bfloat16, jnp.int32
LIVE = 128
ROWS = 72
EARLY = 8
LATE = 8
HALVES = 4
MANY = 4
FEW = 2


def neighbour(offset, sign):
    where = []
    for axis, step in zip(("gx", "gy", "gz"), offset):
        count = lax.axis_size(axis)
        where.append(lax.rem(lax.axis_index(axis) + sign * step + count, count))
    return tuple(where)


def meet(offsets, sign):
    barrier = pltpu.get_barrier_semaphore()
    for offset in offsets:
        pl.semaphore_signal(barrier, inc=1, device_id=neighbour(offset, sign), device_id_type=MESH_IDS)
    return barrier


def move(sources, targets, sems):
    copies = [pltpu.make_async_copy(s, t, sems.at[k]) for k, (s, t) in enumerate(zip(sources, targets))]
    for copy in copies:
        copy.start()
    return copies


def finish(copies):
    for copy in copies:
        copy.wait()


def one_hot(row, count):
    levels = lax.broadcasted_iota(jnp.int16, (count, row.shape[1]), 0)
    return jnp.where(levels == row.astype(jnp.int16), jnp.ones((), BF16), jnp.zeros((), BF16))


def split_two(value):
    high = value.astype(BF16).astype(F32)
    return high, value - high


def take_lanes(table, index):
    return jnp.take_along_axis(table, index, axis=1, mode="promise_in_bounds")


def pick(tab, n, c, low, high):
    value = take_lanes(tab[c * n], low)
    for ch in range(1, n):
        value = jnp.where(high == ch, take_lanes(tab[c * n + ch], low), value)
    return value


def geometry(low_i, high_i, low_j, high_j, own_tab, tab, chunks, n):
    gap = [pick(tab, n, c, low_j, high_j) - pick(own_tab, chunks, c, low_i, high_i) for c in range(3)]
    return gap, gap[0] * gap[0] + gap[1] * gap[1] + gap[2] * gap[2]


def spread(row, tab, first):
    for ch in range(row.shape[1] // 128):
        tab[first + ch] = jnp.broadcast_to(row[:, 128 * ch:128 * ch + 128], (8, 128))


def compact(own_list, par_list, mask_list, own_tab, tab, chunks, n, words, live, ranks, packed):
    rows = own_list.shape[0]
    lane = lax.broadcasted_iota(I32, (8, 128), 1)

    def find(v, carry):
        at = pl.ds(pl.multiple_of(8 * v, 8), 8)
        own, partner = own_list[at, :], par_list[at, :]
        gap, squared = geometry(own & 127, own >> 7, partner & 127, partner >> 7, own_tab, tab, chunks, n)
        alive = jnp.logical_and(mask_list[at, :] > 0, squared < 1.0)
        live[at, :] = jnp.where(alive, 1.0, 0.0)
        words[at, :] = jnp.where(alive, (own << 8) + (partner << 17) + LIVE, 0)
        return carry
    lax.fori_loop(0, rows // 8, find, 0, unroll=True)
    above = jnp.where(lax.broadcasted_iota(I32, (128, 128), 0) < lax.broadcasted_iota(I32, (128, 128), 1), 1.0, 0.0)
    adder = jnp.concatenate([above, jnp.ones((128, 128), F32)], 1).astype(BF16)
    ranks[0:rows, :] = jnp.dot(live[0:rows, :].astype(BF16), adder, preferred_element_type=F32)

    tiles = rows // 8
    stand = jnp.zeros((8, 128), I32)
    slots = [jnp.zeros((8, 128), I32) for _ in range(tiles)]
    for v in range(tiles):
        at = slice(8 * v, 8 * v + 8)
        word = words[at, :]
        rank = ranks[at, 0:128].astype(I32)
        number = ranks[at, 128:256].astype(I32)
        word = jnp.where(word > 0, word + (lane - rank), 0)
        for bit in range(7):
            moved = pltpu.roll(word, 128 - (1 << bit), 1)
            stay = jnp.where((word & (1 << bit)) > 0, 0, word)
            word = jnp.where((moved & (1 << bit)) > 0, moved, stay)
        turn = (lane - stand) & 127
        word = take_lanes(word, turn)
        row = jnp.where(turn < number, (stand + turn) >> 7, -1)
        for t in range(v + 1):
            slots[t] = jnp.where(row == t, word, slots[t])
        stand = stand + number
    for t in range(tiles):
        packed[8 * t:8 * t + 8, :] = slots[t]
    return stand


def weights(radial, mid, last, out, w_mids, w_lasts, w_radials):
    nb, channels = radial.shape
    high, low = split_two(radial[...] * 0.5)
    spot = lax.broadcasted_iota(I32, (nb, 4 * nb), 1)
    term = lax.broadcasted_iota(I32, (nb, 4 * nb), 0)
    place_high = jnp.where((spot == term) | (spot == term + nb), 1.0, 0.0).astype(BF16)
    place_low = jnp.where(spot == term + 2 * nb, 1.0, 0.0).astype(BF16)
    w_radial = (lax.dot_general(high.astype(BF16), place_high, TN, preferred_element_type=F32)
                + lax.dot_general(low.astype(BF16), place_low, TN, preferred_element_type=F32)).astype(BF16)
    w_mid = (mid[...].astype(F32) * 0.5).astype(BF16)
    w_last = (last[...].astype(F32) * 0.5).astype(BF16)
    for store, w in ((w_mids, w_mid), (w_lasts, w_last), (w_radials, w_radial)):
        for half in range(HALVES):
            store[channels * half:channels * half + channels, :] = jnp.concatenate(
                [w if other == half else jnp.zeros_like(w) for other in range(HALVES)], 1)
    eye = lax.broadcasted_iota(I32, (channels, channels), 0) == lax.broadcasted_iota(I32, (channels, channels), 1)
    return jnp.sum(jnp.where(eye, jnp.broadcast_to(out[...], (channels, channels)), 0.0), 1, keepdims=True)


def activate(y, tangent):
    up = 1.0 + jnp.tanh(y)
    value = y * up
    return value, (up + value * (2.0 - up)) * tangent


def pair_step(packed, own_tab, tab, chunks, n, left_tab, right_tab, w_mids, w_lasts, w_radials, w_out,
              hot_own, hot_par, quant, acc_own, acc_par, width):
    nb = 8
    centers = lax.broadcasted_iota(I32, (nb, 128), 0).astype(F32) / (nb - 1)
    zero = jnp.zeros((), BF16)

    def stages(t, u):
        word = packed[pl.ds(pl.multiple_of(8 * t, 8), 8), :]
        own, partner = (word >> 8) & 511, word >> 17
        low_i, high_i, low_j, high_j = own & 127, own >> 7, partner & 127, partner >> 7
        wide = lambda x, half: jnp.concatenate([x[2 * half:2 * half + 1], x[2 * half + 1:2 * half + 2]], 1)

        def gather(low, high, keep, table, groups, half):
            hot = one_hot(wide(low, half), 128)
            keep[u, :, 256 * half:256 * half + 256] = hot
            top = wide(high, half)
            odd = jnp.broadcast_to((top & 1).astype(jnp.int16), (128, 256))
            hot = jnp.concatenate([jnp.where(odd == jnp.int16(0), hot, zero), jnp.where(odd == jnp.int16(1), hot, zero)], 0)
            found = jnp.dot(table[...], hot, preferred_element_type=F32)
            group = top >> 1
            value = found[0:64]
            for g in range(1, groups):
                value = jnp.where(group == g, found[64 * g:64 * g + 64], value)
            return value

        gathered = [gather(low_i, high_i, hot_own, left_tab, chunks // 2, half)
                    + gather(low_j, high_j, hot_par, right_tab, n // 2, half) for half in range(HALVES)]
        yield
        gap, squared = geometry(low_i, high_i, low_j, high_j, own_tab, tab, chunks, n)
        weight = jnp.where((word & LIVE) > 0, pick(own_tab, chunks, 3, low_i, high_i) * pick(tab, n, 3, low_j, high_j), 0.0)
        radials = []
        for half in range(HALVES):
            tiles, slants = [], []
            for r in (2 * half, 2 * half + 1):
                off = squared[r:r + 1] - centers
                basis = jnp.exp(-WIDTH * off * off)
                tiles.append(basis)
                slants.append((-2.0 * WIDTH) * off * basis)
            high, low = split_two(jnp.concatenate(tiles + slants, 1))
            radials += [high, low, high, jnp.zeros_like(low)]
        radials = jnp.dot(w_radials[...], jnp.concatenate(radials, 0).astype(BF16), preferred_element_type=F32)
        yield
        quarter = lambda x, half: x[64 * half:64 * half + 64]
        now = [activate(g + quarter(radials, half)[:, 0:256], quarter(radials, half)[:, 256:512]) for half, g in enumerate(gathered)]
        for w in (w_mids, w_lasts):
            stack = jnp.concatenate([jnp.concatenate(pair, 1).astype(BF16) for pair in now], 0)
            mixed = jnp.dot(w[...], stack, preferred_element_type=F32)
            yield
            now = [activate(quarter(mixed, half)[:, 0:256], quarter(mixed, half)[:, 256:512]) for half in range(HALVES)]
        reads = [jnp.sum(value * w_out, 0, keepdims=True) for value, _ in now]
        slopes = [jnp.sum(slope * w_out, 0, keepdims=True) for _, slope in now]
        yield
        tall = lambda xs: jnp.concatenate([x[:, 128 * k:128 * k + 128] for x in xs for k in range(2)], 0)
        readout, reslope = tall(reads), tall(slopes)
        near = jnp.maximum(1.0 - squared, 0.0)
        envelope = near * near
        energy = weight * envelope * readout
        slope = weight * (envelope * reslope - 2.0 * near * readout)
        outs = [2.0 * g * slope for g in gap] + [energy]
        for q, out in enumerate(outs):
            high, low = split_two(out)
            quant[u, 8 * q:8 * q + 8, :] = high
            quant[u, 32 + 8 * q:40 + 8 * q, :] = low
        a_own, a_par = [], []
        for r in range(8):
            tile = quant[u, pl.ds(r, 8, stride=8), :]
            a_own.append(jnp.concatenate([jnp.where(high_i[r:r + 1] == ch, tile, 0.0) for ch in range(chunks)], 0))
            a_par.append(jnp.concatenate([jnp.where(high_j[r:r + 1] == ch, tile, 0.0) for ch in range(n)], 0))
        acc_own[...] += lax.dot_general(jnp.concatenate(a_own, 1).astype(BF16), hot_own[u], NT, preferred_element_type=F32)
        acc_par[...] += lax.dot_general(jnp.concatenate(a_par, 1).astype(BF16), hot_par[u], NT, preferred_element_type=F32)

    def step(t, carry):
        streams = [stages(width * t + u, u) for u in range(width)]
        while streams:
            streams = [stream for stream in streams if next(stream, True) is None]
        return carry
    return step


def trips(stand):
    return (jnp.max(stand) + 128 * FEW - 1) // (128 * FEW)


def offer_kernel(pos_hbm, feat_hbm, species_hbm, scale_hbm, first_hbm, second_hbm, send_hbm,
                 one_hbm, two_hbm, mask_hbm, radial_hbm, mid_hbm, last_hbm, out_hbm,
                 own_out, left_out, right_out, ghost_out, packed_out, stand_out, acc_own_out, acc_loc_out,
                 pos, feat, species, scale, first, second, send, one, two, mask, radial, mid, last, out,
                 offered, own, left_tab, right_tab, packed, stand, acc_own, acc_loc,
                 own_tab, words, live, ranks, hot_own, hot_par, quant, w_mids, w_lasts, w_radials,
                 in_sem, out_sem, last_sem, send_sem, recv_sem):
    paths = [OFFSETS[k] for k in DIRECT]
    barrier = meet(paths, 1)
    loads = move((pos_hbm, feat_hbm, species_hbm, scale_hbm, first_hbm, second_hbm, send_hbm,
                  one_hbm, two_hbm, mask_hbm, radial_hbm, mid_hbm, last_hbm, out_hbm),
                 (pos, feat, species, scale, first, second, send, one, two, mask, radial, mid, last, out), in_sem)
    finish(loads[0:7])
    count = pos.shape[1]
    chunks = count // 128
    where = pos[...]
    kinds = species[...]
    scales = scale[...].astype(F32)
    gain = jnp.zeros(kinds.shape, F32)
    for kind in range(scales.shape[1]):
        gain = jnp.where(kinds == kind, scales[:, kind:kind + 1], gain)
    right = (jnp.dot(second[...], feat[...], preferred_element_type=F32).astype(BF16).astype(F32) * 0.5).astype(BF16)
    high = where.astype(BF16).astype(F32)
    tail = jnp.concatenate([high, where - high, gain, jnp.zeros((9, count), F32)], 0).astype(BF16)
    payload = jnp.concatenate([right, tail], 0)
    offered[...] = jnp.dot(payload, one_hot(send[...], count), preferred_element_type=F32).astype(BF16)[0:ROWS]
    pl.semaphore_wait(barrier, len(paths))

    def remote(source, k, offset):
        copy = pltpu.make_async_remote_copy(
            src_ref=source, dst_ref=ghost_out.at[k], send_sem=send_sem.at[k], recv_sem=recv_sem.at[k],
            device_id=neighbour(offset, -1), device_id_type=MESH_IDS)
        copy.start()
        return copy
    copies = [remote(offered, k, OFFSETS[k]) for k in DIRECT]

    own[0:3, :] = where
    own[3:4, :] = gain
    own[4:8, :] = jnp.zeros((4, count), F32)
    left = (jnp.dot(first[...], feat[...], preferred_element_type=F32).astype(BF16).astype(F32) * 0.5).astype(BF16)
    for g in range(count // 256):
        left_tab[64 * g:64 * g + 64, :] = left[:, 256 * g:256 * g + 256]
        right_tab[64 * g:64 * g + 64, :] = right[:, 256 * g:256 * g + 256]
    for c in range(4):
        spread(own[c:c + 1, :], own_tab, c * chunks)
    finish(loads[7:])
    w_out = weights(radial, mid, last, out, w_mids, w_lasts, w_radials)
    copies[0].wait_recv()
    relays = [remote(ghost_out.at[2], k, OFFSETS[step]) for step, k in RELAYED]
    stand[...] = compact(one, two, mask, own_tab, own_tab, chunks, chunks, words, live, ranks, packed)
    acc_own[...] = jnp.zeros_like(acc_own)
    acc_loc[...] = jnp.zeros_like(acc_loc)
    step = pair_step(packed, own_tab, own_tab, chunks, chunks, left_tab, right_tab, w_mids, w_lasts, w_radials, w_out,
                     hot_own, hot_par, quant, acc_own, acc_loc, MANY)
    stores = move((own, left_tab, right_tab, packed, stand), (own_out, left_out, right_out, packed_out, stand_out), out_sem)
    lax.fori_loop(0, EARLY // MANY, step, 0)
    stores += move((acc_own, acc_loc), (acc_own_out, acc_loc_out), last_sem)
    copies[0].wait_send()
    finish(copies[1:])
    finish(relays)
    finish(stores)


def pairs_kernel(own_hbm, left_hbm, right_hbm, ghost_hbm, packed_hbm, stand_hbm, acc_own_hbm, acc_loc_hbm,
                 one_hbm, two_hbm, mask_hbm, radial_hbm, mid_hbm, last_hbm, out_hbm,
                 acc_own_out, acc_loc_out, force_out,
                 own, left_tab, right_tab, ghost, packed, stand, acc_own, acc_loc, one, two, mask, radial, mid, last, out,
                 own_tab, ghost_tab, gtable, gpacked, words, live, ranks, hot_own, hot_par, quant, acc_gho, force,
                 w_mids, w_lasts, w_radials, in_sem, out_sem, last_sem):
    loads = move((own_hbm, ghost_hbm, one_hbm, two_hbm, mask_hbm, left_hbm, right_hbm, packed_hbm, stand_hbm,
                  acc_own_hbm, acc_loc_hbm, radial_hbm, mid_hbm, last_hbm, out_hbm),
                 (own, ghost, one, two, mask, left_tab, right_tab, packed, stand,
                  acc_own, acc_loc, radial, mid, last, out), in_sem)
    finish(loads[0:5])
    count = own.shape[1]
    chunks = count // 128
    sends = ghost.shape[2]
    per = sends // 128
    gchunks = len(OFFSETS) * per
    for c in range(4):
        spread(own[c:c + 1, :], own_tab, c * chunks)
    for k, offset in enumerate(OFFSETS):
        gtable[64 * k:64 * k + 64, :] = ghost[k, 0:64, :]
        tail = ghost[k, 64:72, :].astype(F32)
        for c in range(4):
            row = tail[c:c + 1] + tail[c + 3:c + 4] + float(offset[c]) if c < 3 else tail[6:7]
            spread(row, ghost_tab, c * gchunks + k * per)
    finish(loads[5:])
    w_out = weights(radial, mid, last, out, w_mids, w_lasts, w_radials)
    gstand = compact(one, two, mask, own_tab, ghost_tab, chunks, gchunks, words, live, ranks, gpacked)
    acc_gho[...] = jnp.zeros_like(acc_gho)
    gstep = pair_step(gpacked, own_tab, ghost_tab, chunks, gchunks, left_tab, gtable, w_mids, w_lasts, w_radials, w_out,
                      hot_own, hot_par, quant, acc_own, acc_gho, FEW)
    lax.fori_loop(0, trips(gstand), gstep, 0)
    for ch in range(gchunks):
        cols = slice(128 * (ch % per), 128 * (ch % per) + 128)
        force[ch // per, 0:4, cols] = acc_gho[8 * ch:8 * ch + 4, :] + acc_gho[8 * ch + 4:8 * ch + 8, :]
        force[ch // per, 4:8, cols] = jnp.zeros((4, 128), F32)
    step = pair_step(packed, own_tab, own_tab, chunks, chunks, left_tab, right_tab, w_mids, w_lasts, w_radials, w_out,
                     hot_own, hot_par, quant, acc_own, acc_loc, FEW)
    stores = move((force,), (force_out,), out_sem)
    lax.fori_loop((EARLY + LATE) // FEW, trips(stand[...]), step, 0)
    finish(stores + move((acc_own, acc_loc), (acc_own_out, acc_loc_out), last_sem))


def home_kernel(own_hbm, left_hbm, right_hbm, packed_hbm, acc_own_hbm, acc_loc_hbm, force_hbm, send_hbm,
                radial_hbm, mid_hbm, last_hbm, out_hbm,
                result_out,
                own, left_tab, right_tab, packed, acc_own, acc_loc, send, radial, mid, last, out,
                arrived, own_tab, hot_own, hot_par, quant, w_mids, w_lasts, w_radials, result,
                in_sem, out_sem, send_sem, recv_sem):
    barrier = meet(OFFSETS, -1)
    loads = move((own_hbm, left_hbm, right_hbm, packed_hbm, acc_own_hbm, acc_loc_hbm, send_hbm,
                  radial_hbm, mid_hbm, last_hbm, out_hbm),
                 (own, left_tab, right_tab, packed, acc_own, acc_loc, send, radial, mid, last, out), in_sem)
    pl.semaphore_wait(barrier, len(OFFSETS))
    copies = []
    for k, offset in enumerate(OFFSETS):
        copy = pltpu.make_async_remote_copy(
            src_ref=force_hbm.at[k], dst_ref=arrived.at[k], send_sem=send_sem.at[k], recv_sem=recv_sem.at[k],
            device_id=neighbour(offset, 1), device_id_type=MESH_IDS)
        copy.start()
        copies.append(copy)
    finish(loads)
    count = own.shape[1]
    chunks = count // 128
    for c in range(4):
        spread(own[c:c + 1, :], own_tab, c * chunks)
    w_out = weights(radial, mid, last, out, w_mids, w_lasts, w_radials)
    step = pair_step(packed, own_tab, own_tab, chunks, chunks, left_tab, right_tab, w_mids, w_lasts, w_radials, w_out,
                     hot_own, hot_par, quant, acc_own, acc_loc, MANY)
    lax.fori_loop(EARLY // MANY, (EARLY + LATE) // MANY, step, 0)
    hot = one_hot(send[...], count)
    finish(copies)
    total = arrived[0]
    for k in range(1, len(OFFSETS)):
        total = total + arrived[k]
    high, rest = split_two(total)
    mid_part, low = split_two(rest)
    parts = jnp.concatenate([high, mid_part, low, jnp.zeros_like(low)], 0).astype(BF16)
    back = lax.dot_general(parts, hot, NT, preferred_element_type=F32)
    back = back[0:8] + back[8:16] + back[16:24]
    for ch in range(chunks):
        cols = slice(128 * ch, 128 * ch + 128)
        mine = acc_own[8 * ch:8 * ch + 4, :] + acc_own[8 * ch + 4:8 * ch + 8, :]
        other = acc_loc[8 * ch:8 * ch + 4, :] + acc_loc[8 * ch + 4:8 * ch + 8, :]
        result[0:3, cols] = mine[0:3] - other[0:3] - back[0:3, cols]
        result[3:4, cols] = mine[3:4]
    finish(move((result,), (result_out,), out_sem))


def on_device(positions, features, species, species_scale, w_first, w_second, w_radial, w_mid, w_last, w_out,
              ghost_send, local_first, local_second, local_mask, ghost_owner, ghost_index, ghost_mask):
    v, shape = pltpu.VMEM, jax.ShapeDtypeStruct
    count = positions.shape[1]
    sends = ghost_send.shape[0]
    channels, nb = w_radial.shape
    blocks = len(OFFSETS)
    chunks, gchunks = count // 128, blocks * sends // 128
    lrows, grows = local_first.shape[0] // 128, ghost_owner.shape[0] // 128
    buffers = lambda arrays: [v(x.shape, x.dtype) for x in arrays]
    sems = lambda number: pltpu.SemaphoreType.DMA((number,))
    send_row = ghost_send.reshape(1, sends)
    net = [w_radial.T, w_mid, w_last, w_out.reshape(1, channels)]
    local = [x.reshape(lrows, 128) for x in (local_first, local_second, local_mask)]
    ghostly = [x.reshape(grows, 128) for x in (ghost_owner, ghost_index, ghost_mask)]
    blocks_w = [v((4 * channels, 4 * channels), BF16), v((4 * channels, 4 * channels), BF16), v((4 * channels, 16 * nb), BF16)]
    hots = lambda width: [v((width, 128, 1024), BF16), v((width, 128, 1024), BF16), v((width, 64, 128), F32)]
    table = shape((channels * count // 256, 256), BF16)
    acc = shape((8 * chunks, 128), F32)
    own_tab = v((4 * chunks, 8, 128), F32)

    args = [positions, features, species.reshape(1, count), species_scale.reshape(1, -1), w_first, w_second, send_row] + local + net
    made = [shape((8, count), F32), table, table, shape((blocks, ROWS, sends), BF16),
            shape((lrows, 128), I32), shape((8, 128), I32), acc, acc]
    own, left_tab, right_tab, ghosts, packed, stand, acc_own, acc_loc = pl.pallas_call(
        offer_kernel,
        name="offer",
        out_shape=made,
        in_specs=[HBM] * len(args),
        out_specs=[HBM] * len(made),
        scratch_shapes=buffers(args) + [v((ROWS, sends), BF16)] + buffers(made[0:3] + made[4:]) + [
            own_tab, v((lrows, 128), I32), v((lrows, 128), F32), v((lrows, 256), F32)] + hots(MANY) + blocks_w + [
            sems(len(args)), sems(5), sems(2), sems(blocks), sems(blocks)],
        compiler_params=pltpu.CompilerParams(collective_id=0, has_side_effects=True, vmem_limit_bytes=60 << 20),
    )(*args)

    args = [own, left_tab, right_tab, ghosts, packed, stand, acc_own, acc_loc] + ghostly + net
    made = [acc, acc, shape((blocks, 8, sends), F32)]
    acc_own, acc_loc, gforce = pl.pallas_call(
        pairs_kernel,
        name="pairs",
        out_shape=made,
        in_specs=[HBM] * len(args),
        out_specs=[HBM] * len(made),
        scratch_shapes=buffers(args) + [
            own_tab, v((4 * gchunks, 8, 128), F32), v((channels * gchunks // 2, 256), BF16), v((grows, 128), I32),
            v((grows, 128), I32), v((grows, 128), F32), v((grows, 256), F32)] + hots(FEW) + [
            v((8 * gchunks, 128), F32), v((blocks, 8, sends), F32)] + blocks_w + [sems(len(args)), sems(1), sems(2)],
        compiler_params=pltpu.CompilerParams(vmem_limit_bytes=60 << 20),
    )(*args)

    args = [own, left_tab, right_tab, packed, acc_own, acc_loc, gforce, send_row] + net
    made = [shape((4, count), F32)]
    result, = pl.pallas_call(
        home_kernel,
        name="home",
        out_shape=made,
        in_specs=[HBM] * len(args),
        out_specs=[HBM] * len(made),
        scratch_shapes=buffers(args[:6] + args[7:]) + [v((blocks, 8, sends), F32), own_tab] + hots(MANY) + blocks_w + buffers(made) + [
            sems(len(args) - 1), sems(len(made)), sems(blocks), sems(blocks)],
        compiler_params=pltpu.CompilerParams(collective_id=1, has_side_effects=True, vmem_limit_bytes=60 << 20),
    )(*args)
    return result[0:3], result[3]


def solution(mesh):
    everywhere = ("gx", "gy", "gz")
    wide, flat, copied = P(None, everywhere), P(everywhere), P()
    in_specs = (wide, wide, flat) + (copied,) * 7 + (flat,) * 7
    return jax.shard_map(on_device, mesh=mesh, in_specs=in_specs, out_specs=(wide, flat), check_vma=False)
```

```python
import jax
import jax.numpy as jnp
from jax import lax
from jax.experimental import pallas as pl
from jax.experimental.pallas import tpu as pltpu
from jax.sharding import PartitionSpec as P

OFFSETS = ((1, 0, 0), (0, 1, 0), (0, 0, 1), (1, 1, 0), (1, 0, 1), (0, 1, 1), (1, 1, 1))
DIRECT = (2, 0, 1, 3)
RELAYED = ((0, 4), (1, 5), (3, 6))
MESH_IDS = pl.DeviceIdType.MESH
HBM = pl.BlockSpec(memory_space=pltpu.HBM)
NT = (((1,), (1,)), ((), ()))
TN = (((0,), (0,)), ((), ()))
WIDTH = 24.0
F32, BF16, I32 = jnp.float32, jnp.bfloat16, jnp.int32
LIVE = 128
ROWS = 72
EARLY = 8
LATE = 8
HALVES = 4
MANY = 4
FEW = 2


def neighbour(offset, sign):
    where = []
    for axis, step in zip(("gx", "gy", "gz"), offset):
        count = lax.axis_size(axis)
        where.append(lax.rem(lax.axis_index(axis) + sign * step + count, count))
    return tuple(where)


def meet(offsets, sign):
    barrier = pltpu.get_barrier_semaphore()
    for offset in offsets:
        pl.semaphore_signal(barrier, inc=1, device_id=neighbour(offset, sign), device_id_type=MESH_IDS)
    return barrier


def move(sources, targets, sems):
    copies = [pltpu.make_async_copy(s, t, sems.at[k]) for k, (s, t) in enumerate(zip(sources, targets))]
    for copy in copies:
        copy.start()
    return copies


def finish(copies):
    for copy in copies:
        copy.wait()


def one_hot(row, count):
    levels = lax.broadcasted_iota(jnp.int16, (count, row.shape[1]), 0)
    return jnp.where(levels == row.astype(jnp.int16), jnp.ones((), BF16), jnp.zeros((), BF16))


def split_two(value):
    high = value.astype(BF16).astype(F32)
    return high, value - high


def take_lanes(table, index):
    return jnp.take_along_axis(table, index, axis=1, mode="promise_in_bounds")


def pick(tab, n, c, low, high):
    value = take_lanes(tab[c * n], low)
    for ch in range(1, n):
        value = jnp.where(high == ch, take_lanes(tab[c * n + ch], low), value)
    return value


def geometry(low_i, high_i, low_j, high_j, own_tab, tab, chunks, n):
    gap = [pick(tab, n, c, low_j, high_j) - pick(own_tab, chunks, c, low_i, high_i) for c in range(3)]
    return gap, gap[0] * gap[0] + gap[1] * gap[1] + gap[2] * gap[2]


def spread(row, tab, first):
    for ch in range(row.shape[1] // 128):
        tab[first + ch] = jnp.broadcast_to(row[:, 128 * ch:128 * ch + 128], (8, 128))


def compact(own_list, par_list, mask_list, own_tab, tab, chunks, n, words, live, ranks, packed):
    rows = own_list.shape[0]
    lane = lax.broadcasted_iota(I32, (8, 128), 1)

    def find(v, carry):
        at = pl.ds(pl.multiple_of(8 * v, 8), 8)
        own, partner = own_list[at, :], par_list[at, :]
        gap, squared = geometry(own & 127, own >> 7, partner & 127, partner >> 7, own_tab, tab, chunks, n)
        alive = jnp.logical_and(mask_list[at, :] > 0, squared < 1.0)
        live[at, :] = jnp.where(alive, 1.0, 0.0)
        words[at, :] = jnp.where(alive, (own << 8) + (partner << 17) + LIVE, 0)
        return carry
    lax.fori_loop(0, rows // 8, find, 0, unroll=True)
    above = jnp.where(lax.broadcasted_iota(I32, (128, 128), 0) < lax.broadcasted_iota(I32, (128, 128), 1), 1.0, 0.0)
    adder = jnp.concatenate([above, jnp.ones((128, 128), F32)], 1).astype(BF16)
    ranks[0:rows, :] = jnp.dot(live[0:rows, :].astype(BF16), adder, preferred_element_type=F32)

    tiles = rows // 8
    stand = jnp.zeros((8, 128), I32)
    slots = [jnp.zeros((8, 128), I32) for _ in range(tiles)]
    for v in range(tiles):
        at = slice(8 * v, 8 * v + 8)
        word = words[at, :]
        rank = ranks[at, 0:128].astype(I32)
        number = ranks[at, 128:256].astype(I32)
        word = jnp.where(word > 0, word + (lane - rank), 0)
        for bit in range(7):
            moved = pltpu.roll(word, 128 - (1 << bit), 1)
            stay = jnp.where((word & (1 << bit)) > 0, 0, word)
            word = jnp.where((moved & (1 << bit)) > 0, moved, stay)
        turn = (lane - stand) & 127
        word = take_lanes(word, turn)
        row = jnp.where(turn < number, (stand + turn) >> 7, -1)
        for t in range(v + 1):
            slots[t] = jnp.where(row == t, word, slots[t])
        stand = stand + number
    for t in range(tiles):
        packed[8 * t:8 * t + 8, :] = slots[t]
    return stand


def weights(radial, mid, last, out, w_mids, w_lasts, w_radials):
    nb, channels = radial.shape
    high, low = split_two(radial[...] * 0.5)
    spot = lax.broadcasted_iota(I32, (nb, 4 * nb), 1)
    term = lax.broadcasted_iota(I32, (nb, 4 * nb), 0)
    place_high = jnp.where((spot == term) | (spot == term + nb), 1.0, 0.0).astype(BF16)
    place_low = jnp.where(spot == term + 2 * nb, 1.0, 0.0).astype(BF16)
    w_radial = (lax.dot_general(high.astype(BF16), place_high, TN, preferred_element_type=F32)
                + lax.dot_general(low.astype(BF16), place_low, TN, preferred_element_type=F32)).astype(BF16)
    w_mid = (mid[...].astype(F32) * 0.5).astype(BF16)
    w_last = (last[...].astype(F32) * 0.5).astype(BF16)
    for store, w in ((w_mids, w_mid), (w_lasts, w_last), (w_radials, w_radial)):
        for half in range(HALVES):
            store[channels * half:channels * half + channels, :] = jnp.concatenate(
                [w if other == half else jnp.zeros_like(w) for other in range(HALVES)], 1)
    eye = lax.broadcasted_iota(I32, (channels, channels), 0) == lax.broadcasted_iota(I32, (channels, channels), 1)
    return jnp.sum(jnp.where(eye, jnp.broadcast_to(out[...], (channels, channels)), 0.0), 1, keepdims=True)


def activate(y, tangent):
    up = 1.0 + jnp.tanh(y)
    value = y * up
    return value, (up + value * (2.0 - up)) * tangent


def pair_step(packed, own_tab, tab, chunks, n, left_tab, right_tab, w_mids, w_lasts, w_radials, w_out,
              hot_own, hot_par, quant, acc_own, acc_par, width):
    nb = 8
    centers = lax.broadcasted_iota(I32, (nb, 128), 0).astype(F32) / (nb - 1)
    zero = jnp.zeros((), BF16)

    def stages(t, u):
        word = packed[pl.ds(pl.multiple_of(8 * t, 8), 8), :]
        own, partner = (word >> 8) & 511, word >> 17
        low_i, high_i, low_j, high_j = own & 127, own >> 7, partner & 127, partner >> 7
        wide = lambda x, half: jnp.concatenate([x[2 * half:2 * half + 1], x[2 * half + 1:2 * half + 2]], 1)

        def gather(low, high, keep, table, groups, half):
            hot = one_hot(wide(low, half), 128)
            keep[u, :, 256 * half:256 * half + 256] = hot[0:64] + hot[64:128]
            top = wide(high, half)
            odd = jnp.broadcast_to((top & 1).astype(jnp.int16), (128, 256))
            hot = jnp.concatenate([jnp.where(odd == jnp.int16(0), hot, zero), jnp.where(odd == jnp.int16(1), hot, zero)], 0)
            found = jnp.dot(table[...], hot, preferred_element_type=F32)
            group = top >> 1
            value = found[0:64]
            for g in range(1, groups):
                value = jnp.where(group == g, found[64 * g:64 * g + 64], value)
            return value

        gathered = [gather(low_i, high_i, hot_own, left_tab, chunks // 2, half)
                    + gather(low_j, high_j, hot_par, right_tab, n // 2, half) for half in range(HALVES)]
        yield
        gap, squared = geometry(low_i, high_i, low_j, high_j, own_tab, tab, chunks, n)
        weight = jnp.where((word & LIVE) > 0, pick(own_tab, chunks, 3, low_i, high_i) * pick(tab, n, 3, low_j, high_j), 0.0)
        radials = []
        for half in range(HALVES):
            tiles, slants = [], []
            for r in (2 * half, 2 * half + 1):
                off = squared[r:r + 1] - centers
                basis = jnp.exp(-WIDTH * off * off)
                tiles.append(basis)
                slants.append((-2.0 * WIDTH) * off * basis)
            high, low = split_two(jnp.concatenate(tiles + slants, 1))
            radials += [high, low, high, jnp.zeros_like(low)]
        radials = jnp.dot(w_radials[...], jnp.concatenate(radials, 0).astype(BF16), preferred_element_type=F32)
        yield
        quarter = lambda x, half: x[64 * half:64 * half + 64]
        now = [activate(g + quarter(radials, half)[:, 0:256], quarter(radials, half)[:, 256:512]) for half, g in enumerate(gathered)]
        for w in (w_mids, w_lasts):
            stack = jnp.concatenate([jnp.concatenate(pair, 1).astype(BF16) for pair in now], 0)
            mixed = jnp.dot(w[...], stack, preferred_element_type=F32)
            yield
            now = [activate(quarter(mixed, half)[:, 0:256], quarter(mixed, half)[:, 256:512]) for half in range(HALVES)]
        reads = [jnp.sum(value * w_out, 0, keepdims=True) for value, _ in now]
        slopes = [jnp.sum(slope * w_out, 0, keepdims=True) for _, slope in now]
        yield
        tall = lambda xs: jnp.concatenate([x[:, 128 * k:128 * k + 128] for x in xs for k in range(2)], 0)
        readout, reslope = tall(reads), tall(slopes)
        near = jnp.maximum(1.0 - squared, 0.0)
        envelope = near * near
        energy = weight * envelope * readout
        slope = weight * (envelope * reslope - 2.0 * near * readout)
        outs = [2.0 * g * slope for g in gap] + [energy]
        for q, out in enumerate(outs):
            high, low = split_two(out)
            quant[u, 8 * q:8 * q + 8, :] = high
            quant[u, 32 + 8 * q:40 + 8 * q, :] = low
        a_own, a_par = [], []
        part_i, part_j = own >> 6, partner >> 6
        for r in range(8):
            tile = quant[u, pl.ds(r, 8, stride=8), :]
            a_own.append(jnp.concatenate([jnp.where(part_i[r:r + 1] == ch, tile, 0.0) for ch in range(2 * chunks)], 0))
            a_par.append(jnp.concatenate([jnp.where(part_j[r:r + 1] == ch, tile, 0.0) for ch in range(2 * n)], 0))
        acc_own[...] += lax.dot_general(jnp.concatenate(a_own, 1).astype(BF16), hot_own[u], NT, preferred_element_type=F32)
        acc_par[...] += lax.dot_general(jnp.concatenate(a_par, 1).astype(BF16), hot_par[u], NT, preferred_element_type=F32)

    def step(t, carry):
        streams = [stages(width * t + u, u) for u in range(width)]
        while streams:
            streams = [stream for stream in streams if next(stream, True) is None]
        return carry
    return step


def joined(acc, ch):
    return jnp.concatenate([acc[8 * k:8 * k + 4, :] + acc[8 * k + 4:8 * k + 8, :] for k in (2 * ch, 2 * ch + 1)], 1)


def trips(stand):
    return (jnp.max(stand) + 128 * FEW - 1) // (128 * FEW)


def offer_kernel(pos_hbm, feat_hbm, species_hbm, scale_hbm, first_hbm, second_hbm, send_hbm,
                 one_hbm, two_hbm, mask_hbm, radial_hbm, mid_hbm, last_hbm, out_hbm,
                 own_out, left_out, right_out, ghost_out, packed_out, stand_out, acc_own_out, acc_loc_out,
                 pos, feat, species, scale, first, second, send, one, two, mask, radial, mid, last, out,
                 offered, own, left_tab, right_tab, packed, stand, acc_own, acc_loc,
                 own_tab, words, live, ranks, hot_own, hot_par, quant, w_mids, w_lasts, w_radials,
                 in_sem, out_sem, last_sem, send_sem, recv_sem):
    paths = [OFFSETS[k] for k in DIRECT]
    barrier = meet(paths, 1)
    loads = move((pos_hbm, feat_hbm, species_hbm, scale_hbm, first_hbm, second_hbm, send_hbm,
                  one_hbm, two_hbm, mask_hbm, radial_hbm, mid_hbm, last_hbm, out_hbm),
                 (pos, feat, species, scale, first, second, send, one, two, mask, radial, mid, last, out), in_sem)
    finish(loads[0:7])
    count = pos.shape[1]
    chunks = count // 128
    where = pos[...]
    kinds = species[...]
    scales = scale[...].astype(F32)
    gain = jnp.zeros(kinds.shape, F32)
    for kind in range(scales.shape[1]):
        gain = jnp.where(kinds == kind, scales[:, kind:kind + 1], gain)
    right = (jnp.dot(second[...], feat[...], preferred_element_type=F32).astype(BF16).astype(F32) * 0.5).astype(BF16)
    high = where.astype(BF16).astype(F32)
    tail = jnp.concatenate([high, where - high, gain, jnp.zeros((9, count), F32)], 0).astype(BF16)
    payload = jnp.concatenate([right, tail], 0)
    offered[...] = jnp.dot(payload, one_hot(send[...], count), preferred_element_type=F32).astype(BF16)[0:ROWS]
    pl.semaphore_wait(barrier, len(paths))

    def remote(source, k, offset):
        copy = pltpu.make_async_remote_copy(
            src_ref=source, dst_ref=ghost_out.at[k], send_sem=send_sem.at[k], recv_sem=recv_sem.at[k],
            device_id=neighbour(offset, -1), device_id_type=MESH_IDS)
        copy.start()
        return copy
    copies = [remote(offered, k, OFFSETS[k]) for k in DIRECT]

    own[0:3, :] = where
    own[3:4, :] = gain
    own[4:8, :] = jnp.zeros((4, count), F32)
    left = (jnp.dot(first[...], feat[...], preferred_element_type=F32).astype(BF16).astype(F32) * 0.5).astype(BF16)
    for g in range(count // 256):
        left_tab[64 * g:64 * g + 64, :] = left[:, 256 * g:256 * g + 256]
        right_tab[64 * g:64 * g + 64, :] = right[:, 256 * g:256 * g + 256]
    for c in range(4):
        spread(own[c:c + 1, :], own_tab, c * chunks)
    finish(loads[7:])
    w_out = weights(radial, mid, last, out, w_mids, w_lasts, w_radials)
    stand[...] = compact(one, two, mask, own_tab, own_tab, chunks, chunks, words, live, ranks, packed)
    copies[0].wait_recv()
    relays = [remote(ghost_out.at[2], k, OFFSETS[step]) for step, k in RELAYED]
    acc_own[...] = jnp.zeros_like(acc_own)
    acc_loc[...] = jnp.zeros_like(acc_loc)
    step = pair_step(packed, own_tab, own_tab, chunks, chunks, left_tab, right_tab, w_mids, w_lasts, w_radials, w_out,
                     hot_own, hot_par, quant, acc_own, acc_loc, MANY)
    stores = move((own, left_tab, right_tab, packed, stand), (own_out, left_out, right_out, packed_out, stand_out), out_sem)
    lax.fori_loop(0, EARLY // MANY, step, 0)
    stores += move((acc_own, acc_loc), (acc_own_out, acc_loc_out), last_sem)
    copies[0].wait_send()
    finish(copies[1:])
    finish(relays)
    finish(stores)


def pairs_kernel(own_hbm, left_hbm, right_hbm, ghost_hbm, packed_hbm, stand_hbm, acc_own_hbm, acc_loc_hbm,
                 one_hbm, two_hbm, mask_hbm, radial_hbm, mid_hbm, last_hbm, out_hbm,
                 acc_own_out, acc_loc_out, force_out,
                 own, left_tab, right_tab, ghost, packed, stand, acc_own, acc_loc, one, two, mask, radial, mid, last, out,
                 own_tab, ghost_tab, gtable, gpacked, words, live, ranks, hot_own, hot_par, quant, acc_gho, force,
                 w_mids, w_lasts, w_radials, in_sem, out_sem, last_sem):
    loads = move((own_hbm, ghost_hbm, one_hbm, two_hbm, mask_hbm, left_hbm, right_hbm, packed_hbm, stand_hbm,
                  acc_own_hbm, acc_loc_hbm, radial_hbm, mid_hbm, last_hbm, out_hbm),
                 (own, ghost, one, two, mask, left_tab, right_tab, packed, stand,
                  acc_own, acc_loc, radial, mid, last, out), in_sem)
    finish(loads[0:5])
    count = own.shape[1]
    chunks = count // 128
    sends = ghost.shape[2]
    per = sends // 128
    gchunks = len(OFFSETS) * per
    for c in range(4):
        spread(own[c:c + 1, :], own_tab, c * chunks)
    for k, offset in enumerate(OFFSETS):
        gtable[64 * k:64 * k + 64, :] = ghost[k, 0:64, :]
        tail = ghost[k, 64:72, :].astype(F32)
        for c in range(4):
            row = tail[c:c + 1] + tail[c + 3:c + 4] + float(offset[c]) if c < 3 else tail[6:7]
            spread(row, ghost_tab, c * gchunks + k * per)
    finish(loads[5:])
    w_out = weights(radial, mid, last, out, w_mids, w_lasts, w_radials)
    gstand = compact(one, two, mask, own_tab, ghost_tab, chunks, gchunks, words, live, ranks, gpacked)
    acc_gho[...] = jnp.zeros_like(acc_gho)
    gstep = pair_step(gpacked, own_tab, ghost_tab, chunks, gchunks, left_tab, gtable, w_mids, w_lasts, w_radials, w_out,
                      hot_own, hot_par, quant, acc_own, acc_gho, FEW)
    lax.fori_loop(0, trips(gstand), gstep, 0)
    for ch in range(gchunks):
        cols = slice(128 * (ch % per), 128 * (ch % per) + 128)
        force[ch // per, 0:4, cols] = joined(acc_gho, ch)
        force[ch // per, 4:8, cols] = jnp.zeros((4, 128), F32)
    step = pair_step(packed, own_tab, own_tab, chunks, chunks, left_tab, right_tab, w_mids, w_lasts, w_radials, w_out,
                     hot_own, hot_par, quant, acc_own, acc_loc, FEW)
    stores = move((force,), (force_out,), out_sem)
    lax.fori_loop((EARLY + LATE) // FEW, trips(stand[...]), step, 0)
    finish(stores + move((acc_own, acc_loc), (acc_own_out, acc_loc_out), last_sem))


def home_kernel(own_hbm, left_hbm, right_hbm, packed_hbm, acc_own_hbm, acc_loc_hbm, force_hbm,
                radial_hbm, mid_hbm, last_hbm, out_hbm,
                acc_own_out, acc_loc_out, arrived_out,
                own, left_tab, right_tab, packed, acc_own, acc_loc, radial, mid, last, out,
                own_tab, hot_own, hot_par, quant, w_mids, w_lasts, w_radials,
                in_sem, out_sem, send_sem, recv_sem):
    barrier = meet(OFFSETS, -1)
    finish(move((own_hbm, left_hbm, right_hbm, packed_hbm, acc_own_hbm, acc_loc_hbm, radial_hbm, mid_hbm, last_hbm, out_hbm),
                (own, left_tab, right_tab, packed, acc_own, acc_loc, radial, mid, last, out), in_sem))
    pl.semaphore_wait(barrier, len(OFFSETS))
    copies = []
    for k, offset in enumerate(OFFSETS):
        copy = pltpu.make_async_remote_copy(
            src_ref=force_hbm.at[k], dst_ref=arrived_out.at[k], send_sem=send_sem.at[k], recv_sem=recv_sem.at[k],
            device_id=neighbour(offset, 1), device_id_type=MESH_IDS)
        copy.start()
        copies.append(copy)
    chunks = own.shape[1] // 128
    for c in range(4):
        spread(own[c:c + 1, :], own_tab, c * chunks)
    w_out = weights(radial, mid, last, out, w_mids, w_lasts, w_radials)
    step = pair_step(packed, own_tab, own_tab, chunks, chunks, left_tab, right_tab, w_mids, w_lasts, w_radials, w_out,
                     hot_own, hot_par, quant, acc_own, acc_loc, MANY)
    lax.fori_loop(EARLY // MANY, (EARLY + LATE) // MANY, step, 0)
    stores = move((acc_own, acc_loc), (acc_own_out, acc_loc_out), out_sem)
    finish(copies)
    finish(stores)


def join_kernel(acc_own_hbm, acc_loc_hbm, arrived_hbm, send_hbm, force_out, energy_out,
                acc_own, acc_loc, arrived, send, result, energy, in_sem, out_sem):
    finish(move((acc_own_hbm, acc_loc_hbm, arrived_hbm, send_hbm), (acc_own, acc_loc, arrived, send), in_sem))
    count = result.shape[1]
    hot = one_hot(send[...], count)
    total = arrived[0]
    for k in range(1, len(OFFSETS)):
        total = total + arrived[k]
    high, rest = split_two(total)
    mid_part, low = split_two(rest)
    parts = jnp.concatenate([high, mid_part, low, jnp.zeros_like(low)], 0).astype(BF16)
    back = lax.dot_general(parts, hot, NT, preferred_element_type=F32)
    back = back[0:8] + back[8:16] + back[16:24]
    for ch in range(count // 128):
        cols = slice(128 * ch, 128 * ch + 128)
        mine = joined(acc_own, ch)
        result[:, cols] = mine[0:3] - joined(acc_loc, ch)[0:3] - back[0:3, cols]
        energy[:, cols] = mine[3:4]
    finish(move((result, energy), (force_out, energy_out), out_sem))


def on_device(positions, features, species, species_scale, w_first, w_second, w_radial, w_mid, w_last, w_out,
              ghost_send, local_first, local_second, local_mask, ghost_owner, ghost_index, ghost_mask):
    v, shape = pltpu.VMEM, jax.ShapeDtypeStruct
    count = positions.shape[1]
    sends = ghost_send.shape[0]
    channels, nb = w_radial.shape
    blocks = len(OFFSETS)
    chunks, gchunks = count // 128, blocks * sends // 128
    lrows, grows = local_first.shape[0] // 128, ghost_owner.shape[0] // 128
    buffers = lambda arrays: [v(x.shape, x.dtype) for x in arrays]
    sems = lambda number: pltpu.SemaphoreType.DMA((number,))
    send_row = ghost_send.reshape(1, sends)
    net = [w_radial.T, w_mid, w_last, w_out.reshape(1, channels)]
    local = [x.reshape(lrows, 128) for x in (local_first, local_second, local_mask)]
    ghostly = [x.reshape(grows, 128) for x in (ghost_owner, ghost_index, ghost_mask)]
    blocks_w = [v((4 * channels, 4 * channels), BF16), v((4 * channels, 4 * channels), BF16), v((4 * channels, 16 * nb), BF16)]
    hots = lambda width: [v((width, 64, 1024), BF16), v((width, 64, 1024), BF16), v((width, 64, 128), F32)]
    table = shape((channels * count // 256, 256), BF16)
    acc = shape((16 * chunks, 64), F32)
    own_tab = v((4 * chunks, 8, 128), F32)

    args = [positions, features, species.reshape(1, count), species_scale.reshape(1, -1), w_first, w_second, send_row] + local + net
    made = [shape((8, count), F32), table, table, shape((blocks, ROWS, sends), BF16),
            shape((lrows, 128), I32), shape((8, 128), I32), acc, acc]
    own, left_tab, right_tab, ghosts, packed, stand, acc_own, acc_loc = pl.pallas_call(
        offer_kernel,
        name="offer",
        out_shape=made,
        in_specs=[HBM] * len(args),
        out_specs=[HBM] * len(made),
        scratch_shapes=buffers(args) + [v((ROWS, sends), BF16)] + buffers(made[0:3] + made[4:]) + [
            own_tab, v((lrows, 128), I32), v((lrows, 128), F32), v((lrows, 256), F32)] + hots(MANY) + blocks_w + [
            sems(len(args)), sems(5), sems(2), sems(blocks), sems(blocks)],
        compiler_params=pltpu.CompilerParams(collective_id=0, has_side_effects=True, vmem_limit_bytes=60 << 20),
    )(*args)

    args = [own, left_tab, right_tab, ghosts, packed, stand, acc_own, acc_loc] + ghostly + net
    made = [acc, acc, shape((blocks, 8, sends), F32)]
    acc_own, acc_loc, gforce = pl.pallas_call(
        pairs_kernel,
        name="pairs",
        out_shape=made,
        in_specs=[HBM] * len(args),
        out_specs=[HBM] * len(made),
        scratch_shapes=buffers(args) + [
            own_tab, v((4 * gchunks, 8, 128), F32), v((channels * gchunks // 2, 256), BF16), v((grows, 128), I32),
            v((grows, 128), I32), v((grows, 128), F32), v((grows, 256), F32)] + hots(FEW) + [
            v((16 * gchunks, 64), F32), v((blocks, 8, sends), F32)] + blocks_w + [sems(len(args)), sems(1), sems(2)],
        compiler_params=pltpu.CompilerParams(vmem_limit_bytes=60 << 20),
    )(*args)

    args = [own, left_tab, right_tab, packed, acc_own, acc_loc, gforce] + net
    made = [acc, acc, shape((blocks, 8, sends), F32)]
    acc_own, acc_loc, arrived = pl.pallas_call(
        home_kernel,
        name="home",
        out_shape=made,
        in_specs=[HBM] * len(args),
        out_specs=[HBM] * len(made),
        scratch_shapes=buffers(args[:6] + args[7:]) + [own_tab] + hots(MANY) + blocks_w + [
            sems(len(args) - 1), sems(2), sems(blocks), sems(blocks)],
        compiler_params=pltpu.CompilerParams(collective_id=1, has_side_effects=True, vmem_limit_bytes=60 << 20),
    )(*args)

    args = [acc_own, acc_loc, arrived, send_row]
    made = [shape((3, count), F32), shape((1, count), F32)]
    forces, energy = pl.pallas_call(
        join_kernel,
        name="join",
        out_shape=made,
        in_specs=[HBM] * len(args),
        out_specs=[HBM] * len(made),
        scratch_shapes=buffers(args) + buffers(made) + [sems(len(args)), sems(len(made))],
        compiler_params=pltpu.CompilerParams(vmem_limit_bytes=60 << 20),
    )(*args)
    return forces, energy.reshape(count)


def solution(mesh):
    everywhere = ("gx", "gy", "gz")
    wide, flat, copied = P(None, everywhere), P(everywhere), P()
    in_specs = (wide, wide, flat) + (copied,) * 7 + (flat,) * 7
    return jax.shard_map(on_device, mesh=mesh, in_specs=in_specs, out_specs=(wide, flat), check_vma=False)
```

```python
import jax
import jax.numpy as jnp
from jax import lax
from jax.experimental import pallas as pl
from jax.experimental.pallas import tpu as pltpu
from jax.sharding import PartitionSpec as P

OFFSETS = ((1, 0, 0), (0, 1, 0), (0, 0, 1), (1, 1, 0), (1, 0, 1), (0, 1, 1), (1, 1, 1))
DIRECT = (2, 0, 1, 3)
RELAYED = ((0, 4), (1, 5), (3, 6))
MESH_IDS = pl.DeviceIdType.MESH
HBM = pl.BlockSpec(memory_space=pltpu.HBM)
NT = (((1,), (1,)), ((), ()))
TN = (((0,), (0,)), ((), ()))
WIDTH = 24.0
F32, BF16, I32 = jnp.float32, jnp.bfloat16, jnp.int32
LIVE = 128
ROWS = 72
EARLY = 8
LATE = 8
HALVES = 4
MANY = 4
FEW = 2
GHOSTLY = 3


def neighbour(offset, sign):
    where = []
    for axis, step in zip(("gx", "gy", "gz"), offset):
        count = lax.axis_size(axis)
        where.append(lax.rem(lax.axis_index(axis) + sign * step + count, count))
    return tuple(where)


def meet(offsets, sign):
    barrier = pltpu.get_barrier_semaphore()
    for offset in offsets:
        pl.semaphore_signal(barrier, inc=1, device_id=neighbour(offset, sign), device_id_type=MESH_IDS)
    return barrier


def move(sources, targets, sems):
    copies = [pltpu.make_async_copy(s, t, sems.at[k]) for k, (s, t) in enumerate(zip(sources, targets))]
    for copy in copies:
        copy.start()
    return copies


def finish(copies):
    for copy in copies:
        copy.wait()


def one_hot(row, count):
    levels = lax.broadcasted_iota(jnp.int16, (count, row.shape[1]), 0)
    return jnp.where(levels == row.astype(jnp.int16), jnp.ones((), BF16), jnp.zeros((), BF16))


def split_two(value):
    high = value.astype(BF16).astype(F32)
    return high, value - high


def take_lanes(table, index):
    return jnp.take_along_axis(table, index, axis=1, mode="promise_in_bounds")


def pick(tab, n, c, low, high):
    value = take_lanes(tab[c * n], low)
    for ch in range(1, n):
        value = jnp.where(high == ch, take_lanes(tab[c * n + ch], low), value)
    return value


def geometry(low_i, high_i, low_j, high_j, own_tab, tab, chunks, n):
    gap = [pick(tab, n, c, low_j, high_j) - pick(own_tab, chunks, c, low_i, high_i) for c in range(3)]
    return gap, gap[0] * gap[0] + gap[1] * gap[1] + gap[2] * gap[2]


def spread(row, tab, first):
    for ch in range(row.shape[1] // 128):
        tab[first + ch] = jnp.broadcast_to(row[:, 128 * ch:128 * ch + 128], (8, 128))


def compact(own_list, par_list, mask_list, own_tab, tab, chunks, n, words, live, ranks, packed):
    rows = own_list.shape[0]
    lane = lax.broadcasted_iota(I32, (8, 128), 1)

    def find(v, carry):
        at = pl.ds(pl.multiple_of(8 * v, 8), 8)
        own, partner = own_list[at, :], par_list[at, :]
        gap, squared = geometry(own & 127, own >> 7, partner & 127, partner >> 7, own_tab, tab, chunks, n)
        alive = jnp.logical_and(mask_list[at, :] > 0, squared < 1.0)
        live[at, :] = jnp.where(alive, 1.0, 0.0)
        words[at, :] = jnp.where(alive, (own << 8) + (partner << 17) + LIVE, 0)
        return carry
    lax.fori_loop(0, rows // 8, find, 0, unroll=True)
    above = jnp.where(lax.broadcasted_iota(I32, (128, 128), 0) < lax.broadcasted_iota(I32, (128, 128), 1), 1.0, 0.0)
    adder = jnp.concatenate([above, jnp.ones((128, 128), F32)], 1).astype(BF16)
    ranks[0:rows, :] = jnp.dot(live[0:rows, :].astype(BF16), adder, preferred_element_type=F32)

    tiles = rows // 8
    stand = jnp.zeros((8, 128), I32)
    slots = [jnp.zeros((8, 128), I32) for _ in range(tiles)]
    for v in range(tiles):
        at = slice(8 * v, 8 * v + 8)
        word = words[at, :]
        rank = ranks[at, 0:128].astype(I32)
        number = ranks[at, 128:256].astype(I32)
        word = jnp.where(word > 0, word + (lane - rank), 0)
        for bit in range(7):
            moved = pltpu.roll(word, 128 - (1 << bit), 1)
            stay = jnp.where((word & (1 << bit)) > 0, 0, word)
            word = jnp.where((moved & (1 << bit)) > 0, moved, stay)
        turn = (lane - stand) & 127
        word = take_lanes(word, turn)
        row = jnp.where(turn < number, (stand + turn) >> 7, -1)
        for t in range(v + 1):
            slots[t] = jnp.where(row == t, word, slots[t])
        stand = stand + number
    for t in range(tiles):
        packed[8 * t:8 * t + 8, :] = slots[t]
    return stand


def weights(radial, mid, last, out, w_mids, w_lasts, w_radials):
    nb, channels = radial.shape
    high, low = split_two(radial[...] * 0.5)
    spot = lax.broadcasted_iota(I32, (nb, 4 * nb), 1)
    term = lax.broadcasted_iota(I32, (nb, 4 * nb), 0)
    place_high = jnp.where((spot == term) | (spot == term + nb), 1.0, 0.0).astype(BF16)
    place_low = jnp.where(spot == term + 2 * nb, 1.0, 0.0).astype(BF16)
    w_radial = (lax.dot_general(high.astype(BF16), place_high, TN, preferred_element_type=F32)
                + lax.dot_general(low.astype(BF16), place_low, TN, preferred_element_type=F32)).astype(BF16)
    w_mid = (mid[...].astype(F32) * 0.5).astype(BF16)
    w_last = (last[...].astype(F32) * 0.5).astype(BF16)
    for store, w in ((w_mids, w_mid), (w_lasts, w_last), (w_radials, w_radial)):
        for half in range(HALVES):
            store[channels * half:channels * half + channels, :] = jnp.concatenate(
                [w if other == half else jnp.zeros_like(w) for other in range(HALVES)], 1)
    eye = lax.broadcasted_iota(I32, (channels, channels), 0) == lax.broadcasted_iota(I32, (channels, channels), 1)
    return jnp.sum(jnp.where(eye, jnp.broadcast_to(out[...], (channels, channels)), 0.0), 1, keepdims=True)


def activate(y, tangent):
    up = 1.0 + jnp.tanh(y)
    value = y * up
    return value, (up + value * (2.0 - up)) * tangent


def pair_step(packed, own_tab, tab, chunks, n, left_tab, right_tab, w_mids, w_lasts, w_radials, w_out,
              hot_own, hot_par, quant, acc_own, acc_par, width):
    nb = 8
    centers = lax.broadcasted_iota(I32, (nb, 128), 0).astype(F32) / (nb - 1)
    zero = jnp.zeros((), BF16)

    def stages(t, u):
        word = packed[pl.ds(pl.multiple_of(8 * t, 8), 8), :]
        own, partner = (word >> 8) & 511, word >> 17
        low_i, high_i, low_j, high_j = own & 127, own >> 7, partner & 127, partner >> 7
        wide = lambda x, half: jnp.concatenate([x[2 * half:2 * half + 1], x[2 * half + 1:2 * half + 2]], 1)

        def gather(low, high, keep, table, groups, half):
            hot = one_hot(wide(low, half), 128)
            keep[u, :, 256 * half:256 * half + 256] = hot[0:64] + hot[64:128]
            top = wide(high, half)
            odd = jnp.broadcast_to((top & 1).astype(jnp.int16), (128, 256))
            hot = jnp.concatenate([jnp.where(odd == jnp.int16(0), hot, zero), jnp.where(odd == jnp.int16(1), hot, zero)], 0)
            found = jnp.dot(table[...], hot, preferred_element_type=F32)
            group = top >> 1
            value = found[0:64]
            for g in range(1, groups):
                value = jnp.where(group == g, found[64 * g:64 * g + 64], value)
            return value

        gathered = [gather(low_i, high_i, hot_own, left_tab, chunks // 2, half)
                    + gather(low_j, high_j, hot_par, right_tab, n // 2, half) for half in range(HALVES)]
        yield
        gap, squared = geometry(low_i, high_i, low_j, high_j, own_tab, tab, chunks, n)
        weight = jnp.where((word & LIVE) > 0, pick(own_tab, chunks, 3, low_i, high_i) * pick(tab, n, 3, low_j, high_j), 0.0)
        radials = []
        for half in range(HALVES):
            tiles, slants = [], []
            for r in (2 * half, 2 * half + 1):
                off = squared[r:r + 1] - centers
                basis = jnp.exp(-WIDTH * off * off)
                tiles.append(basis)
                slants.append((-2.0 * WIDTH) * off * basis)
            high, low = split_two(jnp.concatenate(tiles + slants, 1))
            radials += [high, low, high, jnp.zeros_like(low)]
        radials = jnp.dot(w_radials[...], jnp.concatenate(radials, 0).astype(BF16), preferred_element_type=F32)
        yield
        quarter = lambda x, half: x[64 * half:64 * half + 64]
        now = [activate(g + quarter(radials, half)[:, 0:256], quarter(radials, half)[:, 256:512]) for half, g in enumerate(gathered)]
        for w in (w_mids, w_lasts):
            stack = jnp.concatenate([jnp.concatenate(pair, 1).astype(BF16) for pair in now], 0)
            mixed = jnp.dot(w[...], stack, preferred_element_type=F32)
            yield
            now = [activate(quarter(mixed, half)[:, 0:256], quarter(mixed, half)[:, 256:512]) for half in range(HALVES)]
        reads = [jnp.sum(value * w_out, 0, keepdims=True) for value, _ in now]
        slopes = [jnp.sum(slope * w_out, 0, keepdims=True) for _, slope in now]
        yield
        tall = lambda xs: jnp.concatenate([x[:, 128 * k:128 * k + 128] for x in xs for k in range(2)], 0)
        readout, reslope = tall(reads), tall(slopes)
        near = jnp.maximum(1.0 - squared, 0.0)
        envelope = near * near
        energy = weight * envelope * readout
        slope = weight * (envelope * reslope - 2.0 * near * readout)
        outs = [2.0 * g * slope for g in gap] + [energy]
        for q, out in enumerate(outs):
            quant[u, 8 * q:8 * q + 8, :] = out
            quant[u, 32 + 8 * q:40 + 8 * q, :] = out
        a_own, a_par = [], []
        part_i, part_j = own >> 6, partner >> 6
        which = lax.broadcasted_iota(I32, (8, 128), 0) >> 2
        for r in range(8):
            tile = quant[u, pl.ds(r, 8, stride=8), :]
            pick_i, pick_j = part_i[r:r + 1] - which, part_j[r:r + 1] - which
            a_own.append(jnp.concatenate([jnp.where(pick_i == 2 * ch, tile, 0.0) for ch in range(chunks)], 0))
            a_par.append(jnp.concatenate([jnp.where(pick_j == 2 * ch, tile, 0.0) for ch in range(n)], 0))
        acc_own[...] += lax.dot_general(jnp.concatenate(a_own, 1).astype(BF16), hot_own[u], NT, preferred_element_type=F32)
        acc_par[...] += lax.dot_general(jnp.concatenate(a_par, 1).astype(BF16), hot_par[u], NT, preferred_element_type=F32)

    def step(t, carry):
        streams = [stages(width * t + u, u) for u in range(width)]
        while streams:
            streams = [stream for stream in streams if next(stream, True) is None]
        return carry
    return step


def joined(acc, ch):
    return jnp.concatenate([acc[8 * ch:8 * ch + 4, :], acc[8 * ch + 4:8 * ch + 8, :]], 1)


def trips(stand, width):
    return (jnp.max(stand) + (128 * width - 1)) // (128 * width)


def offer_kernel(pos_hbm, feat_hbm, species_hbm, scale_hbm, first_hbm, second_hbm, send_hbm,
                 one_hbm, two_hbm, mask_hbm, radial_hbm, mid_hbm, last_hbm, out_hbm,
                 own_out, left_out, right_out, ghost_out, packed_out, stand_out, acc_own_out, acc_loc_out,
                 pos, feat, species, scale, first, second, send, one, two, mask, radial, mid, last, out,
                 offered, own, left_tab, right_tab, packed, stand, acc_own, acc_loc,
                 own_tab, words, live, ranks, hot_own, hot_par, quant, w_mids, w_lasts, w_radials,
                 in_sem, out_sem, last_sem, send_sem, recv_sem):
    paths = [OFFSETS[k] for k in DIRECT]
    barrier = meet(paths, 1)
    loads = move((pos_hbm, feat_hbm, species_hbm, scale_hbm, first_hbm, second_hbm, send_hbm,
                  one_hbm, two_hbm, mask_hbm, radial_hbm, mid_hbm, last_hbm, out_hbm),
                 (pos, feat, species, scale, first, second, send, one, two, mask, radial, mid, last, out), in_sem)
    finish(loads[0:7])
    count = pos.shape[1]
    chunks = count // 128
    where = pos[...]
    kinds = species[...]
    scales = scale[...].astype(F32)
    gain = jnp.zeros(kinds.shape, F32)
    for kind in range(scales.shape[1]):
        gain = jnp.where(kinds == kind, scales[:, kind:kind + 1], gain)
    right = (jnp.dot(second[...], feat[...], preferred_element_type=F32).astype(BF16).astype(F32) * 0.5).astype(BF16)
    high = where.astype(BF16).astype(F32)
    tail = jnp.concatenate([high, where - high, gain, jnp.zeros((9, count), F32)], 0).astype(BF16)
    payload = jnp.concatenate([right, tail], 0)
    offered[...] = jnp.dot(payload, one_hot(send[...], count), preferred_element_type=F32).astype(BF16)[0:ROWS]
    pl.semaphore_wait(barrier, len(paths))

    def remote(source, k, offset):
        copy = pltpu.make_async_remote_copy(
            src_ref=source, dst_ref=ghost_out.at[k], send_sem=send_sem.at[k], recv_sem=recv_sem.at[k],
            device_id=neighbour(offset, -1), device_id_type=MESH_IDS)
        copy.start()
        return copy
    copies = [remote(offered, k, OFFSETS[k]) for k in DIRECT]

    own[0:3, :] = where
    own[3:4, :] = gain
    own[4:8, :] = jnp.zeros((4, count), F32)
    left = (jnp.dot(first[...], feat[...], preferred_element_type=F32).astype(BF16).astype(F32) * 0.5).astype(BF16)
    for g in range(count // 256):
        left_tab[64 * g:64 * g + 64, :] = left[:, 256 * g:256 * g + 256]
        right_tab[64 * g:64 * g + 64, :] = right[:, 256 * g:256 * g + 256]
    for c in range(4):
        spread(own[c:c + 1, :], own_tab, c * chunks)
    finish(loads[7:])
    w_out = weights(radial, mid, last, out, w_mids, w_lasts, w_radials)
    stand[...] = compact(one, two, mask, own_tab, own_tab, chunks, chunks, words, live, ranks, packed)
    copies[0].wait_recv()
    relays = [remote(ghost_out.at[2], k, OFFSETS[step]) for step, k in RELAYED]
    acc_own[...] = jnp.zeros_like(acc_own)
    acc_loc[...] = jnp.zeros_like(acc_loc)
    step = pair_step(packed, own_tab, own_tab, chunks, chunks, left_tab, right_tab, w_mids, w_lasts, w_radials, w_out,
                     hot_own, hot_par, quant, acc_own, acc_loc, MANY)
    stores = move((own, left_tab, right_tab, packed, stand), (own_out, left_out, right_out, packed_out, stand_out), out_sem)
    lax.fori_loop(0, EARLY // MANY, step, 0)
    stores += move((acc_own, acc_loc), (acc_own_out, acc_loc_out), last_sem)
    copies[0].wait_send()
    finish(copies[1:])
    finish(relays)
    finish(stores)


def pairs_kernel(own_hbm, left_hbm, right_hbm, ghost_hbm, packed_hbm, stand_hbm, acc_own_hbm, acc_loc_hbm,
                 one_hbm, two_hbm, mask_hbm, radial_hbm, mid_hbm, last_hbm, out_hbm,
                 acc_own_out, acc_loc_out, force_out,
                 own, left_tab, right_tab, ghost, packed, stand, acc_own, acc_loc, one, two, mask, radial, mid, last, out,
                 own_tab, ghost_tab, gtable, gpacked, words, live, ranks, hot_own, hot_par, quant, acc_gho, force,
                 w_mids, w_lasts, w_radials, in_sem, out_sem, last_sem):
    loads = move((own_hbm, ghost_hbm, one_hbm, two_hbm, mask_hbm, left_hbm, right_hbm, packed_hbm, stand_hbm,
                  acc_own_hbm, acc_loc_hbm, radial_hbm, mid_hbm, last_hbm, out_hbm),
                 (own, ghost, one, two, mask, left_tab, right_tab, packed, stand,
                  acc_own, acc_loc, radial, mid, last, out), in_sem)
    finish(loads[0:5])
    count = own.shape[1]
    chunks = count // 128
    sends = ghost.shape[2]
    per = sends // 128
    gchunks = len(OFFSETS) * per
    for c in range(4):
        spread(own[c:c + 1, :], own_tab, c * chunks)
    for k, offset in enumerate(OFFSETS):
        gtable[64 * k:64 * k + 64, :] = ghost[k, 0:64, :]
        tail = ghost[k, 64:72, :].astype(F32)
        for c in range(4):
            row = tail[c:c + 1] + tail[c + 3:c + 4] + float(offset[c]) if c < 3 else tail[6:7]
            spread(row, ghost_tab, c * gchunks + k * per)
    finish(loads[5:])
    w_out = weights(radial, mid, last, out, w_mids, w_lasts, w_radials)
    gstand = compact(one, two, mask, own_tab, ghost_tab, chunks, gchunks, words, live, ranks, gpacked)
    acc_gho[...] = jnp.zeros_like(acc_gho)
    gstep = pair_step(gpacked, own_tab, ghost_tab, chunks, gchunks, left_tab, gtable, w_mids, w_lasts, w_radials, w_out,
                      hot_own, hot_par, quant, acc_own, acc_gho, GHOSTLY)
    lax.fori_loop(0, trips(gstand, GHOSTLY), gstep, 0)
    for ch in range(gchunks):
        cols = slice(128 * (ch % per), 128 * (ch % per) + 128)
        force[ch // per, 0:4, cols] = joined(acc_gho, ch)
        force[ch // per, 4:8, cols] = jnp.zeros((4, 128), F32)
    step = pair_step(packed, own_tab, own_tab, chunks, chunks, left_tab, right_tab, w_mids, w_lasts, w_radials, w_out,
                     hot_own, hot_par, quant, acc_own, acc_loc, FEW)
    stores = move((force,), (force_out,), out_sem)
    lax.fori_loop((EARLY + LATE) // FEW, trips(stand[...], FEW), step, 0)
    finish(stores + move((acc_own, acc_loc), (acc_own_out, acc_loc_out), last_sem))


def home_kernel(own_hbm, left_hbm, right_hbm, packed_hbm, acc_own_hbm, acc_loc_hbm, force_hbm,
                radial_hbm, mid_hbm, last_hbm, out_hbm,
                acc_own_out, acc_loc_out, arrived_out,
                own, left_tab, right_tab, packed, acc_own, acc_loc, radial, mid, last, out,
                own_tab, hot_own, hot_par, quant, w_mids, w_lasts, w_radials,
                in_sem, out_sem, send_sem, recv_sem):
    barrier = meet(OFFSETS, -1)
    finish(move((own_hbm, left_hbm, right_hbm, packed_hbm, acc_own_hbm, acc_loc_hbm, radial_hbm, mid_hbm, last_hbm, out_hbm),
                (own, left_tab, right_tab, packed, acc_own, acc_loc, radial, mid, last, out), in_sem))
    pl.semaphore_wait(barrier, len(OFFSETS))
    copies = []
    for k, offset in enumerate(OFFSETS):
        copy = pltpu.make_async_remote_copy(
            src_ref=force_hbm.at[k], dst_ref=arrived_out.at[k], send_sem=send_sem.at[k], recv_sem=recv_sem.at[k],
            device_id=neighbour(offset, 1), device_id_type=MESH_IDS)
        copy.start()
        copies.append(copy)
    chunks = own.shape[1] // 128
    for c in range(4):
        spread(own[c:c + 1, :], own_tab, c * chunks)
    w_out = weights(radial, mid, last, out, w_mids, w_lasts, w_radials)
    step = pair_step(packed, own_tab, own_tab, chunks, chunks, left_tab, right_tab, w_mids, w_lasts, w_radials, w_out,
                     hot_own, hot_par, quant, acc_own, acc_loc, MANY)
    lax.fori_loop(EARLY // MANY, (EARLY + LATE) // MANY, step, 0)
    stores = move((acc_own, acc_loc), (acc_own_out, acc_loc_out), out_sem)
    finish(copies)
    finish(stores)


def join_kernel(acc_own_hbm, acc_loc_hbm, arrived_hbm, send_hbm, force_out, energy_out,
                acc_own, acc_loc, arrived, send, result, energy, in_sem, out_sem):
    finish(move((acc_own_hbm, acc_loc_hbm, arrived_hbm, send_hbm), (acc_own, acc_loc, arrived, send), in_sem))
    count = result.shape[1]
    hot = one_hot(send[...], count)
    total = arrived[0]
    for k in range(1, len(OFFSETS)):
        total = total + arrived[k]
    high, rest = split_two(total)
    mid_part, low = split_two(rest)
    parts = jnp.concatenate([high, mid_part, low, jnp.zeros_like(low)], 0).astype(BF16)
    back = lax.dot_general(parts, hot, NT, preferred_element_type=F32)
    back = back[0:8] + back[8:16] + back[16:24]
    for ch in range(count // 128):
        cols = slice(128 * ch, 128 * ch + 128)
        mine = joined(acc_own, ch)
        result[:, cols] = mine[0:3] - joined(acc_loc, ch)[0:3] - back[0:3, cols]
        energy[:, cols] = mine[3:4]
    finish(move((result, energy), (force_out, energy_out), out_sem))


def on_device(positions, features, species, species_scale, w_first, w_second, w_radial, w_mid, w_last, w_out,
              ghost_send, local_first, local_second, local_mask, ghost_owner, ghost_index, ghost_mask):
    v, shape = pltpu.VMEM, jax.ShapeDtypeStruct
    count = positions.shape[1]
    sends = ghost_send.shape[0]
    channels, nb = w_radial.shape
    blocks = len(OFFSETS)
    chunks, gchunks = count // 128, blocks * sends // 128
    lrows, grows = local_first.shape[0] // 128, ghost_owner.shape[0] // 128
    buffers = lambda arrays: [v(x.shape, x.dtype) for x in arrays]
    sems = lambda number: pltpu.SemaphoreType.DMA((number,))
    send_row = ghost_send.reshape(1, sends)
    net = [w_radial.T, w_mid, w_last, w_out.reshape(1, channels)]
    local = [x.reshape(lrows, 128) for x in (local_first, local_second, local_mask)]
    ghostly = [x.reshape(grows, 128) for x in (ghost_owner, ghost_index, ghost_mask)]
    blocks_w = [v((4 * channels, 4 * channels), BF16), v((4 * channels, 4 * channels), BF16), v((4 * channels, 16 * nb), BF16)]
    hots = lambda width: [v((width, 64, 1024), BF16), v((width, 64, 1024), BF16), v((width, 64, 128), F32)]
    table = shape((channels * count // 256, 256), BF16)
    acc = shape((8 * chunks, 64), F32)
    own_tab = v((4 * chunks, 8, 128), F32)

    args = [positions, features, species.reshape(1, count), species_scale.reshape(1, -1), w_first, w_second, send_row] + local + net
    made = [shape((8, count), F32), table, table, shape((blocks, ROWS, sends), BF16),
            shape((lrows, 128), I32), shape((8, 128), I32), acc, acc]
    own, left_tab, right_tab, ghosts, packed, stand, acc_own, acc_loc = pl.pallas_call(
        offer_kernel,
        name="offer",
        out_shape=made,
        in_specs=[HBM] * len(args),
        out_specs=[HBM] * len(made),
        scratch_shapes=buffers(args) + [v((ROWS, sends), BF16)] + buffers(made[0:3] + made[4:]) + [
            own_tab, v((lrows, 128), I32), v((lrows, 128), F32), v((lrows, 256), F32)] + hots(MANY) + blocks_w + [
            sems(len(args)), sems(5), sems(2), sems(blocks), sems(blocks)],
        compiler_params=pltpu.CompilerParams(collective_id=0, has_side_effects=True, vmem_limit_bytes=60 << 20),
    )(*args)

    args = [own, left_tab, right_tab, ghosts, packed, stand, acc_own, acc_loc] + ghostly + net
    made = [acc, acc, shape((blocks, 8, sends), F32)]
    acc_own, acc_loc, gforce = pl.pallas_call(
        pairs_kernel,
        name="pairs",
        out_shape=made,
        in_specs=[HBM] * len(args),
        out_specs=[HBM] * len(made),
        scratch_shapes=buffers(args) + [
            own_tab, v((4 * gchunks, 8, 128), F32), v((channels * gchunks // 2, 256), BF16), v((grows, 128), I32),
            v((grows, 128), I32), v((grows, 128), F32), v((grows, 256), F32)] + hots(GHOSTLY) + [
            v((8 * gchunks, 64), F32), v((blocks, 8, sends), F32)] + blocks_w + [sems(len(args)), sems(1), sems(2)],
        compiler_params=pltpu.CompilerParams(vmem_limit_bytes=60 << 20),
    )(*args)

    args = [own, left_tab, right_tab, packed, acc_own, acc_loc, gforce] + net
    made = [acc, acc, shape((blocks, 8, sends), F32)]
    acc_own, acc_loc, arrived = pl.pallas_call(
        home_kernel,
        name="home",
        out_shape=made,
        in_specs=[HBM] * len(args),
        out_specs=[HBM] * len(made),
        scratch_shapes=buffers(args[:6] + args[7:]) + [own_tab] + hots(MANY) + blocks_w + [
            sems(len(args) - 1), sems(2), sems(blocks), sems(blocks)],
        compiler_params=pltpu.CompilerParams(collective_id=1, has_side_effects=True, vmem_limit_bytes=60 << 20),
    )(*args)

    args = [acc_own, acc_loc, arrived, send_row]
    made = [shape((3, count), F32), shape((1, count), F32)]
    forces, energy = pl.pallas_call(
        join_kernel,
        name="join",
        out_shape=made,
        in_specs=[HBM] * len(args),
        out_specs=[HBM] * len(made),
        scratch_shapes=buffers(args) + buffers(made) + [sems(len(args)), sems(len(made))],
        compiler_params=pltpu.CompilerParams(vmem_limit_bytes=60 << 20),
    )(*args)
    return forces, energy.reshape(count)


def solution(mesh):
    everywhere = ("gx", "gy", "gz")
    wide, flat, copied = P(None, everywhere), P(everywhere), P()
    in_specs = (wide, wide, flat) + (copied,) * 7 + (flat,) * 7
    return jax.shard_map(on_device, mesh=mesh, in_specs=in_specs, out_specs=(wide, flat), check_vma=False)
```

```python
import jax
import jax.numpy as jnp
from jax import lax
from jax.experimental import pallas as pl
from jax.experimental.pallas import tpu as pltpu
from jax.sharding import PartitionSpec as P

OFFSETS = ((1, 0, 0), (0, 1, 0), (0, 0, 1), (1, 1, 0), (1, 0, 1), (0, 1, 1), (1, 1, 1))
DIRECT = (2, 0, 1, 3)
RELAYED = ((0, 4), (1, 5), (3, 6))
MESH_IDS = pl.DeviceIdType.MESH
HBM = pl.BlockSpec(memory_space=pltpu.HBM)
NT = (((1,), (1,)), ((), ()))
TN = (((0,), (0,)), ((), ()))
WIDTH = 24.0
F32, BF16, I32 = jnp.float32, jnp.bfloat16, jnp.int32
LIVE = 128
ROWS = 72
EARLY = 8
LATE = 8
HALVES = 4
MANY = 4
FEW = 2
GHOSTLY = 3


def neighbour(offset, sign):
    where = []
    for axis, step in zip(("gx", "gy", "gz"), offset):
        count = lax.axis_size(axis)
        where.append(lax.rem(lax.axis_index(axis) + sign * step + count, count))
    return tuple(where)


def meet(offsets, sign):
    barrier = pltpu.get_barrier_semaphore()
    for offset in offsets:
        pl.semaphore_signal(barrier, inc=1, device_id=neighbour(offset, sign), device_id_type=MESH_IDS)
    return barrier


def move(sources, targets, sems):
    copies = [pltpu.make_async_copy(s, t, sems.at[k]) for k, (s, t) in enumerate(zip(sources, targets))]
    for copy in copies:
        copy.start()
    return copies


def finish(copies):
    for copy in copies:
        copy.wait()


def one_hot(row, count):
    levels = lax.broadcasted_iota(jnp.int16, (count, row.shape[1]), 0)
    return jnp.where(levels == row.astype(jnp.int16), jnp.ones((), BF16), jnp.zeros((), BF16))


def split_two(value):
    high = value.astype(BF16).astype(F32)
    return high, value - high


def take_lanes(table, index):
    return jnp.take_along_axis(table, index, axis=1, mode="promise_in_bounds")


def pick(tab, n, c, low, high):
    value = take_lanes(tab[c * n], low)
    for ch in range(1, n):
        value = jnp.where(high == ch, take_lanes(tab[c * n + ch], low), value)
    return value


def geometry(low_i, high_i, low_j, high_j, own_tab, tab, chunks, n):
    gap = [pick(tab, n, c, low_j, high_j) - pick(own_tab, chunks, c, low_i, high_i) for c in range(3)]
    return gap, gap[0] * gap[0] + gap[1] * gap[1] + gap[2] * gap[2]


def spread(row, tab, first):
    for ch in range(row.shape[1] // 128):
        tab[first + ch] = jnp.broadcast_to(row[:, 128 * ch:128 * ch + 128], (8, 128))


def compact(own_list, par_list, mask_list, own_tab, tab, chunks, n, words, live, ranks, packed):
    rows = own_list.shape[0]
    lane = lax.broadcasted_iota(I32, (8, 128), 1)

    def find(v, carry):
        at = pl.ds(pl.multiple_of(8 * v, 8), 8)
        own, partner = own_list[at, :], par_list[at, :]
        gap, squared = geometry(own & 127, own >> 7, partner & 127, partner >> 7, own_tab, tab, chunks, n)
        alive = jnp.logical_and(mask_list[at, :] > 0, squared < 1.0)
        live[at, :] = jnp.where(alive, 1.0, 0.0)
        words[at, :] = jnp.where(alive, (own << 8) + (partner << 17) + LIVE, 0)
        return carry
    lax.fori_loop(0, rows // 8, find, 0, unroll=True)
    above = jnp.where(lax.broadcasted_iota(I32, (128, 128), 0) < lax.broadcasted_iota(I32, (128, 128), 1), 1.0, 0.0)
    adder = jnp.concatenate([above, jnp.ones((128, 128), F32)], 1).astype(BF16)
    ranks[0:rows, :] = jnp.dot(live[0:rows, :].astype(BF16), adder, preferred_element_type=F32)

    tiles = rows // 8
    stand = jnp.zeros((8, 128), I32)
    slots = [jnp.zeros((8, 128), I32) for _ in range(tiles)]
    for v in range(tiles):
        at = slice(8 * v, 8 * v + 8)
        word = words[at, :]
        rank = ranks[at, 0:128].astype(I32)
        number = ranks[at, 128:256].astype(I32)
        word = jnp.where(word > 0, word + (lane - rank), 0)
        for bit in range(7):
            moved = pltpu.roll(word, 128 - (1 << bit), 1)
            stay = jnp.where((word & (1 << bit)) > 0, 0, word)
            word = jnp.where((moved & (1 << bit)) > 0, moved, stay)
        turn = (lane - stand) & 127
        word = take_lanes(word, turn)
        row = jnp.where(turn < number, (stand + turn) >> 7, -1)
        for t in range(v + 1):
            slots[t] = jnp.where(row == t, word, slots[t])
        stand = stand + number
    for t in range(tiles):
        packed[8 * t:8 * t + 8, :] = slots[t]
    return stand


def weights(radial, mid, last, out, w_mids, w_lasts, w_radials):
    nb, channels = radial.shape
    high, low = split_two(radial[...] * 0.5)
    spot = lax.broadcasted_iota(I32, (nb, 4 * nb), 1)
    term = lax.broadcasted_iota(I32, (nb, 4 * nb), 0)
    place_high = jnp.where((spot == term) | (spot == term + nb), 1.0, 0.0).astype(BF16)
    place_low = jnp.where(spot == term + 2 * nb, 1.0, 0.0).astype(BF16)
    w_radial = (lax.dot_general(high.astype(BF16), place_high, TN, preferred_element_type=F32)
                + lax.dot_general(low.astype(BF16), place_low, TN, preferred_element_type=F32)).astype(BF16)
    w_mid = (mid[...].astype(F32) * 0.5).astype(BF16)
    w_last = (last[...].astype(F32) * 0.5).astype(BF16)
    for store, w in ((w_mids, w_mid), (w_lasts, w_last), (w_radials, w_radial)):
        for half in range(HALVES):
            store[channels * half:channels * half + channels, :] = jnp.concatenate(
                [w if other == half else jnp.zeros_like(w) for other in range(HALVES)], 1)
    eye = lax.broadcasted_iota(I32, (channels, channels), 0) == lax.broadcasted_iota(I32, (channels, channels), 1)
    return jnp.sum(jnp.where(eye, jnp.broadcast_to(out[...], (channels, channels)), 0.0), 1, keepdims=True)


def activate(y, tangent):
    up = 1.0 + jnp.tanh(y)
    value = y * up
    return value, (up + value * (2.0 - up)) * tangent


def activate_hidden(y, tangent):
    up = 1.0 + jnp.tanh(y)
    value = (y * up).astype(BF16)
    up = up.astype(BF16)
    return value, (up + value * (2.0 - up)) * tangent.astype(BF16)


def pair_step(packed, own_tab, tab, chunks, n, left_tab, right_tab, w_mids, w_lasts, w_radials, w_out,
              hot_own, hot_par, quant, acc_own, acc_par, width):
    nb = 8
    centers = lax.broadcasted_iota(I32, (nb, 128), 0).astype(F32) / (nb - 1)
    zero = jnp.zeros((), BF16)

    def stages(t, u):
        word = packed[pl.ds(pl.multiple_of(8 * t, 8), 8), :]
        own, partner = (word >> 8) & 511, word >> 17
        low_i, high_i, low_j, high_j = own & 127, own >> 7, partner & 127, partner >> 7
        wide = lambda x, half: jnp.concatenate([x[2 * half:2 * half + 1], x[2 * half + 1:2 * half + 2]], 1)

        def gather(low, high, keep, table, groups, half):
            hot = one_hot(wide(low, half), 128)
            keep[u, :, 256 * half:256 * half + 256] = hot[0:64] + hot[64:128]
            top = wide(high, half)
            odd = jnp.broadcast_to((top & 1).astype(jnp.int16), (128, 256))
            hot = jnp.concatenate([jnp.where(odd == jnp.int16(0), hot, zero), jnp.where(odd == jnp.int16(1), hot, zero)], 0)
            found = jnp.dot(table[...], hot, preferred_element_type=F32)
            group = top >> 1
            value = found[0:64]
            for g in range(1, groups):
                value = jnp.where(group == g, found[64 * g:64 * g + 64], value)
            return value

        gathered = [gather(low_i, high_i, hot_own, left_tab, chunks // 2, half)
                    + gather(low_j, high_j, hot_par, right_tab, n // 2, half) for half in range(HALVES)]
        yield
        gap, squared = geometry(low_i, high_i, low_j, high_j, own_tab, tab, chunks, n)
        weight = jnp.where((word & LIVE) > 0, pick(own_tab, chunks, 3, low_i, high_i) * pick(tab, n, 3, low_j, high_j), 0.0)
        radials = []
        for half in range(HALVES):
            tiles, slants = [], []
            for r in (2 * half, 2 * half + 1):
                off = squared[r:r + 1] - centers
                basis = jnp.exp(-WIDTH * off * off)
                tiles.append(basis)
                slants.append((-2.0 * WIDTH) * off * basis)
            high, low = split_two(jnp.concatenate(tiles + slants, 1))
            radials += [high, low, high, jnp.zeros_like(low)]
        radials = jnp.dot(w_radials[...], jnp.concatenate(radials, 0).astype(BF16), preferred_element_type=F32)
        yield
        quarter = lambda x, half: x[64 * half:64 * half + 64]
        now = [activate_hidden(g + quarter(radials, half)[:, 0:256], quarter(radials, half)[:, 256:512]) for half, g in enumerate(gathered)]
        for w, act in ((w_mids, activate_hidden), (w_lasts, activate)):
            stack = jnp.concatenate([jnp.concatenate(pair, 1) for pair in now], 0)
            mixed = jnp.dot(w[...], stack, preferred_element_type=F32)
            yield
            now = [act(quarter(mixed, half)[:, 0:256], quarter(mixed, half)[:, 256:512]) for half in range(HALVES)]
        reads = [jnp.sum(value * w_out, 0, keepdims=True) for value, _ in now]
        slopes = [jnp.sum(slope * w_out, 0, keepdims=True) for _, slope in now]
        yield
        tall = lambda xs: jnp.concatenate([x[:, 128 * k:128 * k + 128] for x in xs for k in range(2)], 0)
        readout, reslope = tall(reads), tall(slopes)
        near = jnp.maximum(1.0 - squared, 0.0)
        envelope = near * near
        energy = weight * envelope * readout
        slope = weight * (envelope * reslope - 2.0 * near * readout)
        outs = [2.0 * g * slope for g in gap] + [energy]
        for q, out in enumerate(outs):
            quant[u, 8 * q:8 * q + 8, :] = out
            quant[u, 32 + 8 * q:40 + 8 * q, :] = out
        a_own, a_par = [], []
        part_i, part_j = own >> 6, partner >> 6
        which = lax.broadcasted_iota(I32, (8, 128), 0) >> 2
        for r in range(8):
            tile = quant[u, pl.ds(r, 8, stride=8), :]
            pick_i, pick_j = part_i[r:r + 1] - which, part_j[r:r + 1] - which
            a_own.append(jnp.concatenate([jnp.where(pick_i == 2 * ch, tile, 0.0) for ch in range(chunks)], 0))
            a_par.append(jnp.concatenate([jnp.where(pick_j == 2 * ch, tile, 0.0) for ch in range(n)], 0))
        acc_own[...] += lax.dot_general(jnp.concatenate(a_own, 1).astype(BF16), hot_own[u], NT, preferred_element_type=F32)
        acc_par[...] += lax.dot_general(jnp.concatenate(a_par, 1).astype(BF16), hot_par[u], NT, preferred_element_type=F32)

    def step(t, carry):
        streams = [stages(width * t + u, u) for u in range(width)]
        while streams:
            streams = [stream for stream in streams if next(stream, True) is None]
        return carry
    return step


def joined(acc, ch):
    return jnp.concatenate([acc[8 * ch:8 * ch + 4, :], acc[8 * ch + 4:8 * ch + 8, :]], 1)


def trips(stand, width):
    return (jnp.max(stand) + (128 * width - 1)) // (128 * width)


def offer_kernel(pos_hbm, feat_hbm, species_hbm, scale_hbm, first_hbm, second_hbm, send_hbm,
                 one_hbm, two_hbm, mask_hbm, radial_hbm, mid_hbm, last_hbm, out_hbm,
                 own_out, left_out, right_out, ghost_out, packed_out, stand_out, acc_own_out, acc_loc_out,
                 pos, feat, species, scale, first, second, send, one, two, mask, radial, mid, last, out,
                 offered, own, left_tab, right_tab, packed, stand, acc_own, acc_loc,
                 own_tab, words, live, ranks, hot_own, hot_par, quant, w_mids, w_lasts, w_radials,
                 in_sem, out_sem, last_sem, send_sem, recv_sem):
    paths = [OFFSETS[k] for k in DIRECT]
    barrier = meet(paths, 1)
    loads = move((pos_hbm, feat_hbm, species_hbm, scale_hbm, first_hbm, second_hbm, send_hbm,
                  one_hbm, two_hbm, mask_hbm, radial_hbm, mid_hbm, last_hbm, out_hbm),
                 (pos, feat, species, scale, first, second, send, one, two, mask, radial, mid, last, out), in_sem)
    finish(loads[0:7])
    count = pos.shape[1]
    chunks = count // 128
    where = pos[...]
    kinds = species[...]
    scales = scale[...].astype(F32)
    gain = jnp.zeros(kinds.shape, F32)
    for kind in range(scales.shape[1]):
        gain = jnp.where(kinds == kind, scales[:, kind:kind + 1], gain)
    right = (jnp.dot(second[...], feat[...], preferred_element_type=F32).astype(BF16).astype(F32) * 0.5).astype(BF16)
    high = where.astype(BF16).astype(F32)
    tail = jnp.concatenate([high, where - high, gain, jnp.zeros((9, count), F32)], 0).astype(BF16)
    payload = jnp.concatenate([right, tail], 0)
    offered[...] = jnp.dot(payload, one_hot(send[...], count), preferred_element_type=F32).astype(BF16)[0:ROWS]
    pl.semaphore_wait(barrier, len(paths))

    def remote(source, k, offset):
        copy = pltpu.make_async_remote_copy(
            src_ref=source, dst_ref=ghost_out.at[k], send_sem=send_sem.at[k], recv_sem=recv_sem.at[k],
            device_id=neighbour(offset, -1), device_id_type=MESH_IDS)
        copy.start()
        return copy
    copies = [remote(offered, k, OFFSETS[k]) for k in DIRECT]

    own[0:3, :] = where
    own[3:4, :] = gain
    own[4:8, :] = jnp.zeros((4, count), F32)
    left = (jnp.dot(first[...], feat[...], preferred_element_type=F32).astype(BF16).astype(F32) * 0.5).astype(BF16)
    for g in range(count // 256):
        left_tab[64 * g:64 * g + 64, :] = left[:, 256 * g:256 * g + 256]
        right_tab[64 * g:64 * g + 64, :] = right[:, 256 * g:256 * g + 256]
    for c in range(4):
        spread(own[c:c + 1, :], own_tab, c * chunks)
    finish(loads[7:])
    w_out = weights(radial, mid, last, out, w_mids, w_lasts, w_radials)
    stand[...] = compact(one, two, mask, own_tab, own_tab, chunks, chunks, words, live, ranks, packed)
    copies[0].wait_recv()
    relays = [remote(ghost_out.at[2], k, OFFSETS[step]) for step, k in RELAYED]
    acc_own[...] = jnp.zeros_like(acc_own)
    acc_loc[...] = jnp.zeros_like(acc_loc)
    step = pair_step(packed, own_tab, own_tab, chunks, chunks, left_tab, right_tab, w_mids, w_lasts, w_radials, w_out,
                     hot_own, hot_par, quant, acc_own, acc_loc, MANY)
    stores = move((own, left_tab, right_tab, packed, stand), (own_out, left_out, right_out, packed_out, stand_out), out_sem)
    lax.fori_loop(0, EARLY // MANY, step, 0)
    stores += move((acc_own, acc_loc), (acc_own_out, acc_loc_out), last_sem)
    copies[0].wait_send()
    finish(copies[1:])
    finish(relays)
    finish(stores)


def pairs_kernel(own_hbm, left_hbm, right_hbm, ghost_hbm, packed_hbm, stand_hbm, acc_own_hbm, acc_loc_hbm,
                 one_hbm, two_hbm, mask_hbm, radial_hbm, mid_hbm, last_hbm, out_hbm,
                 acc_own_out, acc_loc_out, force_out,
                 own, left_tab, right_tab, ghost, packed, stand, acc_own, acc_loc, one, two, mask, radial, mid, last, out,
                 own_tab, ghost_tab, gtable, gpacked, words, live, ranks, hot_own, hot_par, quant, acc_gho, force,
                 w_mids, w_lasts, w_radials, in_sem, out_sem, last_sem):
    loads = move((own_hbm, ghost_hbm, one_hbm, two_hbm, mask_hbm, left_hbm, right_hbm, packed_hbm, stand_hbm,
                  acc_own_hbm, acc_loc_hbm, radial_hbm, mid_hbm, last_hbm, out_hbm),
                 (own, ghost, one, two, mask, left_tab, right_tab, packed, stand,
                  acc_own, acc_loc, radial, mid, last, out), in_sem)
    finish(loads[0:5])
    count = own.shape[1]
    chunks = count // 128
    sends = ghost.shape[2]
    per = sends // 128
    gchunks = len(OFFSETS) * per
    for c in range(4):
        spread(own[c:c + 1, :], own_tab, c * chunks)
    for k, offset in enumerate(OFFSETS):
        gtable[64 * k:64 * k + 64, :] = ghost[k, 0:64, :]
        tail = ghost[k, 64:72, :].astype(F32)
        for c in range(4):
            row = tail[c:c + 1] + tail[c + 3:c + 4] + float(offset[c]) if c < 3 else tail[6:7]
            spread(row, ghost_tab, c * gchunks + k * per)
    finish(loads[5:])
    w_out = weights(radial, mid, last, out, w_mids, w_lasts, w_radials)
    gstand = compact(one, two, mask, own_tab, ghost_tab, chunks, gchunks, words, live, ranks, gpacked)
    acc_gho[...] = jnp.zeros_like(acc_gho)
    rest = trips(stand[...], FEW)
    gstep = pair_step(gpacked, own_tab, ghost_tab, chunks, gchunks, left_tab, gtable, w_mids, w_lasts, w_radials, w_out,
                      hot_own, hot_par, quant, acc_own, acc_gho, GHOSTLY)
    lax.fori_loop(0, trips(gstand, GHOSTLY), gstep, 0)
    for ch in range(gchunks):
        cols = slice(128 * (ch % per), 128 * (ch % per) + 128)
        force[ch // per, 0:4, cols] = joined(acc_gho, ch)
        force[ch // per, 4:8, cols] = jnp.zeros((4, 128), F32)
    step = pair_step(packed, own_tab, own_tab, chunks, chunks, left_tab, right_tab, w_mids, w_lasts, w_radials, w_out,
                     hot_own, hot_par, quant, acc_own, acc_loc, FEW)
    stores = move((force,), (force_out,), out_sem)
    lax.fori_loop((EARLY + LATE) // FEW, rest, step, 0)
    finish(stores + move((acc_own, acc_loc), (acc_own_out, acc_loc_out), last_sem))


def home_kernel(own_hbm, left_hbm, right_hbm, packed_hbm, acc_own_hbm, acc_loc_hbm, force_hbm,
                radial_hbm, mid_hbm, last_hbm, out_hbm,
                acc_own_out, acc_loc_out, arrived_out,
                own, left_tab, right_tab, packed, acc_own, acc_loc, radial, mid, last, out,
                own_tab, hot_own, hot_par, quant, w_mids, w_lasts, w_radials,
                in_sem, out_sem, send_sem, recv_sem):
    barrier = meet(OFFSETS, -1)
    finish(move((own_hbm, left_hbm, right_hbm, packed_hbm, acc_own_hbm, acc_loc_hbm, radial_hbm, mid_hbm, last_hbm, out_hbm),
                (own, left_tab, right_tab, packed, acc_own, acc_loc, radial, mid, last, out), in_sem))
    pl.semaphore_wait(barrier, len(OFFSETS))
    copies = []
    for k, offset in enumerate(OFFSETS):
        copy = pltpu.make_async_remote_copy(
            src_ref=force_hbm.at[k], dst_ref=arrived_out.at[k], send_sem=send_sem.at[k], recv_sem=recv_sem.at[k],
            device_id=neighbour(offset, 1), device_id_type=MESH_IDS)
        copy.start()
        copies.append(copy)
    chunks = own.shape[1] // 128
    for c in range(4):
        spread(own[c:c + 1, :], own_tab, c * chunks)
    w_out = weights(radial, mid, last, out, w_mids, w_lasts, w_radials)
    step = pair_step(packed, own_tab, own_tab, chunks, chunks, left_tab, right_tab, w_mids, w_lasts, w_radials, w_out,
                     hot_own, hot_par, quant, acc_own, acc_loc, MANY)
    lax.fori_loop(EARLY // MANY, (EARLY + LATE) // MANY, step, 0)
    stores = move((acc_own, acc_loc), (acc_own_out, acc_loc_out), out_sem)
    finish(copies)
    finish(stores)


def join_kernel(acc_own_hbm, acc_loc_hbm, arrived_hbm, send_hbm, force_out, energy_out,
                acc_own, acc_loc, arrived, send, result, energy, in_sem, out_sem):
    finish(move((acc_own_hbm, acc_loc_hbm, arrived_hbm, send_hbm), (acc_own, acc_loc, arrived, send), in_sem))
    count = result.shape[1]
    hot = one_hot(send[...], count)
    total = arrived[0]
    for k in range(1, len(OFFSETS)):
        total = total + arrived[k]
    high, rest = split_two(total)
    mid_part, low = split_two(rest)
    parts = jnp.concatenate([high, mid_part, low, jnp.zeros_like(low)], 0).astype(BF16)
    back = lax.dot_general(parts, hot, NT, preferred_element_type=F32)
    back = back[0:8] + back[8:16] + back[16:24]
    for ch in range(count // 128):
        cols = slice(128 * ch, 128 * ch + 128)
        mine = joined(acc_own, ch)
        result[:, cols] = mine[0:3] - joined(acc_loc, ch)[0:3] - back[0:3, cols]
        energy[:, cols] = mine[3:4]
    finish(move((result, energy), (force_out, energy_out), out_sem))


def on_device(positions, features, species, species_scale, w_first, w_second, w_radial, w_mid, w_last, w_out,
              ghost_send, local_first, local_second, local_mask, ghost_owner, ghost_index, ghost_mask):
    v, shape = pltpu.VMEM, jax.ShapeDtypeStruct
    count = positions.shape[1]
    sends = ghost_send.shape[0]
    channels, nb = w_radial.shape
    blocks = len(OFFSETS)
    chunks, gchunks = count // 128, blocks * sends // 128
    lrows, grows = local_first.shape[0] // 128, ghost_owner.shape[0] // 128
    buffers = lambda arrays: [v(x.shape, x.dtype) for x in arrays]
    sems = lambda number: pltpu.SemaphoreType.DMA((number,))
    send_row = ghost_send.reshape(1, sends)
    net = [w_radial.T, w_mid, w_last, w_out.reshape(1, channels)]
    local = [x.reshape(lrows, 128) for x in (local_first, local_second, local_mask)]
    ghostly = [x.reshape(grows, 128) for x in (ghost_owner, ghost_index, ghost_mask)]
    blocks_w = [v((4 * channels, 4 * channels), BF16), v((4 * channels, 4 * channels), BF16), v((4 * channels, 16 * nb), BF16)]
    hots = lambda width: [v((width, 64, 1024), BF16), v((width, 64, 1024), BF16), v((width, 64, 128), F32)]
    table = shape((channels * count // 256, 256), BF16)
    acc = shape((8 * chunks, 64), F32)
    own_tab = v((4 * chunks, 8, 128), F32)

    args = [positions, features, species.reshape(1, count), species_scale.reshape(1, -1), w_first, w_second, send_row] + local + net
    made = [shape((8, count), F32), table, table, shape((blocks, ROWS, sends), BF16),
            shape((lrows, 128), I32), shape((8, 128), I32), acc, acc]
    own, left_tab, right_tab, ghosts, packed, stand, acc_own, acc_loc = pl.pallas_call(
        offer_kernel,
        name="offer",
        out_shape=made,
        in_specs=[HBM] * len(args),
        out_specs=[HBM] * len(made),
        scratch_shapes=buffers(args) + [v((ROWS, sends), BF16)] + buffers(made[0:3] + made[4:]) + [
            own_tab, v((lrows, 128), I32), v((lrows, 128), F32), v((lrows, 256), F32)] + hots(MANY) + blocks_w + [
            sems(len(args)), sems(5), sems(2), sems(blocks), sems(blocks)],
        compiler_params=pltpu.CompilerParams(collective_id=0, has_side_effects=True, vmem_limit_bytes=60 << 20),
    )(*args)

    args = [own, left_tab, right_tab, ghosts, packed, stand, acc_own, acc_loc] + ghostly + net
    made = [acc, acc, shape((blocks, 8, sends), F32)]
    acc_own, acc_loc, gforce = pl.pallas_call(
        pairs_kernel,
        name="pairs",
        out_shape=made,
        in_specs=[HBM] * len(args),
        out_specs=[HBM] * len(made),
        scratch_shapes=buffers(args) + [
            own_tab, v((4 * gchunks, 8, 128), F32), v((channels * gchunks // 2, 256), BF16), v((grows, 128), I32),
            v((grows, 128), I32), v((grows, 128), F32), v((grows, 256), F32)] + hots(GHOSTLY) + [
            v((8 * gchunks, 64), F32), v((blocks, 8, sends), F32)] + blocks_w + [sems(len(args)), sems(1), sems(2)],
        compiler_params=pltpu.CompilerParams(vmem_limit_bytes=60 << 20),
    )(*args)

    args = [own, left_tab, right_tab, packed, acc_own, acc_loc, gforce] + net
    made = [acc, acc, shape((blocks, 8, sends), F32)]
    acc_own, acc_loc, arrived = pl.pallas_call(
        home_kernel,
        name="home",
        out_shape=made,
        in_specs=[HBM] * len(args),
        out_specs=[HBM] * len(made),
        scratch_shapes=buffers(args[:6] + args[7:]) + [own_tab] + hots(MANY) + blocks_w + [
            sems(len(args) - 1), sems(2), sems(blocks), sems(blocks)],
        compiler_params=pltpu.CompilerParams(collective_id=1, has_side_effects=True, vmem_limit_bytes=60 << 20),
    )(*args)

    args = [acc_own, acc_loc, arrived, send_row]
    made = [shape((3, count), F32), shape((1, count), F32)]
    forces, energy = pl.pallas_call(
        join_kernel,
        name="join",
        out_shape=made,
        in_specs=[HBM] * len(args),
        out_specs=[HBM] * len(made),
        scratch_shapes=buffers(args) + buffers(made) + [sems(len(args)), sems(len(made))],
        compiler_params=pltpu.CompilerParams(vmem_limit_bytes=60 << 20),
    )(*args)
    return forces, energy.reshape(count)


def solution(mesh):
    everywhere = ("gx", "gy", "gz")
    wide, flat, copied = P(None, everywhere), P(everywhere), P()
    in_specs = (wide, wide, flat) + (copied,) * 7 + (flat,) * 7
    return jax.shard_map(on_device, mesh=mesh, in_specs=in_specs, out_specs=(wide, flat), check_vma=False)
```

```python
import jax
import jax.numpy as jnp
from jax import lax
from jax.experimental import pallas as pl
from jax.experimental.pallas import tpu as pltpu
from jax.sharding import PartitionSpec as P

OFFSETS = ((1, 0, 0), (0, 1, 0), (0, 0, 1), (1, 1, 0), (1, 0, 1), (0, 1, 1), (1, 1, 1))
DIRECT = (2, 0, 1, 3)
RELAYED = ((0, 4), (1, 5), (3, 6))
MESH_IDS = pl.DeviceIdType.MESH
HBM = pl.BlockSpec(memory_space=pltpu.HBM)
NT = (((1,), (1,)), ((), ()))
TN = (((0,), (0,)), ((), ()))
WIDTH = 24.0
F32, BF16, I32 = jnp.float32, jnp.bfloat16, jnp.int32
LIVE = 128
ROWS = 72
EARLY = 4
LATE = 12
HALVES = 4
MANY = 4
FEW = 2
GHOSTLY = 3


def neighbour(offset, sign):
    where = []
    for axis, step in zip(("gx", "gy", "gz"), offset):
        count = lax.axis_size(axis)
        where.append(lax.rem(lax.axis_index(axis) + sign * step + count, count))
    return tuple(where)


def meet(offsets, sign):
    barrier = pltpu.get_barrier_semaphore()
    for offset in offsets:
        pl.semaphore_signal(barrier, inc=1, device_id=neighbour(offset, sign), device_id_type=MESH_IDS)
    return barrier


def move(sources, targets, sems):
    copies = [pltpu.make_async_copy(s, t, sems.at[k]) for k, (s, t) in enumerate(zip(sources, targets))]
    for copy in copies:
        copy.start()
    return copies


def finish(copies):
    for copy in copies:
        copy.wait()


def one_hot(row, count):
    levels = lax.broadcasted_iota(jnp.int16, (count, row.shape[1]), 0)
    return jnp.where(levels == row.astype(jnp.int16), jnp.ones((), BF16), jnp.zeros((), BF16))


def split_two(value):
    high = value.astype(BF16).astype(F32)
    return high, value - high


def take_lanes(table, index):
    return jnp.take_along_axis(table, index, axis=1, mode="promise_in_bounds")


def pick(tab, n, c, low, high):
    value = take_lanes(tab[c * n], low)
    for ch in range(1, n):
        value = jnp.where(high == ch, take_lanes(tab[c * n + ch], low), value)
    return value


def geometry(low_i, high_i, low_j, high_j, own_tab, tab, chunks, n):
    gap = [pick(tab, n, c, low_j, high_j) - pick(own_tab, chunks, c, low_i, high_i) for c in range(3)]
    return gap, gap[0] * gap[0] + gap[1] * gap[1] + gap[2] * gap[2]


def spread(row, tab, first):
    for ch in range(row.shape[1] // 128):
        tab[first + ch] = jnp.broadcast_to(row[:, 128 * ch:128 * ch + 128], (8, 128))


def compact(own_list, par_list, mask_list, own_tab, tab, chunks, n, words, live, ranks, packed):
    rows = own_list.shape[0]
    lane = lax.broadcasted_iota(I32, (8, 128), 1)

    def find(v, carry):
        at = pl.ds(pl.multiple_of(8 * v, 8), 8)
        own, partner = own_list[at, :], par_list[at, :]
        gap, squared = geometry(own & 127, own >> 7, partner & 127, partner >> 7, own_tab, tab, chunks, n)
        alive = jnp.logical_and(mask_list[at, :] > 0, squared < 1.0)
        live[at, :] = jnp.where(alive, 1.0, 0.0)
        words[at, :] = jnp.where(alive, (own << 8) + (partner << 17) + LIVE, 0)
        return carry
    lax.fori_loop(0, rows // 8, find, 0, unroll=True)
    above = jnp.where(lax.broadcasted_iota(I32, (128, 128), 0) < lax.broadcasted_iota(I32, (128, 128), 1), 1.0, 0.0)
    adder = jnp.concatenate([above, jnp.ones((128, 128), F32)], 1).astype(BF16)
    ranks[0:rows, :] = jnp.dot(live[0:rows, :].astype(BF16), adder, preferred_element_type=F32)

    tiles = rows // 8
    stand = jnp.zeros((8, 128), I32)
    slots = [jnp.zeros((8, 128), I32) for _ in range(tiles)]
    for v in range(tiles):
        at = slice(8 * v, 8 * v + 8)
        word = words[at, :]
        rank = ranks[at, 0:128].astype(I32)
        number = ranks[at, 128:256].astype(I32)
        word = jnp.where(word > 0, word + (lane - rank), 0)
        for bit in range(7):
            moved = pltpu.roll(word, 128 - (1 << bit), 1)
            stay = jnp.where((word & (1 << bit)) > 0, 0, word)
            word = jnp.where((moved & (1 << bit)) > 0, moved, stay)
        turn = (lane - stand) & 127
        word = take_lanes(word, turn)
        row = jnp.where(turn < number, (stand + turn) >> 7, -1)
        for t in range(v + 1):
            slots[t] = jnp.where(row == t, word, slots[t])
        stand = stand + number
    for t in range(tiles):
        packed[8 * t:8 * t + 8, :] = slots[t]
    return stand


def weights(radial, mid, last, out, w_mids, w_lasts, w_radials):
    nb, channels = radial.shape
    high, low = split_two(radial[...] * 0.5)
    spot = lax.broadcasted_iota(I32, (nb, 4 * nb), 1)
    term = lax.broadcasted_iota(I32, (nb, 4 * nb), 0)
    place_high = jnp.where((spot == term) | (spot == term + nb), 1.0, 0.0).astype(BF16)
    place_low = jnp.where(spot == term + 2 * nb, 1.0, 0.0).astype(BF16)
    w_radial = (lax.dot_general(high.astype(BF16), place_high, TN, preferred_element_type=F32)
                + lax.dot_general(low.astype(BF16), place_low, TN, preferred_element_type=F32)).astype(BF16)
    w_mid = (mid[...].astype(F32) * 0.5).astype(BF16)
    w_last = (last[...].astype(F32) * 0.5).astype(BF16)
    for store, w in ((w_mids, w_mid), (w_lasts, w_last), (w_radials, w_radial)):
        for half in range(HALVES):
            store[channels * half:channels * half + channels, :] = jnp.concatenate(
                [w if other == half else jnp.zeros_like(w) for other in range(HALVES)], 1)
    eye = lax.broadcasted_iota(I32, (channels, channels), 0) == lax.broadcasted_iota(I32, (channels, channels), 1)
    return jnp.sum(jnp.where(eye, jnp.broadcast_to(out[...], (channels, channels)), 0.0), 1, keepdims=True)


def activate(y, tangent):
    up = 1.0 + jnp.tanh(y)
    value = y * up
    return value, (up + value * (2.0 - up)) * tangent


def activate_hidden(y, tangent):
    up = 1.0 + jnp.tanh(y)
    value = (y * up).astype(BF16)
    up = up.astype(BF16)
    return value, (up + value * (2.0 - up)) * tangent.astype(BF16)


def pair_step(packed, own_tab, tab, chunks, n, left_tab, right_tab, w_mids, w_lasts, w_radials, w_out,
              hot_own, hot_par, quant, acc_own, acc_par, width):
    nb = 8
    centers = lax.broadcasted_iota(I32, (nb, 128), 0).astype(F32) / (nb - 1)
    zero = jnp.zeros((), BF16)

    def stages(t, u):
        word = packed[pl.ds(pl.multiple_of(8 * t, 8), 8), :]
        own, partner = (word >> 8) & 511, word >> 17
        low_i, high_i, low_j, high_j = own & 127, own >> 7, partner & 127, partner >> 7
        wide = lambda x, half: jnp.concatenate([x[2 * half:2 * half + 1], x[2 * half + 1:2 * half + 2]], 1)

        def gather(low, high, keep, table, groups, half):
            hot = one_hot(wide(low, half), 128)
            keep[u, :, 256 * half:256 * half + 256] = hot[0:64] + hot[64:128]
            top = wide(high, half)
            odd = jnp.broadcast_to((top & 1).astype(jnp.int16), (128, 256))
            hot = jnp.concatenate([jnp.where(odd == jnp.int16(0), hot, zero), jnp.where(odd == jnp.int16(1), hot, zero)], 0)
            found = jnp.dot(table[...], hot, preferred_element_type=F32)
            group = top >> 1
            value = found[0:64]
            for g in range(1, groups):
                value = jnp.where(group == g, found[64 * g:64 * g + 64], value)
            return value

        gathered = [gather(low_i, high_i, hot_own, left_tab, chunks // 2, half)
                    + gather(low_j, high_j, hot_par, right_tab, n // 2, half) for half in range(HALVES)]
        yield
        gap, squared = geometry(low_i, high_i, low_j, high_j, own_tab, tab, chunks, n)
        weight = jnp.where((word & LIVE) > 0, pick(own_tab, chunks, 3, low_i, high_i) * pick(tab, n, 3, low_j, high_j), 0.0)
        radials = []
        for half in range(HALVES):
            tiles, slants = [], []
            for r in (2 * half, 2 * half + 1):
                off = squared[r:r + 1] - centers
                basis = jnp.exp(-WIDTH * off * off)
                tiles.append(basis)
                slants.append((-2.0 * WIDTH) * off * basis)
            high, low = split_two(jnp.concatenate(tiles + slants, 1))
            radials += [high, low, high, jnp.zeros_like(low)]
        radials = jnp.dot(w_radials[...], jnp.concatenate(radials, 0).astype(BF16), preferred_element_type=F32)
        yield
        quarter = lambda x, half: x[64 * half:64 * half + 64]
        now = [activate_hidden(g + quarter(radials, half)[:, 0:256], quarter(radials, half)[:, 256:512]) for half, g in enumerate(gathered)]
        for w, act in ((w_mids, activate_hidden), (w_lasts, activate)):
            stack = jnp.concatenate([jnp.concatenate(pair, 1) for pair in now], 0)
            mixed = jnp.dot(w[...], stack, preferred_element_type=F32)
            yield
            now = [act(quarter(mixed, half)[:, 0:256], quarter(mixed, half)[:, 256:512]) for half in range(HALVES)]
        reads = [jnp.sum(value * w_out, 0, keepdims=True) for value, _ in now]
        slopes = [jnp.sum(slope * w_out, 0, keepdims=True) for _, slope in now]
        yield
        tall = lambda xs: jnp.concatenate([x[:, 128 * k:128 * k + 128] for x in xs for k in range(2)], 0)
        readout, reslope = tall(reads), tall(slopes)
        near = jnp.maximum(1.0 - squared, 0.0)
        envelope = near * near
        energy = weight * envelope * readout
        slope = weight * (envelope * reslope - 2.0 * near * readout)
        outs = [2.0 * g * slope for g in gap] + [energy]
        for q, out in enumerate(outs):
            quant[u, 8 * q:8 * q + 8, :] = out
            quant[u, 32 + 8 * q:40 + 8 * q, :] = out
        a_own, a_par = [], []
        part_i, part_j = own >> 6, partner >> 6
        which = lax.broadcasted_iota(I32, (8, 128), 0) >> 2
        for r in range(8):
            tile = quant[u, pl.ds(r, 8, stride=8), :]
            pick_i, pick_j = part_i[r:r + 1] - which, part_j[r:r + 1] - which
            a_own.append(jnp.concatenate([jnp.where(pick_i == 2 * ch, tile, 0.0) for ch in range(chunks)], 0))
            a_par.append(jnp.concatenate([jnp.where(pick_j == 2 * ch, tile, 0.0) for ch in range(n)], 0))
        acc_own[...] += lax.dot_general(jnp.concatenate(a_own, 1).astype(BF16), hot_own[u], NT, preferred_element_type=F32)
        acc_par[...] += lax.dot_general(jnp.concatenate(a_par, 1).astype(BF16), hot_par[u], NT, preferred_element_type=F32)

    def step(t, carry):
        streams = [stages(width * t + u, u) for u in range(width)]
        while streams:
            streams = [stream for stream in streams if next(stream, True) is None]
        return carry
    return step


def joined(acc, ch):
    return jnp.concatenate([acc[8 * ch:8 * ch + 4, :], acc[8 * ch + 4:8 * ch + 8, :]], 1)


def trips(stand, width):
    return (jnp.max(stand) + (128 * width - 1)) // (128 * width)


def offer_kernel(pos_hbm, feat_hbm, species_hbm, scale_hbm, first_hbm, second_hbm, send_hbm,
                 one_hbm, two_hbm, mask_hbm, radial_hbm, mid_hbm, last_hbm, out_hbm,
                 own_out, left_out, right_out, ghost_out, packed_out, stand_out, acc_own_out, acc_loc_out,
                 pos, feat, species, scale, first, second, send, one, two, mask, radial, mid, last, out,
                 offered, own, left_tab, right_tab, packed, stand, acc_own, acc_loc,
                 own_tab, words, live, ranks, hot_own, hot_par, quant, w_mids, w_lasts, w_radials,
                 in_sem, out_sem, last_sem, send_sem, recv_sem):
    paths = [OFFSETS[k] for k in DIRECT]
    barrier = meet(paths, 1)
    loads = move((pos_hbm, feat_hbm, species_hbm, scale_hbm, first_hbm, second_hbm, send_hbm,
                  one_hbm, two_hbm, mask_hbm, radial_hbm, mid_hbm, last_hbm, out_hbm),
                 (pos, feat, species, scale, first, second, send, one, two, mask, radial, mid, last, out), in_sem)
    finish(loads[0:7])
    count = pos.shape[1]
    chunks = count // 128
    where = pos[...]
    kinds = species[...]
    scales = scale[...].astype(F32)
    gain = jnp.zeros(kinds.shape, F32)
    for kind in range(scales.shape[1]):
        gain = jnp.where(kinds == kind, scales[:, kind:kind + 1], gain)
    right = (jnp.dot(second[...], feat[...], preferred_element_type=F32).astype(BF16).astype(F32) * 0.5).astype(BF16)
    high = where.astype(BF16).astype(F32)
    tail = jnp.concatenate([high, where - high, gain, jnp.zeros((9, count), F32)], 0).astype(BF16)
    payload = jnp.concatenate([right, tail], 0)
    offered[...] = jnp.dot(payload, one_hot(send[...], count), preferred_element_type=F32).astype(BF16)[0:ROWS]
    pl.semaphore_wait(barrier, len(paths))

    def remote(source, k, offset):
        copy = pltpu.make_async_remote_copy(
            src_ref=source, dst_ref=ghost_out.at[k], send_sem=send_sem.at[k], recv_sem=recv_sem.at[k],
            device_id=neighbour(offset, -1), device_id_type=MESH_IDS)
        copy.start()
        return copy
    copies = [remote(offered, k, OFFSETS[k]) for k in DIRECT]

    own[0:3, :] = where
    own[3:4, :] = gain
    own[4:8, :] = jnp.zeros((4, count), F32)
    left = (jnp.dot(first[...], feat[...], preferred_element_type=F32).astype(BF16).astype(F32) * 0.5).astype(BF16)
    for g in range(count // 256):
        left_tab[64 * g:64 * g + 64, :] = left[:, 256 * g:256 * g + 256]
        right_tab[64 * g:64 * g + 64, :] = right[:, 256 * g:256 * g + 256]
    for c in range(4):
        spread(own[c:c + 1, :], own_tab, c * chunks)
    finish(loads[7:])
    w_out = weights(radial, mid, last, out, w_mids, w_lasts, w_radials)
    stand[...] = compact(one, two, mask, own_tab, own_tab, chunks, chunks, words, live, ranks, packed)
    copies[0].wait_recv()
    relays = [remote(ghost_out.at[2], k, OFFSETS[step]) for step, k in RELAYED]
    acc_own[...] = jnp.zeros_like(acc_own)
    acc_loc[...] = jnp.zeros_like(acc_loc)
    step = pair_step(packed, own_tab, own_tab, chunks, chunks, left_tab, right_tab, w_mids, w_lasts, w_radials, w_out,
                     hot_own, hot_par, quant, acc_own, acc_loc, MANY)
    stores = move((own, left_tab, right_tab, packed, stand), (own_out, left_out, right_out, packed_out, stand_out), out_sem)
    lax.fori_loop(0, EARLY // MANY, step, 0)
    stores += move((acc_own, acc_loc), (acc_own_out, acc_loc_out), last_sem)
    copies[0].wait_send()
    finish(copies[1:])
    finish(relays)
    finish(stores)


def pairs_kernel(own_hbm, left_hbm, right_hbm, ghost_hbm, packed_hbm, stand_hbm, acc_own_hbm, acc_loc_hbm,
                 one_hbm, two_hbm, mask_hbm, radial_hbm, mid_hbm, last_hbm, out_hbm,
                 acc_own_out, acc_loc_out, force_out,
                 own, left_tab, right_tab, ghost, packed, stand, acc_own, acc_loc, one, two, mask, radial, mid, last, out,
                 own_tab, ghost_tab, gtable, gpacked, words, live, ranks, hot_own, hot_par, quant, acc_gho, force,
                 w_mids, w_lasts, w_radials, in_sem, out_sem, last_sem):
    loads = move((own_hbm, ghost_hbm, one_hbm, two_hbm, mask_hbm, left_hbm, right_hbm, packed_hbm, stand_hbm,
                  acc_own_hbm, acc_loc_hbm, radial_hbm, mid_hbm, last_hbm, out_hbm),
                 (own, ghost, one, two, mask, left_tab, right_tab, packed, stand,
                  acc_own, acc_loc, radial, mid, last, out), in_sem)
    finish(loads[0:5])
    count = own.shape[1]
    chunks = count // 128
    sends = ghost.shape[2]
    per = sends // 128
    gchunks = len(OFFSETS) * per
    for c in range(4):
        spread(own[c:c + 1, :], own_tab, c * chunks)
    for k, offset in enumerate(OFFSETS):
        gtable[64 * k:64 * k + 64, :] = ghost[k, 0:64, :]
        tail = ghost[k, 64:72, :].astype(F32)
        for c in range(4):
            row = tail[c:c + 1] + tail[c + 3:c + 4] + float(offset[c]) if c < 3 else tail[6:7]
            spread(row, ghost_tab, c * gchunks + k * per)
    finish(loads[5:])
    w_out = weights(radial, mid, last, out, w_mids, w_lasts, w_radials)
    gstand = compact(one, two, mask, own_tab, ghost_tab, chunks, gchunks, words, live, ranks, gpacked)
    acc_gho[...] = jnp.zeros_like(acc_gho)
    rest = trips(stand[...], FEW)
    gstep = pair_step(gpacked, own_tab, ghost_tab, chunks, gchunks, left_tab, gtable, w_mids, w_lasts, w_radials, w_out,
                      hot_own, hot_par, quant, acc_own, acc_gho, GHOSTLY)
    lax.fori_loop(0, trips(gstand, GHOSTLY), gstep, 0)
    for ch in range(gchunks):
        cols = slice(128 * (ch % per), 128 * (ch % per) + 128)
        force[ch // per, 0:4, cols] = joined(acc_gho, ch)
        force[ch // per, 4:8, cols] = jnp.zeros((4, 128), F32)
    step = pair_step(packed, own_tab, own_tab, chunks, chunks, left_tab, right_tab, w_mids, w_lasts, w_radials, w_out,
                     hot_own, hot_par, quant, acc_own, acc_loc, FEW)
    stores = move((force,), (force_out,), out_sem)
    lax.fori_loop((EARLY + LATE) // FEW, rest, step, 0)
    finish(stores + move((acc_own, acc_loc), (acc_own_out, acc_loc_out), last_sem))


def home_kernel(own_hbm, left_hbm, right_hbm, packed_hbm, acc_own_hbm, acc_loc_hbm, force_hbm,
                radial_hbm, mid_hbm, last_hbm, out_hbm,
                acc_own_out, acc_loc_out, arrived_out,
                own, left_tab, right_tab, packed, acc_own, acc_loc, radial, mid, last, out,
                own_tab, hot_own, hot_par, quant, w_mids, w_lasts, w_radials,
                in_sem, out_sem, send_sem, recv_sem):
    barrier = meet(OFFSETS, -1)
    finish(move((own_hbm, left_hbm, right_hbm, packed_hbm, acc_own_hbm, acc_loc_hbm, radial_hbm, mid_hbm, last_hbm, out_hbm),
                (own, left_tab, right_tab, packed, acc_own, acc_loc, radial, mid, last, out), in_sem))
    pl.semaphore_wait(barrier, len(OFFSETS))
    copies = []
    for k, offset in enumerate(OFFSETS):
        copy = pltpu.make_async_remote_copy(
            src_ref=force_hbm.at[k], dst_ref=arrived_out.at[k], send_sem=send_sem.at[k], recv_sem=recv_sem.at[k],
            device_id=neighbour(offset, 1), device_id_type=MESH_IDS)
        copy.start()
        copies.append(copy)
    chunks = own.shape[1] // 128
    for c in range(4):
        spread(own[c:c + 1, :], own_tab, c * chunks)
    w_out = weights(radial, mid, last, out, w_mids, w_lasts, w_radials)
    step = pair_step(packed, own_tab, own_tab, chunks, chunks, left_tab, right_tab, w_mids, w_lasts, w_radials, w_out,
                     hot_own, hot_par, quant, acc_own, acc_loc, MANY)
    lax.fori_loop(EARLY // MANY, (EARLY + LATE) // MANY, step, 0)
    stores = move((acc_own, acc_loc), (acc_own_out, acc_loc_out), out_sem)
    finish(copies)
    finish(stores)


def join_kernel(acc_own_hbm, acc_loc_hbm, arrived_hbm, send_hbm, force_out, energy_out,
                acc_own, acc_loc, arrived, send, result, energy, in_sem, out_sem):
    finish(move((acc_own_hbm, acc_loc_hbm, arrived_hbm, send_hbm), (acc_own, acc_loc, arrived, send), in_sem))
    count = result.shape[1]
    hot = one_hot(send[...], count)
    total = arrived[0]
    for k in range(1, len(OFFSETS)):
        total = total + arrived[k]
    high, rest = split_two(total)
    mid_part, low = split_two(rest)
    parts = jnp.concatenate([high, mid_part, low, jnp.zeros_like(low)], 0).astype(BF16)
    back = lax.dot_general(parts, hot, NT, preferred_element_type=F32)
    back = back[0:8] + back[8:16] + back[16:24]
    for ch in range(count // 128):
        cols = slice(128 * ch, 128 * ch + 128)
        mine = joined(acc_own, ch)
        result[:, cols] = mine[0:3] - joined(acc_loc, ch)[0:3] - back[0:3, cols]
        energy[:, cols] = mine[3:4]
    finish(move((result, energy), (force_out, energy_out), out_sem))


def on_device(positions, features, species, species_scale, w_first, w_second, w_radial, w_mid, w_last, w_out,
              ghost_send, local_first, local_second, local_mask, ghost_owner, ghost_index, ghost_mask):
    v, shape = pltpu.VMEM, jax.ShapeDtypeStruct
    count = positions.shape[1]
    sends = ghost_send.shape[0]
    channels, nb = w_radial.shape
    blocks = len(OFFSETS)
    chunks, gchunks = count // 128, blocks * sends // 128
    lrows, grows = local_first.shape[0] // 128, ghost_owner.shape[0] // 128
    buffers = lambda arrays: [v(x.shape, x.dtype) for x in arrays]
    sems = lambda number: pltpu.SemaphoreType.DMA((number,))
    send_row = ghost_send.reshape(1, sends)
    net = [w_radial.T, w_mid, w_last, w_out.reshape(1, channels)]
    local = [x.reshape(lrows, 128) for x in (local_first, local_second, local_mask)]
    ghostly = [x.reshape(grows, 128) for x in (ghost_owner, ghost_index, ghost_mask)]
    blocks_w = [v((4 * channels, 4 * channels), BF16), v((4 * channels, 4 * channels), BF16), v((4 * channels, 16 * nb), BF16)]
    hots = lambda width: [v((width, 64, 1024), BF16), v((width, 64, 1024), BF16), v((width, 64, 128), F32)]
    table = shape((channels * count // 256, 256), BF16)
    acc = shape((8 * chunks, 64), F32)
    own_tab = v((4 * chunks, 8, 128), F32)

    args = [positions, features, species.reshape(1, count), species_scale.reshape(1, -1), w_first, w_second, send_row] + local + net
    made = [shape((8, count), F32), table, table, shape((blocks, ROWS, sends), BF16),
            shape((lrows, 128), I32), shape((8, 128), I32), acc, acc]
    own, left_tab, right_tab, ghosts, packed, stand, acc_own, acc_loc = pl.pallas_call(
        offer_kernel,
        name="offer",
        out_shape=made,
        in_specs=[HBM] * len(args),
        out_specs=[HBM] * len(made),
        scratch_shapes=buffers(args) + [v((ROWS, sends), BF16)] + buffers(made[0:3] + made[4:]) + [
            own_tab, v((lrows, 128), I32), v((lrows, 128), F32), v((lrows, 256), F32)] + hots(MANY) + blocks_w + [
            sems(len(args)), sems(5), sems(2), sems(blocks), sems(blocks)],
        compiler_params=pltpu.CompilerParams(collective_id=0, has_side_effects=True, vmem_limit_bytes=60 << 20),
    )(*args)

    args = [own, left_tab, right_tab, ghosts, packed, stand, acc_own, acc_loc] + ghostly + net
    made = [acc, acc, shape((blocks, 8, sends), F32)]
    acc_own, acc_loc, gforce = pl.pallas_call(
        pairs_kernel,
        name="pairs",
        out_shape=made,
        in_specs=[HBM] * len(args),
        out_specs=[HBM] * len(made),
        scratch_shapes=buffers(args) + [
            own_tab, v((4 * gchunks, 8, 128), F32), v((channels * gchunks // 2, 256), BF16), v((grows, 128), I32),
            v((grows, 128), I32), v((grows, 128), F32), v((grows, 256), F32)] + hots(GHOSTLY) + [
            v((8 * gchunks, 64), F32), v((blocks, 8, sends), F32)] + blocks_w + [sems(len(args)), sems(1), sems(2)],
        compiler_params=pltpu.CompilerParams(vmem_limit_bytes=60 << 20),
    )(*args)

    args = [own, left_tab, right_tab, packed, acc_own, acc_loc, gforce] + net
    made = [acc, acc, shape((blocks, 8, sends), F32)]
    acc_own, acc_loc, arrived = pl.pallas_call(
        home_kernel,
        name="home",
        out_shape=made,
        in_specs=[HBM] * len(args),
        out_specs=[HBM] * len(made),
        scratch_shapes=buffers(args[:6] + args[7:]) + [own_tab] + hots(MANY) + blocks_w + [
            sems(len(args) - 1), sems(2), sems(blocks), sems(blocks)],
        compiler_params=pltpu.CompilerParams(collective_id=1, has_side_effects=True, vmem_limit_bytes=60 << 20),
    )(*args)

    args = [acc_own, acc_loc, arrived, send_row]
    made = [shape((3, count), F32), shape((1, count), F32)]
    forces, energy = pl.pallas_call(
        join_kernel,
        name="join",
        out_shape=made,
        in_specs=[HBM] * len(args),
        out_specs=[HBM] * len(made),
        scratch_shapes=buffers(args) + buffers(made) + [sems(len(args)), sems(len(made))],
        compiler_params=pltpu.CompilerParams(vmem_limit_bytes=60 << 20),
    )(*args)
    return forces, energy.reshape(count)


def solution(mesh):
    everywhere = ("gx", "gy", "gz")
    wide, flat, copied = P(None, everywhere), P(everywhere), P()
    in_specs = (wide, wide, flat) + (copied,) * 7 + (flat,) * 7
    return jax.shard_map(on_device, mesh=mesh, in_specs=in_specs, out_specs=(wide, flat), check_vma=False)
```
